256 devices in a mesh: ctx: 32 (over x, y, core), section: 8 (over z).
Axes of the slice: x: 4, y: 4, z: 8, core: 2. Of those that a mesh axis runs over, the one named last changes fastest.
Arguments:
- queries: bfloat16 [8, 8192, 2560], P('section', 'ctx'), may hold values from -7 to 7
- keys: bfloat16 [8, 8192, 2560], P('section', 'ctx'), may hold values from -7 to 7
- values: bfloat16 [8, 8192, 2560], P('section', 'ctx'), may hold values from -6 to 6
- out_grad: bfloat16 [8, 8192, 2560], P('section', 'ctx'), may hold values from -6 to 6
- key_blocks: int32 [8, 32, 20, 4], P('section'), may hold values from 0 to 63, as said below
- list_lengths: int32 [8, 32, 20], P('section'), may hold values from 1 to 4, as said below
Outputs:
- handed_queries: bfloat16 [8, 8192, 2560], P('section', 'ctx')
- handed_keys: bfloat16 [8, 8192, 2560], P('section', 'ctx')
- handed_values: bfloat16 [8, 8192, 2560], P('section', 'ctx')
The draws below stay inside these ranges and needn't reach their ends.
Inputs may be any that keep to these rules, and one draw needn't show every extreme that they name: `key_blocks`: within one list the key blocks lie in the shards of distinct indices of ctx (key block b lies in shard b // 2), so they are distinct. For each section, the used entries of the lists of the 1 query group of one index of ctx name at most 3 key blocks in any one shard, and in every section some index of ctx names exactly 3 in some shard. `list_lengths`: in every section, all lists of the query groups of some index of ctx have length 4.
All inputs are finite; a program needn't handle non-finite values.
Results may differ from the reference program's by a relative error of at most 0.017.
The reference program's roundings to bfloat16 on the way count: a program that leaves them out, or rounds other values in their place, can miss the bound.
Values may be sent and summed in bfloat16 or wider, within the bound.
No kernel may reach another device: no remote copies, remote signals or barrier semaphores. Data moves between devices by JAX's collectives and lax.ppermute only.
A program may use at most 128 MiB of HBM per device.

```python
import math
import jax
import jax.numpy as jnp
from jax import lax

HEADS = 20
DH = 128
BLK = 128
KSEL = 4
KMIN = 1
QPD = 1
SECTIONS = 8
HD = 2560
QG = 256
KPD = 2
GROUPS = 32
KBLOCKS = 64
TOKENS = 8192


def draw_queries(key, part):
    shape = (SECTIONS, TOKENS, HD)
    result = jnp.clip(jax.random.normal(jax.random.fold_in(key, 34), shape, jnp.float32), -6.0, 6.0)
    return result.astype(jnp.bfloat16)


def draw_keys(key, part):
    shape = (SECTIONS, TOKENS, HD)
    result = jnp.clip(jax.random.normal(jax.random.fold_in(key, 36), shape, jnp.float32), -6.0, 6.0)
    return result.astype(jnp.bfloat16)


def list_tables(key):
    device_count = GROUPS // QPD
    entries = QPD * HEADS * KSEL
    split_keys = jax.random.split(jax.random.fold_in(key, 7), SECTIONS * device_count)
    orders = jax.vmap(lambda one: jax.random.permutation(one, device_count))(split_keys)
    orders = orders.reshape(SECTIONS, device_count, device_count).astype(jnp.int32)
    offsets = jax.random.randint(jax.random.fold_in(key, 8), (SECTIONS, device_count), 0, device_count)
    position = (jnp.arange(entries, dtype=jnp.int32)[None, None, :] + offsets[:, :, None]) % device_count
    holders = jnp.take_along_axis(orders, position, axis=2)
    within = jax.random.randint(jax.random.fold_in(key, 9), (SECTIONS, device_count, entries), 0, KPD)
    chosen = (holders * KPD + within).reshape(SECTIONS, GROUPS, HEADS, KSEL).astype(jnp.int32)
    lengths = jax.random.randint(jax.random.fold_in(key, 10), (SECTIONS, GROUPS, HEADS), KMIN, KSEL + 1)
    full_device = jax.random.randint(jax.random.fold_in(key, 11), (SECTIONS,), 0, device_count)
    device_of = jnp.arange(GROUPS, dtype=jnp.int32) // QPD
    lengths = jnp.where(device_of[None, :, None] == full_device[:, None, None], KSEL, lengths)
    return (chosen, lengths.astype(jnp.int32))


def draw_key_blocks(key, part):
    return list_tables(key)[0]


def draw_list_lengths(key, part):
    return list_tables(key)[1]


def level_of(key, dims, shards, smallest, largest):
    level, own = 1.0, jax.random.fold_in(key, 6)
    for dim, parts in shards:
        draws = jnp.exp(jax.random.uniform(jax.random.fold_in(own, dim), (parts,), jnp.float32, smallest / len(shards), largest / len(shards)))
        level = level * jnp.repeat(draws, dims[dim] // parts).reshape([-1 if axis == dim else 1 for axis in range(len(dims))])
    return level


def normal_values(stream_key, dims, deviation, reach, shards=(), kind=jnp.bfloat16):
    factor_of = level_of(stream_key, dims, shards, -0.22, 0.18) if shards else 1.0
    values = jax.random.normal(stream_key, dims, jnp.float32) * deviation * factor_of
    return jnp.minimum(jnp.maximum(values, -reach), reach).astype(kind)


def setup_inputs(seed: int = 0) -> dict:
    splits = jax.random.split(jax.random.key(seed), 7)
    queries = draw_queries(jax.random.fold_in(splits[6], 71), 0)
    keys = draw_keys(jax.random.fold_in(splits[6], 71), 0)
    values = normal_values(splits[2], (SECTIONS, TOKENS, HD), 1.0, 6.0, ((0, 8), (1, 32)))
    out_grad = normal_values(splits[3], (SECTIONS, TOKENS, HD), 1.0, 6.0, ((0, 8), (1, 32)))
    key_blocks = draw_key_blocks(jax.random.fold_in(splits[6], 71), 0)
    list_lengths = draw_list_lengths(jax.random.fold_in(splits[6], 71), 0)
    return dict(queries=queries, keys=keys, values=values, out_grad=out_grad, key_blocks=key_blocks, list_lengths=list_lengths)


def attend(query_tile, grad_tile, key_tiles, value_tiles, is_used, softmax_scale):
    tile_count, list_count, block_rows, head_dim = key_tiles.shape
    hi = lax.Precision.HIGHEST
    query_wide = query_tile.astype(jnp.float32)
    grad_wide = grad_tile.astype(jnp.float32)
    key_wide = key_tiles.reshape(tile_count, list_count * block_rows, head_dim).astype(jnp.float32)
    value_wide = value_tiles.reshape(tile_count, list_count * block_rows, head_dim).astype(jnp.float32)
    scores = jnp.einsum('nqd,nkd->nqk', query_wide, key_wide, precision=hi) * softmax_scale
    key_mask = jnp.repeat(is_used, block_rows, axis=1)[:, None, :]
    scores = jnp.where(key_mask, scores, -jnp.inf)
    row_max = lax.optimization_barrier(jnp.max(scores, axis=-1, keepdims=True))
    exp_scores = jnp.exp(scores - row_max)
    weights = exp_scores / lax.optimization_barrier(jnp.sum(exp_scores, axis=-1, keepdims=True))
    weights_low = weights.astype(jnp.bfloat16)
    weights_back = weights_low.astype(jnp.float32)
    attn_out = jnp.einsum('nqk,nkd->nqd', weights_back, value_wide, precision=hi)
    row_delta = lax.optimization_barrier(jnp.sum(grad_wide * attn_out, axis=-1, keepdims=True))
    dweights = jnp.einsum('nqd,nkd->nqk', grad_wide, value_wide, precision=hi)
    dscores = (weights * (dweights - row_delta)).astype(jnp.bfloat16).astype(jnp.float32)
    query_grad = (jnp.einsum('nqk,nkd->nqd', dscores, key_wide, precision=hi) * softmax_scale).astype(jnp.bfloat16)
    key_terms = (jnp.einsum('nqk,nqd->nkd', dscores, query_wide, precision=hi) * softmax_scale).astype(jnp.bfloat16)
    value_terms = jnp.einsum('nqk,nqd->nkd', weights_back, grad_wide, precision=hi).astype(jnp.bfloat16)
    shape = (tile_count, list_count, block_rows, head_dim)
    return (query_grad, key_terms.reshape(shape), value_terms.reshape(shape))

def reference(queries, keys, values, out_grad, key_blocks, list_lengths):
    softmax_scale = 1.0 / math.sqrt(DH)
    head_index = jnp.arange(HEADS, dtype=jnp.int32)[:, None]
    query_out, key_out, value_out = ([], [], [])
    for section_id in range(SECTIONS):
        key_tiles = keys[section_id].reshape(KBLOCKS, BLK, HEADS, DH).transpose(2, 0, 1, 3)
        value_tiles = values[section_id].reshape(KBLOCKS, BLK, HEADS, DH).transpose(2, 0, 1, 3)
        query_groups = queries[section_id].reshape(GROUPS, QG, HEADS, DH).transpose(0, 2, 1, 3)
        grad_groups = out_grad[section_id].reshape(GROUPS, QG, HEADS, DH).transpose(0, 2, 1, 3)

        def visit(carry, inputs):
            key_sum, value_sum = carry
            query_tile, grad_tile, chosen, lengths = inputs
            is_used = jnp.arange(KSEL, dtype=jnp.int32)[None, :] < lengths[:, None]
            picked_keys = key_tiles[head_index, chosen]
            picked_values = value_tiles[head_index, chosen]
            query_grad, key_terms, value_terms = attend(query_tile, grad_tile, picked_keys, picked_values, is_used, softmax_scale)
            key_terms = lax.optimization_barrier(key_terms)
            value_terms = lax.optimization_barrier(value_terms)
            key_sum = key_sum.at[head_index, chosen].add(key_terms.astype(jnp.float32))
            value_sum = value_sum.at[head_index, chosen].add(value_terms.astype(jnp.float32))
            return ((key_sum, value_sum), query_grad)
        zeros = jnp.zeros((HEADS, KBLOCKS, BLK, DH), jnp.float32)
        (key_sum, value_sum), query_grads = lax.scan(visit, (zeros, zeros), (query_groups, grad_groups, key_blocks[section_id], list_lengths[section_id]))
        query_out.append(query_grads.transpose(0, 2, 1, 3).reshape(TOKENS, HD))
        key_out.append(key_sum.astype(jnp.bfloat16).transpose(1, 2, 0, 3).reshape(TOKENS, HD))
        value_out.append(value_sum.astype(jnp.bfloat16).transpose(1, 2, 0, 3).reshape(TOKENS, HD))
    handed_queries = jnp.roll(jnp.stack(query_out), -1, axis=0)
    handed_keys = jnp.roll(jnp.stack(key_out), -1, axis=0)
    handed_values = jnp.roll(jnp.stack(value_out), -1, axis=0)
    return (handed_queries, handed_keys, handed_values)
```

```python
import functools
import math

import jax
import jax.numpy as jnp
from jax import lax
from jax.experimental import pallas as pl
from jax.experimental.pallas import tpu as pltpu
from jax.sharding import PartitionSpec as P

HEAD_BITS = 8
VMEM = pl.BlockSpec(memory_space=pltpu.VMEM)
SMEM = pl.BlockSpec(memory_space=pltpu.SMEM)
PARAMS = pltpu.CompilerParams(vmem_limit_bytes=56 * 1024 * 1024)
NT = (((1,), (1,)), ((), ()))
NN = (((1,), (0,)), ((), ()))
TN = (((0,), (0,)), ((), ()))


def shifted(value, axis, steps):
    count = lax.axis_size(axis)
    pairs = [(source, (source + steps) % count) for source in range(count)]
    return lax.ppermute(value, axis, pairs)


def exchanged(value):
    return lax.all_to_all(value, "ctx", split_axis=0, concat_axis=0, tiled=True)


def tile_of(code, rows, cols):
    block = lax.shift_right_logical(code, HEAD_BITS)
    head = lax.bitwise_and(code, (1 << HEAD_BITS) - 1)
    return (
        pl.ds(pl.multiple_of(block * rows, rows), rows),
        pl.ds(pl.multiple_of(head * cols, cols), cols),
    )


def pack_kernel(codes, source, packed):
    slots, rows, cols = packed.shape

    def one(slot, carry):
        packed[slot] = source[tile_of(jnp.maximum(codes[slot], 0), rows, cols)]
        return carry

    lax.fori_loop(0, slots, one, 0, unroll=4)


def sum_kernel(codes, terms, total, wide):
    slots, rows, cols = terms.shape
    wide[...] = jnp.zeros_like(wide)

    def one(slot, carry):
        code = codes[slot]

        @pl.when(code >= 0)
        def _():
            where = tile_of(code, rows, cols)
            wide[where] += terms[slot].astype(jnp.float32)

        return carry

    lax.fori_loop(0, slots, one, 0, unroll=4)
    total[...] = wide[...].astype(total.dtype)


def softmax_rows(query, key, used_rows, scale):
    scores = lax.dot_general(key, query, NT, preferred_element_type=jnp.float32) * scale
    row = lax.broadcasted_iota(jnp.int32, scores.shape, 0)
    scores = jnp.where(row < used_rows, scores, -jnp.inf)
    exp_scores = jnp.exp(scores - jnp.max(scores, axis=0, keepdims=True))
    return exp_scores * (1.0 / jnp.sum(exp_scores, axis=0, keepdims=True))


def listed(places, head, list_size, tiles):
    where = [jnp.maximum(places[head * list_size + item], 0) for item in range(list_size)]
    return jnp.concatenate([tiles[place] for place in where], axis=0)


def put_terms(places, head, list_size, terms, out):
    rows = terms.shape[0] // list_size
    for item in range(list_size):
        place = places[head * list_size + item]

        @pl.when(place >= 0)
        def _():
            out[place] = terms[item * rows : (item + 1) * rows]


def value_kernel(list_size, scale, places, lengths, queries, grads, keys, terms):
    rows, cols = keys.shape[1:]

    def one(head, carry):
        columns = pl.ds(pl.multiple_of(head * cols, cols), cols)
        key = listed(places, head, list_size, keys)
        weights = softmax_rows(queries[:, columns], key, lengths[head] * rows, scale)
        made = lax.dot_general(
            weights.astype(jnp.bfloat16),
            grads[:, columns],
            NN,
            preferred_element_type=jnp.float32,
        )
        put_terms(places, head, list_size, made.astype(jnp.bfloat16), terms)
        return carry

    lax.fori_loop(0, lengths.shape[0], one, 0)


def key_kernel(
    list_size, scale, places, lengths, queries, grads, keys, values, query_grad, terms
):
    rows, cols = keys.shape[1:]

    def one(head, carry):
        columns = pl.ds(pl.multiple_of(head * cols, cols), cols)
        query = queries[:, columns]
        key = listed(places, head, list_size, keys)
        value = listed(places, head, list_size, values)
        weights = softmax_rows(query, key, lengths[head] * rows, scale)
        weights_low = weights.astype(jnp.bfloat16).astype(jnp.float32)
        dweights = lax.dot_general(
            value, grads[:, columns], NT, preferred_element_type=jnp.float32
        )
        row_delta = jnp.sum(weights_low * dweights, axis=0, keepdims=True)
        dscores = (weights * (dweights - row_delta)).astype(jnp.bfloat16)
        made = lax.dot_general(dscores, query, NN, preferred_element_type=jnp.float32)
        put_terms(places, head, list_size, (made * scale).astype(jnp.bfloat16), terms)
        flipped = lax.dot_general(key, dscores, TN, preferred_element_type=jnp.float32)
        query_grad[:, columns] = (flipped * scale).T.astype(jnp.bfloat16)
        return carry

    lax.fori_loop(0, lengths.shape[0], one, 0)


def local(queries, keys, values, out_grad, key_blocks, list_lengths):
    ctx_count = lax.axis_size("ctx")
    my_index = lax.axis_index("ctx")
    row_count, column_count = queries.shape[1:]
    head_count = list_lengths.shape[2]
    head_dim = column_count // head_count
    list_size = key_blocks.shape[3]
    block_rows = row_count // 2
    entries = head_count * list_size
    capacity = (entries + ctx_count - 1) // ctx_count
    slots = ctx_count * capacity
    scale = 1.0 / math.sqrt(head_dim)

    chosen = key_blocks[0]
    lengths = list_lengths[0]
    items = jnp.arange(list_size, dtype=jnp.int32)
    heads = jnp.arange(head_count, dtype=jnp.int32)
    peers = jnp.arange(ctx_count, dtype=jnp.int32)
    is_used = items[None, None, :] < lengths[:, :, None]
    is_mine = is_used & ((chosen >> 1) == my_index)
    hit = jnp.sum(jnp.where(is_mine, 1 + (chosen & 1), 0), axis=2)
    rank = jnp.sum(
        jnp.where((heads[None, None, :] < heads[None, :, None]) & (hit[:, None, :] > 0), 1, 0),
        axis=2,
    )
    code = ((hit - 1) << HEAD_BITS) + heads[None, :]
    ranks = jnp.arange(capacity, dtype=jnp.int32)
    codes = jnp.max(
        jnp.where(
            (hit[:, None, :] > 0) & (rank[:, None, :] == ranks[None, :, None]),
            code[:, None, :],
            -1,
        ),
        axis=2,
    ).reshape(slots)

    my_lengths = lax.dynamic_index_in_dim(lengths, my_index, 0, keepdims=False)
    my_chosen = lax.dynamic_index_in_dim(chosen, my_index, 0, keepdims=False)
    my_used = items[None, :] < my_lengths[:, None]
    my_holder = jnp.where(my_used, my_chosen >> 1, -1)
    earlier = (heads[None, None, :, None] < heads[:, None, None, None]) & (
        my_holder[None, None, :, :] == my_holder[:, :, None, None]
    )
    my_rank = jnp.sum(jnp.where(earlier, 1, 0), axis=(2, 3))
    places = jnp.where(my_used, my_holder * capacity + my_rank, -1).reshape(entries)

    packed_shape = jax.ShapeDtypeStruct((slots, block_rows, head_dim), jnp.bfloat16)
    flat_shape = jax.ShapeDtypeStruct((row_count, column_count), jnp.bfloat16)
    sent_shape = (ctx_count, capacity, block_rows, head_dim)

    def pack(name, source):
        packed = pl.pallas_call(
            pack_kernel,
            out_shape=packed_shape,
            in_specs=[SMEM, VMEM],
            out_specs=VMEM,
            compiler_params=PARAMS,
            name=name,
        )(codes, source)
        return exchanged(packed.reshape(sent_shape)).reshape(packed_shape.shape)

    def add_up(name, terms):
        returned = exchanged(terms.reshape(sent_shape)).reshape(packed_shape.shape)
        return pl.pallas_call(
            sum_kernel,
            out_shape=flat_shape,
            in_specs=[SMEM, VMEM],
            out_specs=VMEM,
            scratch_shapes=[pltpu.VMEM((row_count, column_count), jnp.float32)],
            compiler_params=PARAMS,
            name=name,
        )(codes, returned)

    fetched_keys = pack("pack_keys", keys[0])
    fetched_values = pack("pack_values", values[0])
    value_terms = pl.pallas_call(
        functools.partial(value_kernel, list_size, scale),
        out_shape=packed_shape,
        in_specs=[SMEM, SMEM, VMEM, VMEM, VMEM],
        out_specs=VMEM,
        compiler_params=PARAMS,
        name="value_terms",
    )(places, my_lengths, queries[0], out_grad[0], fetched_keys)
    query_grad, key_terms = pl.pallas_call(
        functools.partial(key_kernel, list_size, scale),
        out_shape=(flat_shape, packed_shape),
        in_specs=[SMEM, SMEM, VMEM, VMEM, VMEM, VMEM],
        out_specs=(VMEM, VMEM),
        compiler_params=PARAMS,
        name="key_terms",
    )(places, my_lengths, queries[0], out_grad[0], fetched_keys, fetched_values)
    value_grad = add_up("sum_values", value_terms)
    key_grad = add_up("sum_keys", key_terms)
    handed_queries = shifted(query_grad, "section", -1)
    handed_values = shifted(value_grad, "section", -1)
    handed_keys = shifted(key_grad, "section", -1)
    return (handed_queries[None], handed_keys[None], handed_values[None])


def solution(mesh):
    placed = (
        P("section", "ctx", None),
        P("section", "ctx", None),
        P("section", "ctx", None),
        P("section", "ctx", None),
        P("section", None, None, None),
        P("section", None, None),
    )
    return jax.shard_map(
        local,
        mesh=mesh,
        in_specs=placed,
        out_specs=(P("section", "ctx", None), P("section", "ctx", None), P("section", "ctx", None)),
        check_vma=False,
    )
```

```python
import functools
import math

import jax
import jax.numpy as jnp
from jax import lax
from jax.experimental import pallas as pl
from jax.experimental.pallas import tpu as pltpu
from jax.sharding import PartitionSpec as P

HEAD_BITS = 8
VMEM = pl.BlockSpec(memory_space=pltpu.VMEM)
SMEM = pl.BlockSpec(memory_space=pltpu.SMEM)
PARAMS = pltpu.CompilerParams(vmem_limit_bytes=56 * 1024 * 1024)
NT = (((1,), (1,)), ((), ()))
NN = (((1,), (0,)), ((), ()))
TN = (((0,), (0,)), ((), ()))


def shifted(value, axis, steps):
    count = lax.axis_size(axis)
    pairs = [(source, (source + steps) % count) for source in range(count)]
    return lax.ppermute(value, axis, pairs)


def tile_of(code, rows, cols):
    block = lax.shift_right_logical(code, HEAD_BITS)
    head = lax.bitwise_and(code, (1 << HEAD_BITS) - 1)
    return (
        pl.ds(pl.multiple_of(block * rows, rows), rows),
        pl.ds(pl.multiple_of(head * cols, cols), cols),
    )


def pack_kernel(codes, source, packed):
    slots, rows, cols = packed.shape

    def one(slot, carry):
        packed[slot] = source[tile_of(jnp.maximum(codes[slot], 0), rows, cols)]
        return carry

    lax.fori_loop(0, slots, one, 0, unroll=4)


def add_terms(codes, terms, wide):
    slots, rows, cols = terms.shape
    wide[...] = jnp.zeros_like(wide)

    def one(slot, carry):
        code = codes[slot]

        @pl.when(code >= 0)
        def _():
            wide[tile_of(code, rows, cols)] += terms[slot].astype(jnp.float32)

        return carry

    lax.fori_loop(0, slots, one, 0, unroll=4)


def sum_kernel(codes, terms, total, wide):
    add_terms(codes, terms, wide)
    total[...] = wide[...].astype(total.dtype)


def join_kernel(codes, head_part, terms, total, wide):
    add_terms(codes, terms, wide)
    tail_rows = terms.shape[1]
    head_rows = total.shape[0] // 2 - tail_rows
    for block in range(2):
        start = block * (head_rows + tail_rows)
        total[start : start + head_rows] = head_part[block * head_rows : (block + 1) * head_rows]
        total[start + head_rows : start + head_rows + tail_rows] = wide[
            block * tail_rows : (block + 1) * tail_rows
        ].astype(total.dtype)


def weights_of(query, key, length, list_size, scale):
    scores = lax.dot_general(key, query, NT, preferred_element_type=jnp.float32)
    row_max = jnp.max(scores, axis=0, keepdims=True)
    exp_scores = jnp.exp2((scores - row_max) * (scale * math.log2(math.e)))
    rows = key.shape[0] // list_size
    parts = [exp_scores[item * rows : (item + 1) * rows] for item in range(list_size)]
    kept = [jnp.where(item < length, 1.0, 0.0).astype(jnp.float32) for item in range(list_size)]
    total = sum(keep * jnp.sum(part, axis=0, keepdims=True) for keep, part in zip(kept, parts))
    inverse = 1.0 / total
    return [part * (inverse * keep) for keep, part in zip(kept, parts)]


def listed(places, head, list_size, tiles):
    return jnp.concatenate(
        [tiles[places[head * list_size + item]] for item in range(list_size)], axis=0
    )


def put_terms(places, head, list_size, length, terms, outs):
    rows = terms.shape[0] // list_size
    for item in range(list_size):

        @pl.when(item < length)
        def _():
            place = places[head * list_size + item]
            start = item * rows
            for out in outs:
                count = out.shape[1]
                out[place] = terms[start : start + count]
                start += count


def value_kernel(list_size, scale, places, lengths, queries, grads, keys, *terms):
    cols = keys.shape[2]

    def one(head, carry):
        columns = pl.ds(pl.multiple_of(head * cols, cols), cols)
        key = listed(places, head, list_size, keys)
        weights = weights_of(queries[:, columns], key, lengths[head], list_size, scale)
        weights_low = jnp.concatenate([part.astype(jnp.bfloat16) for part in weights], axis=0)
        made = lax.dot_general(
            weights_low, grads[:, columns], NN, preferred_element_type=jnp.float32
        )
        put_terms(places, head, list_size, lengths[head], made.astype(jnp.bfloat16), terms)
        return carry

    lax.fori_loop(0, lengths.shape[0], one, 0, unroll=4)


def key_kernel(
    list_size, scale, places, lengths, queries, grads, keys, values, query_grad, terms
):
    rows, cols = keys.shape[1:]

    def one(head, carry):
        columns = pl.ds(pl.multiple_of(head * cols, cols), cols)
        query = queries[:, columns]
        key = listed(places, head, list_size, keys)
        value = listed(places, head, list_size, values)
        weights = weights_of(query, key, lengths[head], list_size, scale)
        weights_low = [part.astype(jnp.bfloat16).astype(jnp.float32) for part in weights]
        joined = lax.dot_general(
            value, grads[:, columns], NT, preferred_element_type=jnp.float32
        )
        dweights = [joined[item * rows : (item + 1) * rows] for item in range(list_size)]
        row_delta = sum(
            jnp.sum(low * part, axis=0, keepdims=True)
            for low, part in zip(weights_low, dweights)
        )
        dscores = jnp.concatenate(
            [
                (weight * (part - row_delta)).astype(jnp.bfloat16)
                for weight, part in zip(weights, dweights)
            ],
            axis=0,
        )
        made = lax.dot_general(dscores, query, NN, preferred_element_type=jnp.float32)
        made = (made * scale).astype(jnp.bfloat16)
        put_terms(places, head, list_size, lengths[head], made, [terms])
        flipped = lax.dot_general(key, dscores, TN, preferred_element_type=jnp.float32)
        query_grad[:, columns] = (flipped * scale).astype(jnp.bfloat16).T
        return carry

    lax.fori_loop(0, lengths.shape[0], one, 0, unroll=4)


def local(queries, keys, values, out_grad, key_blocks, list_lengths):
    ctx_count = lax.axis_size("ctx")
    my_index = lax.axis_index("ctx")
    row_count, column_count = queries.shape[1:]
    head_count = list_lengths.shape[2]
    head_dim = column_count // head_count
    list_size = key_blocks.shape[3]
    block_rows = row_count // 2
    entries = head_count * list_size
    capacity = (entries + ctx_count - 1) // ctx_count
    slots = ctx_count * capacity
    scale = 1.0 / math.sqrt(head_dim)

    chosen = key_blocks[0]
    lengths = list_lengths[0]
    items = jnp.arange(list_size, dtype=jnp.int32)
    heads = jnp.arange(head_count, dtype=jnp.int32)
    peers = jnp.arange(ctx_count, dtype=jnp.int32)
    is_used = items[None, None, :] < lengths[:, :, None]
    is_mine = is_used & ((chosen >> 1) == my_index)
    hit = jnp.sum(jnp.where(is_mine, 1 + (chosen & 1), 0), axis=2)
    rank = jnp.sum(
        jnp.where((heads[None, None, :] < heads[None, :, None]) & (hit[:, None, :] > 0), 1, 0),
        axis=2,
    )
    code = ((hit - 1) << HEAD_BITS) + heads[None, :]
    ranks = jnp.arange(capacity, dtype=jnp.int32)
    codes = jnp.max(
        jnp.where(
            (hit[:, None, :] > 0) & (rank[:, None, :] == ranks[None, :, None]),
            code[:, None, :],
            -1,
        ),
        axis=2,
    ).reshape(slots)

    my_lengths = lax.dynamic_index_in_dim(lengths, my_index, 0, keepdims=False)
    my_chosen = lax.dynamic_index_in_dim(chosen, my_index, 0, keepdims=False)
    my_used = items[None, :] < my_lengths[:, None]
    my_holder = jnp.where(my_used, my_chosen >> 1, -1)
    earlier = (heads[None, None, :, None] < heads[:, None, None, None]) & (
        my_holder[None, None, :, :] == my_holder[:, :, None, None]
    )
    my_rank = jnp.sum(jnp.where(earlier, 1, 0), axis=(2, 3))
    places = my_holder * capacity + my_rank
    places = jnp.where(my_used, places, places[:, :1]).reshape(entries)

    first_rows = block_rows // 2
    last_rows = block_rows - first_rows
    flat_shape = jax.ShapeDtypeStruct((row_count, column_count), jnp.bfloat16)

    def packed_shape(rows):
        return jax.ShapeDtypeStruct((slots, rows, head_dim), jnp.bfloat16)

    def exchanged(packed):
        parts = packed.reshape(ctx_count, capacity, *packed.shape[1:])
        parts = lax.all_to_all(parts, "ctx", split_axis=0, concat_axis=0, tiled=True)
        return parts.reshape(packed.shape)

    def pack(name, source):
        return exchanged(
            pl.pallas_call(
                pack_kernel,
                out_shape=packed_shape(block_rows),
                in_specs=[SMEM, VMEM],
                out_specs=VMEM,
                compiler_params=PARAMS,
                name=name,
            )(codes, source)
        )

    def add_up(name, returned):
        rows = 2 * returned.shape[1]
        return pl.pallas_call(
            sum_kernel,
            out_shape=jax.ShapeDtypeStruct((rows, column_count), jnp.bfloat16),
            in_specs=[SMEM, VMEM],
            out_specs=VMEM,
            scratch_shapes=[pltpu.VMEM((rows, column_count), jnp.float32)],
            compiler_params=PARAMS,
            name=name,
        )(codes, returned)

    fetched_keys = pack("pack_keys", keys[0])
    fetched_values = pack("pack_values", values[0])
    first_terms, last_terms = pl.pallas_call(
        functools.partial(value_kernel, list_size, scale),
        out_shape=(packed_shape(first_rows), packed_shape(last_rows)),
        in_specs=[SMEM, SMEM, VMEM, VMEM, VMEM],
        out_specs=(VMEM, VMEM),
        compiler_params=PARAMS,
        name="value_terms",
    )(places, my_lengths, queries[0], out_grad[0], fetched_keys)
    handed_terms = shifted(last_terms, "section", -1)
    handed_codes = shifted(codes, "section", -1)
    query_grad, key_terms = pl.pallas_call(
        functools.partial(key_kernel, list_size, scale),
        out_shape=(flat_shape, packed_shape(block_rows)),
        in_specs=[SMEM, SMEM, VMEM, VMEM, VMEM, VMEM],
        out_specs=(VMEM, VMEM),
        compiler_params=PARAMS,
        name="key_terms",
    )(places, my_lengths, queries[0], out_grad[0], fetched_keys, fetched_values)
    handed_queries = shifted(query_grad, "section", -1)
    first_values = add_up("sum_values", exchanged(first_terms))
    handed_first = shifted(first_values, "section", -1)
    key_terms, handed_terms, handed_codes = lax.optimization_barrier(
        (key_terms, handed_terms, handed_codes)
    )
    returned_keys = exchanged(key_terms)
    returned_keys, handed_queries, handed_first = lax.optimization_barrier(
        (returned_keys, handed_queries, handed_first)
    )
    key_grad = add_up("sum_keys", returned_keys)
    handed_keys = shifted(key_grad, "section", -1)
    handed_values = pl.pallas_call(
        join_kernel,
        out_shape=flat_shape,
        in_specs=[SMEM, VMEM, VMEM],
        out_specs=VMEM,
        scratch_shapes=[pltpu.VMEM((2 * last_rows, column_count), jnp.float32)],
        compiler_params=PARAMS,
        name="join_values",
    )(handed_codes, handed_first, exchanged(handed_terms))
    return (handed_queries[None], handed_keys[None], handed_values[None])


def solution(mesh):
    placed = (
        P("section", "ctx", None),
        P("section", "ctx", None),
        P("section", "ctx", None),
        P("section", "ctx", None),
        P("section", None, None, None),
        P("section", None, None),
    )
    return jax.shard_map(
        local,
        mesh=mesh,
        in_specs=placed,
        out_specs=(P("section", "ctx", None), P("section", "ctx", None), P("section", "ctx", None)),
        check_vma=False,
    )
```

```python
import functools
import math

import jax
import jax.numpy as jnp
from jax import lax
from jax.experimental import pallas as pl
from jax.experimental.pallas import tpu as pltpu
from jax.sharding import PartitionSpec as P

HEAD_BITS = 8
VMEM = pl.BlockSpec(memory_space=pltpu.VMEM)
SMEM = pl.BlockSpec(memory_space=pltpu.SMEM)
ANY = pl.BlockSpec(memory_space=pl.ANY)
PARAMS = pltpu.CompilerParams(vmem_limit_bytes=56 * 1024 * 1024)
NT = (((1,), (1,)), ((), ()))
NN = (((1,), (0,)), ((), ()))
TN = (((0,), (0,)), ((), ()))
copy = pltpu.make_async_copy


def shifted(value, axis, steps):
    count = lax.axis_size(axis)
    pairs = [(source, (source + steps) % count) for source in range(count)]
    return lax.ppermute(value, axis, pairs)


def tile_of(code, rows, cols):
    block = lax.shift_right_logical(code, HEAD_BITS)
    head = lax.bitwise_and(code, (1 << HEAD_BITS) - 1)
    return (
        pl.ds(pl.multiple_of(block * rows, rows), rows),
        pl.ds(pl.multiple_of(head * cols, cols), cols),
    )


def pack_kernel(codes, source, packed):
    slots, rows, cols = packed.shape

    def one(slot, carry):
        packed[slot] = source[tile_of(jnp.maximum(codes[slot], 0), rows, cols)]
        return carry

    lax.fori_loop(0, slots, one, 0, unroll=4)


def add_slots(codes, terms, wide, first, count):
    rows, cols = terms.shape[1:]
    for item in range(count):
        slot = first + item
        code = codes[slot]
        code = jnp.where(code < 0, 2 << HEAD_BITS, code)
        wide[tile_of(code, rows, cols)] += terms[slot].astype(jnp.float32)


def add_terms(codes, terms, wide, parts):
    wide[...] = jnp.zeros_like(wide)
    step = terms.shape[0] // parts

    def one_part(part, carry):
        add_slots(codes, terms, wide, part * step, step)
        return carry

    lax.fori_loop(0, parts, one_part, 0)


def send_columns(ready, total, sent, parts, fill):
    width = total.shape[1] // parts
    copies = []
    for part in range(parts):
        columns = pl.ds(part * width, width)
        fill(columns)
        copies.append(copy(ready.at[:, columns], total.at[:, columns], sent.at[part]))
        copies[-1].start()
    for one in copies:
        one.wait()


def sum_kernel(parts, codes, terms, total, wide, ready, sent):
    add_terms(codes, terms, wide, parts)
    rows = total.shape[0]

    def fill(columns):
        ready[:, columns] = wide[:rows, columns].astype(ready.dtype)

    send_columns(ready, total, sent, sent.shape[0], fill)


def join_kernel(
    parts, codes, keys, head_part, terms, key_out, total, wide, ready, head, sent, got, put
):
    head_copy = copy(head_part, head, got)
    head_copy.start()
    key_copy = copy(keys, key_out, put)
    key_copy.start()
    add_terms(codes, terms, wide, parts)
    head_copy.wait()
    tail_rows = terms.shape[1]
    head_rows = total.shape[0] // 2 - tail_rows

    def fill(columns):
        for block in range(2):
            start = block * (head_rows + tail_rows)
            middle = start + head_rows
            ready[start:middle, columns] = head[
                block * head_rows : (block + 1) * head_rows, columns
            ]
            ready[middle : middle + tail_rows, columns] = wide[
                block * tail_rows : (block + 1) * tail_rows, columns
            ].astype(ready.dtype)

    send_columns(ready, total, sent, sent.shape[0], fill)
    key_copy.wait()


def place_kernel(source, out):
    out[...] = source[...]


def weights_of(query, key, length, list_size, scale):
    scores = lax.dot_general(key, query, NT, preferred_element_type=jnp.float32)
    row_max = jnp.max(scores, axis=0, keepdims=True)
    exp_scores = jnp.exp2((scores - row_max) * (scale * math.log2(math.e)))
    rows = key.shape[0] // list_size
    parts = [exp_scores[item * rows : (item + 1) * rows] for item in range(list_size)]
    kept = [jnp.where(item < length, 1.0, 0.0).astype(jnp.float32) for item in range(list_size)]
    total = sum(keep * jnp.sum(part, axis=0, keepdims=True) for keep, part in zip(kept, parts))
    inverse = 1.0 / total
    return [part * (inverse * keep) for keep, part in zip(kept, parts)]


class Grouped:
    def __init__(self, places, lengths, list_size, group, cols):
        self.places, self.lengths = places, lengths
        self.list_size, self.group, self.cols = list_size, group, cols
        self.groups = lengths.shape[0] // group

    def head(self, head):
        return pl.ds(pl.multiple_of(head * self.cols, self.cols), self.cols)

    def wide(self, index, source, held, sems):
        width = self.group * self.cols
        columns = pl.ds(pl.multiple_of(index * width, width), width)
        return copy(source.at[:, columns], held.at[:, columns], sems.at[index])

    def fetches(self, index, sources, tiles):
        made = [self.wide(index, *source) for source in sources]
        count = self.group * self.list_size
        for item in range(count):
            entry = index * count + item
            for source, held, sems in tiles:
                made.append(
                    copy(source.at[self.places[entry]], held.at[entry], sems.at[entry])
                )
        return made

    def puts(self, entry, made, outs, sems):
        start, copies = 0, []
        for which, out in enumerate(outs):
            count = out.shape[1]
            copies.append(
                copy(
                    made.at[entry, pl.ds(start, count)],
                    out.at[self.places[entry]],
                    sems.at[which, entry],
                )
            )
            start += count
        return copies

    def each_put(self, head, made, outs, sems, act):
        for item in range(self.list_size):

            @pl.when(item < self.lengths[head])
            def _():
                for one in self.puts(head * self.list_size + item, made, outs, sems):
                    act(one)

    def run(self, sources, tiles, made, outs, sems, compute, finish=None):
        def start(index):
            for one in self.fetches(index, sources, tiles):
                one.start()

        start(0)

        def one_group(index, carry):
            @pl.when(index + 1 < self.groups)
            def _():
                start(index + 1)

            for one in self.fetches(index, sources, tiles):
                one.wait()
            for item in range(self.group):
                head = index * self.group + item
                terms = compute(head)
                entries = pl.ds(head * self.list_size, self.list_size)
                made[entries] = terms.reshape(self.list_size, -1, self.cols)
                self.each_put(head, made, outs, sems, lambda one: one.start())
            if finish is not None:
                finish(index).start()
            return carry

        lax.fori_loop(0, self.groups, one_group, 0)

        def last(head, carry):
            self.each_put(head, made, outs, sems, lambda one: one.wait())
            return carry

        lax.fori_loop(0, self.lengths.shape[0], last, 0)
        if finish is not None:
            for index in range(self.groups):
                finish(index).wait()


def value_kernel(
    list_size, group, scale, places, lengths, queries, grads, keys, first, last,
    query_held, grad_held, key_held, made, query_sem, grad_sem, key_sem, out_sem,
):
    cols = keys.shape[2]
    walk = Grouped(places, lengths, list_size, group, cols)

    def compute(head):
        columns = walk.head(head)
        key = key_held[pl.ds(head * list_size, list_size)].reshape(-1, cols)
        weights = weights_of(query_held[:, columns], key, lengths[head], list_size, scale)
        weights_low = jnp.concatenate([part.astype(jnp.bfloat16) for part in weights], axis=0)
        return lax.dot_general(
            weights_low, grad_held[:, columns], NN, preferred_element_type=jnp.float32
        ).astype(jnp.bfloat16)

    walk.run(
        [(queries, query_held, query_sem), (grads, grad_held, grad_sem)],
        [(keys, key_held, key_sem)],
        made,
        [first, last],
        out_sem,
        compute,
    )


def key_kernel(
    list_size, group, scale, places, lengths, queries, grads, keys, values, query_grad, terms,
    query_held, grad_held, key_held, value_held, made, query_made,
    query_sem, grad_sem, key_sem, value_sem, out_sem, query_out_sem,
):
    rows, cols = keys.shape[1:]
    walk = Grouped(places, lengths, list_size, group, cols)

    def compute(head):
        columns = walk.head(head)
        entries = pl.ds(head * list_size, list_size)
        query = query_held[:, columns]
        key = key_held[entries].reshape(-1, cols)
        value = value_held[entries].reshape(-1, cols)
        weights = weights_of(query, key, lengths[head], list_size, scale)
        weights_low = [part.astype(jnp.bfloat16).astype(jnp.float32) for part in weights]
        joined = lax.dot_general(
            value, grad_held[:, columns], NT, preferred_element_type=jnp.float32
        )
        dweights = [joined[item * rows : (item + 1) * rows] for item in range(list_size)]
        row_delta = sum(
            jnp.sum(low * part, axis=0, keepdims=True)
            for low, part in zip(weights_low, dweights)
        )
        dscores = jnp.concatenate(
            [
                (weight * (part - row_delta)).astype(jnp.bfloat16)
                for weight, part in zip(weights, dweights)
            ],
            axis=0,
        )
        flipped = lax.dot_general(key, dscores, TN, preferred_element_type=jnp.float32)
        query_made[:, columns] = (flipped * scale).astype(jnp.bfloat16).T
        made_terms = lax.dot_general(dscores, query, NN, preferred_element_type=jnp.float32)
        return (made_terms * scale).astype(jnp.bfloat16)

    def finish(index):
        width = group * cols
        columns = pl.ds(pl.multiple_of(index * width, width), width)
        return copy(
            query_made.at[:, columns], query_grad.at[:, columns], query_out_sem.at[index]
        )

    walk.run(
        [(queries, query_held, query_sem), (grads, grad_held, grad_sem)],
        [(keys, key_held, key_sem), (values, value_held, value_sem)],
        made,
        [terms],
        out_sem,
        compute,
        finish,
    )


def local(queries, keys, values, out_grad, key_blocks, list_lengths):
    ctx_count = lax.axis_size("ctx")
    my_index = lax.axis_index("ctx")
    row_count, column_count = queries.shape[1:]
    head_count = list_lengths.shape[2]
    head_dim = column_count // head_count
    list_size = key_blocks.shape[3]
    block_rows = row_count // 2
    entries = head_count * list_size
    capacity = (entries + ctx_count - 1) // ctx_count
    slots = ctx_count * capacity
    scale = 1.0 / math.sqrt(head_dim)
    group = 4 if head_count % 4 == 0 else 1
    groups = head_count // group

    chosen = key_blocks[0]
    lengths = list_lengths[0]
    items = jnp.arange(list_size, dtype=jnp.int32)
    heads = jnp.arange(head_count, dtype=jnp.int32)
    is_used = items[None, None, :] < lengths[:, :, None]
    is_mine = is_used & ((chosen >> 1) == my_index)
    hit = jnp.sum(jnp.where(is_mine, 1 + (chosen & 1), 0), axis=2)
    rank = jnp.sum(
        jnp.where((heads[None, None, :] < heads[None, :, None]) & (hit[:, None, :] > 0), 1, 0),
        axis=2,
    )
    code = ((hit - 1) << HEAD_BITS) + heads[None, :]
    ranks = jnp.arange(capacity, dtype=jnp.int32)
    codes = jnp.max(
        jnp.where(
            (hit[:, None, :] > 0) & (rank[:, None, :] == ranks[None, :, None]),
            code[:, None, :],
            -1,
        ),
        axis=2,
    ).reshape(slots)

    my_lengths = lax.dynamic_index_in_dim(lengths, my_index, 0, keepdims=False)
    my_chosen = lax.dynamic_index_in_dim(chosen, my_index, 0, keepdims=False)
    my_used = items[None, :] < my_lengths[:, None]
    my_holder = jnp.where(my_used, my_chosen >> 1, -1)
    earlier = (heads[None, None, :, None] < heads[:, None, None, None]) & (
        my_holder[None, None, :, :] == my_holder[:, :, None, None]
    )
    my_rank = jnp.sum(jnp.where(earlier, 1, 0), axis=(2, 3))
    places = my_holder * capacity + my_rank
    places = jnp.where(my_used, places, places[:, :1]).reshape(entries)

    first_rows = block_rows // 2
    last_rows = block_rows - first_rows
    add_parts = 8 if slots % 8 == 0 else 1
    send_parts = 5 if head_count % 5 == 0 else 1
    flat_shape = jax.ShapeDtypeStruct((row_count, column_count), jnp.bfloat16)
    dma = pltpu.SemaphoreType.DMA

    def vmem(*shape):
        return pltpu.VMEM(shape, jnp.bfloat16)

    def packed_shape(rows):
        return jax.ShapeDtypeStruct((slots, rows, head_dim), jnp.bfloat16)

    def exchanged(packed):
        parts = packed.reshape(ctx_count, capacity, *packed.shape[1:])
        parts = lax.all_to_all(parts, "ctx", split_axis=0, concat_axis=0, tiled=True)
        return parts.reshape(packed.shape)

    def pack(name, source):
        return pl.pallas_call(
            pack_kernel,
            out_shape=packed_shape(block_rows),
            in_specs=[SMEM, VMEM],
            out_specs=VMEM,
            compiler_params=PARAMS,
            name=name,
        )(codes, source)

    def near(value):
        return pltpu.with_memory_space_constraint(value, pltpu.VMEM)

    def wide_sum(rows):
        return pltpu.VMEM((3 * rows, column_count), jnp.float32)

    def add_up(name, returned):
        rows = returned.shape[1]
        return pl.pallas_call(
            functools.partial(sum_kernel, add_parts),
            out_shape=jax.ShapeDtypeStruct((2 * rows, column_count), jnp.bfloat16),
            in_specs=[SMEM, VMEM],
            out_specs=ANY,
            scratch_shapes=[wide_sum(rows), vmem(2 * rows, column_count), dma((send_parts,))],
            compiler_params=PARAMS,
            name=name,
        )(codes, returned)

    flat = vmem(row_count, column_count)
    tiles = vmem(entries, block_rows, head_dim)
    wide_sem, tile_sem = dma((groups,)), dma((entries,))
    fetched_keys = exchanged(pack("pack_keys", keys[0]))
    handed_codes = shifted(codes, "section", -1)
    packed_values, handed_codes = lax.optimization_barrier(
        (pack("pack_values", values[0]), handed_codes)
    )
    fetched_values = exchanged(packed_values)
    first_terms, last_terms = pl.pallas_call(
        functools.partial(value_kernel, list_size, group, scale),
        out_shape=(packed_shape(first_rows), packed_shape(last_rows)),
        in_specs=[SMEM, SMEM, ANY, ANY, ANY],
        out_specs=(ANY, ANY),
        scratch_shapes=[flat, flat, tiles, tiles]
        + [wide_sem, wide_sem, tile_sem, dma((2, entries))],
        compiler_params=PARAMS,
        name="value_terms",
    )(places, my_lengths, queries[0], out_grad[0], fetched_keys)
    handed_terms = shifted(last_terms, "section", -1)
    query_grad, key_terms = pl.pallas_call(
        functools.partial(key_kernel, list_size, group, scale),
        out_shape=(flat_shape, packed_shape(block_rows)),
        in_specs=[SMEM, SMEM, ANY, ANY, ANY, ANY],
        out_specs=(ANY, ANY),
        scratch_shapes=[flat, flat, tiles, tiles, tiles, flat]
        + [wide_sem, wide_sem, tile_sem, tile_sem, dma((1, entries)), wide_sem],
        compiler_params=PARAMS,
        name="key_terms",
    )(places, my_lengths, queries[0], out_grad[0], fetched_keys, fetched_values)
    handed_queries = shifted(query_grad, "section", -1)
    first_values = add_up("sum_values", exchanged(first_terms))
    handed_first = shifted(first_values, "section", -1)
    key_terms, handed_terms = lax.optimization_barrier((key_terms, handed_terms))
    returned_keys = exchanged(key_terms)
    handed_queries = pl.pallas_call(
        place_kernel,
        out_shape=flat_shape,
        in_specs=[VMEM],
        out_specs=VMEM,
        compiler_params=PARAMS,
        name="place_queries",
    )(near(handed_queries))
    returned_keys, handed_queries, handed_first = lax.optimization_barrier(
        (returned_keys, handed_queries, handed_first)
    )
    key_grad = add_up("sum_keys", near(returned_keys))
    key_grad, handed_terms = lax.optimization_barrier((key_grad, handed_terms))
    handed_keys = shifted(key_grad, "section", -1)
    handed_keys, handed_values = pl.pallas_call(
        functools.partial(join_kernel, add_parts),
        out_shape=(flat_shape, flat_shape),
        in_specs=[SMEM, VMEM, ANY, VMEM],
        out_specs=(ANY, ANY),
        scratch_shapes=[wide_sum(last_rows), flat, vmem(2 * first_rows, column_count)]
        + [dma((send_parts,)), dma, dma],
        compiler_params=PARAMS,
        name="join_values",
    )(handed_codes, near(handed_keys), handed_first, near(exchanged(handed_terms)))
    return (handed_queries[None], handed_keys[None], handed_values[None])


def solution(mesh):
    placed = (
        P("section", "ctx", None),
        P("section", "ctx", None),
        P("section", "ctx", None),
        P("section", "ctx", None),
        P("section", None, None, None),
        P("section", None, None),
    )
    return jax.shard_map(
        local,
        mesh=mesh,
        in_specs=placed,
        out_specs=(P("section", "ctx", None), P("section", "ctx", None), P("section", "ctx", None)),
        check_vma=False,
    )
```

```python
import functools
import math

import jax
import jax.numpy as jnp
from jax import lax
from jax.experimental import pallas as pl
from jax.experimental.pallas import tpu as pltpu
from jax.sharding import PartitionSpec as P

HEAD_BITS = 8
VMEM = pl.BlockSpec(memory_space=pltpu.VMEM)
SMEM = pl.BlockSpec(memory_space=pltpu.SMEM)
ANY = pl.BlockSpec(memory_space=pl.ANY)
PARAMS = pltpu.CompilerParams(vmem_limit_bytes=56 * 1024 * 1024)
NT = (((1,), (1,)), ((), ()))
NN = (((1,), (0,)), ((), ()))
TN = (((0,), (0,)), ((), ()))
copy = pltpu.make_async_copy


def shifted(value, axis, steps):
    count = lax.axis_size(axis)
    pairs = [(source, (source + steps) % count) for source in range(count)]
    return lax.ppermute(value, axis, pairs)


def tile_of(code, rows, cols):
    block = lax.shift_right_logical(code, HEAD_BITS)
    head = lax.bitwise_and(code, (1 << HEAD_BITS) - 1)
    return (
        pl.ds(pl.multiple_of(block * rows, rows), rows),
        pl.ds(pl.multiple_of(head * cols, cols), cols),
    )


def pack_kernel(parts, codes, source, packed, held, made, got, sent):
    slots, rows, cols = packed.shape
    step = slots // parts
    whole = copy(source, held, got)
    whole.start()
    whole.wait()

    def part_of(part):
        where = pl.ds(part * step, step)
        return copy(made.at[where], packed.at[where], sent.at[part])

    def one_part(part, carry):
        for item in range(step):
            slot = part * step + item
            made[slot] = held[tile_of(jnp.maximum(codes[slot], 0), rows, cols)]
        part_of(part).start()
        return carry

    lax.fori_loop(0, parts, one_part, 0)
    for part in range(parts):
        part_of(part).wait()


def add_slots(codes, terms, wide, first, count):
    rows, cols = terms.shape[1:]
    for item in range(count):
        slot = first + item
        code = codes[slot]
        code = jnp.where(code < 0, 2 << HEAD_BITS, code)
        wide[tile_of(code, rows, cols)] += terms[slot].astype(jnp.float32)


def add_terms(codes, terms, wide, parts):
    wide[...] = jnp.zeros_like(wide)
    step = terms.shape[0] // parts

    def one_part(part, carry):
        add_slots(codes, terms, wide, part * step, step)
        return carry

    lax.fori_loop(0, parts, one_part, 0)


def send_columns(ready, total, sent, parts, fill):
    width = total.shape[1] // parts
    copies = []
    for part in range(parts):
        columns = pl.ds(part * width, width)
        fill(columns)
        copies.append(copy(ready.at[:, columns], total.at[:, columns], sent.at[part]))
        copies[-1].start()
    for one in copies:
        one.wait()


def sum_kernel(parts, codes, terms, total, wide, ready, sent):
    add_terms(codes, terms, wide, parts)
    rows = total.shape[0]

    def fill(columns):
        ready[:, columns] = wide[:rows, columns].astype(ready.dtype)

    send_columns(ready, total, sent, sent.shape[0], fill)


def join_kernel(
    parts, codes, keys, head_part, terms, key_out, total,
    wide, ready, head, key_held, sent, got, key_got, put,
):
    head_copy = copy(head_part, head, got)
    head_copy.start()
    key_in = copy(keys, key_held, key_got)
    key_in.start()
    add_terms(codes, terms, wide, parts)
    key_in.wait()
    key_copy = copy(key_held, key_out, put)
    key_copy.start()
    head_copy.wait()
    tail_rows = terms.shape[1]
    head_rows = total.shape[0] // 2 - tail_rows

    def fill(columns):
        for block in range(2):
            start = block * (head_rows + tail_rows)
            middle = start + head_rows
            ready[start:middle, columns] = head[
                block * head_rows : (block + 1) * head_rows, columns
            ]
            ready[middle : middle + tail_rows, columns] = wide[
                block * tail_rows : (block + 1) * tail_rows, columns
            ].astype(ready.dtype)

    send_columns(ready, total, sent, sent.shape[0], fill)
    key_copy.wait()


def place_kernel(source, out):
    out[...] = source[...]


def weights_of(query, key, length, list_size, scale):
    scores = lax.dot_general(key, query, NT, preferred_element_type=jnp.float32)
    row_max = jnp.max(scores, axis=0, keepdims=True)
    exp_scores = jnp.exp2((scores - row_max) * (scale * math.log2(math.e)))
    rows = key.shape[0] // list_size
    parts = [exp_scores[item * rows : (item + 1) * rows] for item in range(list_size)]
    kept = [jnp.where(item < length, 1.0, 0.0).astype(jnp.float32) for item in range(list_size)]
    total = sum(keep * jnp.sum(part, axis=0, keepdims=True) for keep, part in zip(kept, parts))
    inverse = 1.0 / total
    return [part * (inverse * keep) for keep, part in zip(kept, parts)]


class Grouped:
    def __init__(self, places, lengths, list_size, group, cols):
        self.places, self.lengths = places, lengths
        self.list_size, self.group, self.cols = list_size, group, cols
        self.groups = lengths.shape[0] // group

    def head(self, head):
        return pl.ds(pl.multiple_of(head * self.cols, self.cols), self.cols)

    def wide(self, index, source, held, sems):
        width = self.group * self.cols
        columns = pl.ds(pl.multiple_of(index * width, width), width)
        return copy(source.at[:, columns], held.at[:, columns], sems.at[index])

    def block(self, index, source, held, sems):
        where = pl.ds(index * self.group, self.group)
        return copy(source.at[where], held.at[where], sems.at[index])

    def fetches(self, index, sources, tiles, blocks):
        made = [self.wide(index, *source) for source in sources]
        made += [self.block(index, *source) for source in blocks]
        count = self.group * self.list_size
        for item in range(count):
            entry = index * count + item
            for source, held, sems in tiles:
                made.append(
                    copy(source.at[self.places[entry]], held.at[entry], sems.at[entry])
                )
        return made

    def puts(self, entry, made, outs, sems):
        start, copies = 0, []
        for which, out in enumerate(outs):
            count = out.shape[1]
            copies.append(
                copy(
                    made.at[entry, pl.ds(start, count)],
                    out.at[self.places[entry]],
                    sems.at[which, entry],
                )
            )
            start += count
        return copies

    def each_put(self, head, made, outs, sems, act):
        for item in range(self.list_size):

            @pl.when(item < self.lengths[head])
            def _():
                for one in self.puts(head * self.list_size + item, made, outs, sems):
                    act(one)

    def run(self, sources, tiles, blocks, made, outs, sems, compute, finish):
        def start(index):
            for one in self.fetches(index, sources, tiles, blocks):
                one.start()

        start(0)

        def one_group(index, carry):
            @pl.when(index + 1 < self.groups)
            def _():
                start(index + 1)

            for one in self.fetches(index, sources, tiles, blocks):
                one.wait()
            for item in range(self.group):
                head = index * self.group + item
                terms = compute(head)
                entries = pl.ds(head * self.list_size, self.list_size)
                made[entries] = terms.reshape(self.list_size, -1, self.cols)
                self.each_put(head, made, outs, sems, lambda one: one.start())
            finish(index).start()
            return carry

        lax.fori_loop(0, self.groups, one_group, 0)

        def last(head, carry):
            self.each_put(head, made, outs, sems, lambda one: one.wait())
            return carry

        lax.fori_loop(0, self.lengths.shape[0], last, 0)
        for index in range(self.groups):
            finish(index).wait()


def value_kernel(
    list_size, group, scale, places, lengths, queries, grads, keys, first, last, weights_out,
    query_held, grad_held, key_held, made, weights_made,
    query_sem, grad_sem, key_sem, out_sem, weights_sem,
):
    rows, cols = keys.shape[1:]
    walk = Grouped(places, lengths, list_size, group, cols)

    def compute(head):
        columns = walk.head(head)
        key = key_held[pl.ds(head * list_size, list_size)].reshape(-1, cols)
        weights = weights_of(query_held[:, columns], key, lengths[head], list_size, scale)
        for item, part in enumerate(weights):
            weights_made[head, item * rows : (item + 1) * rows] = part
        weights_low = jnp.concatenate([part.astype(jnp.bfloat16) for part in weights], axis=0)
        return lax.dot_general(
            weights_low, grad_held[:, columns], NN, preferred_element_type=jnp.float32
        ).astype(jnp.bfloat16)

    walk.run(
        [(queries, query_held, query_sem), (grads, grad_held, grad_sem)],
        [(keys, key_held, key_sem)],
        [],
        made,
        [first, last],
        out_sem,
        compute,
        lambda index: walk.block(index, weights_made, weights_out, weights_sem),
    )


def key_kernel(
    list_size, group, scale, places, lengths, queries, grads, keys, values, weights,
    query_grad, terms,
    query_held, grad_held, key_held, value_held, weights_held, made, query_made,
    query_sem, grad_sem, key_sem, value_sem, weights_sem, out_sem, query_out_sem,
):
    cols = keys.shape[2]
    walk = Grouped(places, lengths, list_size, group, cols)

    def compute(head):
        columns = walk.head(head)
        entries = pl.ds(head * list_size, list_size)
        key = key_held[entries].reshape(-1, cols)
        value = value_held[entries].reshape(-1, cols)
        weight = weights_held[head]
        weight_low = weight.astype(jnp.bfloat16).astype(jnp.float32)
        dweights = lax.dot_general(
            value, grad_held[:, columns], NT, preferred_element_type=jnp.float32
        )
        row_delta = jnp.sum(weight_low * dweights, axis=0, keepdims=True)
        dscores = (weight * (dweights - row_delta)).astype(jnp.bfloat16)
        flipped = lax.dot_general(key, dscores, TN, preferred_element_type=jnp.float32)
        query_made[:, columns] = (flipped * scale).astype(jnp.bfloat16).T
        made_terms = lax.dot_general(
            dscores, query_held[:, columns], NN, preferred_element_type=jnp.float32
        )
        return (made_terms * scale).astype(jnp.bfloat16)

    walk.run(
        [(queries, query_held, query_sem), (grads, grad_held, grad_sem)],
        [(keys, key_held, key_sem), (values, value_held, value_sem)],
        [(weights, weights_held, weights_sem)],
        made,
        [terms],
        out_sem,
        compute,
        lambda index: walk.wide(index, query_made, query_grad, query_out_sem),
    )


def local(queries, keys, values, out_grad, key_blocks, list_lengths):
    ctx_count = lax.axis_size("ctx")
    my_index = lax.axis_index("ctx")
    row_count, column_count = queries.shape[1:]
    head_count = list_lengths.shape[2]
    head_dim = column_count // head_count
    list_size = key_blocks.shape[3]
    block_rows = row_count // 2
    entries = head_count * list_size
    capacity = (entries + ctx_count - 1) // ctx_count
    slots = ctx_count * capacity
    scale = 1.0 / math.sqrt(head_dim)
    group = 4 if head_count % 4 == 0 else 1
    groups = head_count // group

    chosen = key_blocks[0]
    lengths = list_lengths[0]
    items = jnp.arange(list_size, dtype=jnp.int32)
    heads = jnp.arange(head_count, dtype=jnp.int32)
    is_used = items[None, None, :] < lengths[:, :, None]
    is_mine = is_used & ((chosen >> 1) == my_index)
    hit = jnp.sum(jnp.where(is_mine, 1 + (chosen & 1), 0), axis=2)
    rank = jnp.sum(
        jnp.where((heads[None, None, :] < heads[None, :, None]) & (hit[:, None, :] > 0), 1, 0),
        axis=2,
    )
    code = ((hit - 1) << HEAD_BITS) + heads[None, :]
    ranks = jnp.arange(capacity, dtype=jnp.int32)
    codes = jnp.max(
        jnp.where(
            (hit[:, None, :] > 0) & (rank[:, None, :] == ranks[None, :, None]),
            code[:, None, :],
            -1,
        ),
        axis=2,
    ).reshape(slots)

    my_lengths = lax.dynamic_index_in_dim(lengths, my_index, 0, keepdims=False)
    my_chosen = lax.dynamic_index_in_dim(chosen, my_index, 0, keepdims=False)
    my_used = items[None, :] < my_lengths[:, None]
    my_holder = jnp.where(my_used, my_chosen >> 1, -1)
    earlier = (heads[None, None, :, None] < heads[:, None, None, None]) & (
        my_holder[None, None, :, :] == my_holder[:, :, None, None]
    )
    my_rank = jnp.sum(jnp.where(earlier, 1, 0), axis=(2, 3))
    places = my_holder * capacity + my_rank
    places = jnp.where(my_used, places, places[:, :1]).reshape(entries)

    first_rows = 3 * block_rows // 8
    last_rows = block_rows - first_rows
    add_parts = 8 if slots % 8 == 0 else 1
    send_parts = 5 if head_count % 5 == 0 else 1
    flat_shape = jax.ShapeDtypeStruct((row_count, column_count), jnp.bfloat16)
    dma = pltpu.SemaphoreType.DMA

    def vmem(*shape):
        return pltpu.VMEM(shape, jnp.bfloat16)

    flat = vmem(row_count, column_count)

    def packed_shape(rows):
        return jax.ShapeDtypeStruct((slots, rows, head_dim), jnp.bfloat16)

    def exchanged(packed):
        parts = packed.reshape(ctx_count, capacity, *packed.shape[1:])
        parts = lax.all_to_all(parts, "ctx", split_axis=0, concat_axis=0, tiled=True)
        return parts.reshape(packed.shape)

    def pack(name, source):
        return pl.pallas_call(
            functools.partial(pack_kernel, add_parts),
            out_shape=packed_shape(block_rows),
            in_specs=[SMEM, ANY],
            out_specs=ANY,
            scratch_shapes=[flat, vmem(slots, block_rows, head_dim), dma, dma((add_parts,))],
            compiler_params=PARAMS,
            name=name,
        )(codes, source)

    def near(value):
        return pltpu.with_memory_space_constraint(value, pltpu.VMEM)

    def wide_sum(rows):
        return pltpu.VMEM((3 * rows, column_count), jnp.float32)

    def add_up(name, returned):
        rows = returned.shape[1]
        return pl.pallas_call(
            functools.partial(sum_kernel, add_parts),
            out_shape=jax.ShapeDtypeStruct((2 * rows, column_count), jnp.bfloat16),
            in_specs=[SMEM, VMEM],
            out_specs=ANY,
            scratch_shapes=[wide_sum(rows), vmem(2 * rows, column_count), dma((send_parts,))],
            compiler_params=PARAMS,
            name=name,
        )(codes, returned)

    tiles = vmem(entries, block_rows, head_dim)
    wide_sem, tile_sem = dma((groups,)), dma((entries,))
    fetched_keys = exchanged(pack("pack_keys", keys[0]))
    handed_codes = shifted(codes, "section", -1)
    packed_values, handed_codes = lax.optimization_barrier(
        (pack("pack_values", values[0]), handed_codes)
    )
    fetched_values = exchanged(packed_values)
    weights_shape = (head_count, list_size * block_rows, row_count)
    weights_tile = pltpu.VMEM(weights_shape, jnp.float32)
    first_terms, last_terms, weights = pl.pallas_call(
        functools.partial(value_kernel, list_size, group, scale),
        out_shape=(
            packed_shape(first_rows),
            packed_shape(last_rows),
            jax.ShapeDtypeStruct(weights_shape, jnp.float32),
        ),
        in_specs=[SMEM, SMEM, ANY, ANY, ANY],
        out_specs=(ANY, ANY, ANY),
        scratch_shapes=[flat, flat, tiles, tiles, weights_tile]
        + [wide_sem, wide_sem, tile_sem, dma((2, entries)), wide_sem],
        compiler_params=PARAMS,
        name="value_terms",
    )(places, my_lengths, queries[0], out_grad[0], fetched_keys)
    handed_terms = shifted(last_terms, "section", -1)
    query_grad, key_terms = pl.pallas_call(
        functools.partial(key_kernel, list_size, group, scale),
        out_shape=(flat_shape, packed_shape(block_rows)),
        in_specs=[SMEM, SMEM, ANY, ANY, ANY, ANY, ANY],
        out_specs=(ANY, ANY),
        scratch_shapes=[flat, flat, tiles, tiles, weights_tile, tiles, flat]
        + [wide_sem, wide_sem, tile_sem, tile_sem, wide_sem, dma((1, entries)), wide_sem],
        compiler_params=PARAMS,
        name="key_terms",
    )(places, my_lengths, queries[0], out_grad[0], fetched_keys, fetched_values, weights)
    handed_queries = shifted(query_grad, "section", -1)
    first_values = add_up("sum_values", exchanged(first_terms))
    handed_first = shifted(first_values, "section", -1)
    key_terms, handed_terms = lax.optimization_barrier((key_terms, handed_terms))
    returned_keys = exchanged(key_terms)
    handed_queries = pl.pallas_call(
        place_kernel,
        out_shape=flat_shape,
        in_specs=[VMEM],
        out_specs=VMEM,
        compiler_params=PARAMS,
        name="place_queries",
    )(near(handed_queries))
    returned_keys, handed_queries, handed_first = lax.optimization_barrier(
        (returned_keys, handed_queries, handed_first)
    )
    key_grad = add_up("sum_keys", near(returned_keys))
    key_grad, handed_terms = lax.optimization_barrier((key_grad, handed_terms))
    handed_keys = shifted(key_grad, "section", -1)
    handed_keys, handed_values = pl.pallas_call(
        functools.partial(join_kernel, add_parts),
        out_shape=(flat_shape, flat_shape),
        in_specs=[SMEM, ANY, ANY, VMEM],
        out_specs=(ANY, ANY),
        scratch_shapes=[wide_sum(last_rows), flat, vmem(2 * first_rows, column_count), flat]
        + [dma((send_parts,)), dma, dma, dma],
        compiler_params=PARAMS,
        name="join_values",
    )(handed_codes, handed_keys, handed_first, near(exchanged(handed_terms)))
    return (handed_queries[None], handed_keys[None], handed_values[None])


def solution(mesh):
    placed = (
        P("section", "ctx", None),
        P("section", "ctx", None),
        P("section", "ctx", None),
        P("section", "ctx", None),
        P("section", None, None, None),
        P("section", None, None),
    )
    return jax.shard_map(
        local,
        mesh=mesh,
        in_specs=placed,
        out_specs=(P("section", "ctx", None), P("section", "ctx", None), P("section", "ctx", None)),
        check_vma=False,
    )
```

```python
import functools
import math

import jax
import jax.numpy as jnp
from jax import lax
from jax.experimental import pallas as pl
from jax.experimental.pallas import tpu as pltpu
from jax.sharding import PartitionSpec as P

HEAD_BITS = 8
VMEM = pl.BlockSpec(memory_space=pltpu.VMEM)
SMEM = pl.BlockSpec(memory_space=pltpu.SMEM)
ANY = pl.BlockSpec(memory_space=pl.ANY)
PARAMS = pltpu.CompilerParams(vmem_limit_bytes=56 * 1024 * 1024)
NT = (((1,), (1,)), ((), ()))
NN = (((1,), (0,)), ((), ()))
TN = (((0,), (0,)), ((), ()))
copy = pltpu.make_async_copy


def shifted(value, axis, steps):
    count = lax.axis_size(axis)
    pairs = [(source, (source + steps) % count) for source in range(count)]
    return lax.ppermute(value, axis, pairs)


def tile_of(code, rows, cols):
    block = lax.shift_right_logical(code, HEAD_BITS)
    head = lax.bitwise_and(code, (1 << HEAD_BITS) - 1)
    return (
        pl.ds(pl.multiple_of(block * rows, rows), rows),
        pl.ds(pl.multiple_of(head * cols, cols), cols),
    )


def pack_kernel(parts, codes, source, packed, held, made, got, sent):
    slots, rows, cols = packed.shape
    step = slots // parts
    whole = copy(source, held, got)
    whole.start()
    whole.wait()

    def part_of(part):
        where = pl.ds(part * step, step)
        return copy(made.at[where], packed.at[where], sent.at[part])

    def one_part(part, carry):
        for item in range(step):
            slot = part * step + item
            made[slot] = held[tile_of(jnp.maximum(codes[slot], 0), rows, cols)]
        part_of(part).start()
        return carry

    lax.fori_loop(0, parts, one_part, 0)
    for part in range(parts):
        part_of(part).wait()


def add_slots(codes, terms, wide, first, count):
    rows, cols = terms.shape[1:]
    for item in range(count):
        slot = first + item
        code = codes[slot]
        code = jnp.where(code < 0, 2 << HEAD_BITS, code)
        wide[tile_of(code, rows, cols)] += terms[slot].astype(jnp.float32)


def add_terms(codes, terms, wide, parts):
    wide[...] = jnp.zeros_like(wide)
    step = terms.shape[0] // parts

    def one_part(part, carry):
        add_slots(codes, terms, wide, part * step, step)
        return carry

    lax.fori_loop(0, parts, one_part, 0)


def send_columns(ready, total, sent, parts, fill):
    width = total.shape[1] // parts
    copies = []
    for part in range(parts):
        columns = pl.ds(part * width, width)
        fill(columns)
        copies.append(copy(ready.at[:, columns], total.at[:, columns], sent.at[part]))
        copies[-1].start()
    for one in copies:
        one.wait()


def sum_kernel(parts, codes, terms, total, wide, ready, sent):
    add_terms(codes, terms, wide, parts)
    rows = total.shape[0]

    def fill(columns):
        ready[:, columns] = wide[:rows, columns].astype(ready.dtype)

    send_columns(ready, total, sent, sent.shape[0], fill)


def last_kernel(
    parts, codes, keys, terms, key_out, total, wide, ready, key_held, sent, key_got, put
):
    key_in = copy(keys, key_held, key_got)
    key_in.start()
    add_terms(codes, terms, wide, parts)
    key_in.wait()
    key_copy = copy(key_held, key_out, put)
    key_copy.start()
    rows = total.shape[0]

    def fill(columns):
        ready[:, columns] = wide[:rows, columns].astype(ready.dtype)

    send_columns(ready, total, sent, sent.shape[0], fill)
    key_copy.wait()


def place_kernel(source, out):
    out[...] = source[...]


def weights_of(query, key, length, list_size, scale):
    scores = lax.dot_general(key, query, NT, preferred_element_type=jnp.float32)
    row_max = jnp.max(scores, axis=0, keepdims=True)
    exp_scores = jnp.exp2((scores - row_max) * (scale * math.log2(math.e)))
    rows = key.shape[0] // list_size
    parts = [exp_scores[item * rows : (item + 1) * rows] for item in range(list_size)]
    kept = [jnp.where(item < length, 1.0, 0.0).astype(jnp.float32) for item in range(list_size)]
    total = sum(keep * jnp.sum(part, axis=0, keepdims=True) for keep, part in zip(kept, parts))
    inverse = 1.0 / total
    return [part * (inverse * keep) for keep, part in zip(kept, parts)]


class Grouped:
    def __init__(self, places, lengths, list_size, group, cols):
        self.places, self.lengths = places, lengths
        self.list_size, self.group, self.cols = list_size, group, cols
        self.groups = lengths.shape[0] // group

    def head(self, head):
        return pl.ds(pl.multiple_of(head * self.cols, self.cols), self.cols)

    def wide(self, index, source, held, sems):
        width = self.group * self.cols
        columns = pl.ds(pl.multiple_of(index * width, width), width)
        return copy(source.at[:, columns], held.at[:, columns], sems.at[index])

    def block(self, index, source, held, sems):
        where = pl.ds(index * self.group, self.group)
        return copy(source.at[where], held.at[where], sems.at[index])

    def fetches(self, index, sources, tiles, blocks):
        made = [self.wide(index, *source) for source in sources]
        made += [self.block(index, *source) for source in blocks]
        count = self.group * self.list_size
        for item in range(count):
            entry = index * count + item
            for source, held, sems in tiles:
                made.append(
                    copy(source.at[self.places[entry]], held.at[entry], sems.at[entry])
                )
        return made

    def puts(self, entry, made, outs, sems):
        start, copies = 0, []
        for which, out in enumerate(outs):
            count = out.shape[1]
            copies.append(
                copy(
                    made.at[entry, pl.ds(start, count)],
                    out.at[self.places[entry]],
                    sems.at[which, entry],
                )
            )
            start += count
        return copies

    def each_put(self, head, made, outs, sems, act):
        for item in range(self.list_size):

            @pl.when(item < self.lengths[head])
            def _():
                for one in self.puts(head * self.list_size + item, made, outs, sems):
                    act(one)

    def run(self, sources, tiles, blocks, made, outs, sems, compute, finish):
        def start(index):
            for one in self.fetches(index, sources, tiles, blocks):
                one.start()

        start(0)

        def one_group(index, carry):
            @pl.when(index + 1 < self.groups)
            def _():
                start(index + 1)

            for one in self.fetches(index, sources, tiles, blocks):
                one.wait()
            for item in range(self.group):
                head = index * self.group + item
                terms = compute(head)
                entries = pl.ds(head * self.list_size, self.list_size)
                made[entries] = terms.reshape(self.list_size, -1, self.cols)
                self.each_put(head, made, outs, sems, lambda one: one.start())
            finish(index).start()
            return carry

        lax.fori_loop(0, self.groups, one_group, 0)

        def last(head, carry):
            self.each_put(head, made, outs, sems, lambda one: one.wait())
            return carry

        lax.fori_loop(0, self.lengths.shape[0], last, 0)
        for index in range(self.groups):
            finish(index).wait()


def value_kernel(
    list_size, group, scale, places, lengths, queries, grads, keys, first, last, weights_out,
    query_held, grad_held, key_held, made, weights_made,
    query_sem, grad_sem, key_sem, out_sem, weights_sem,
):
    rows, cols = keys.shape[1:]
    walk = Grouped(places, lengths, list_size, group, cols)

    def compute(head):
        columns = walk.head(head)
        key = key_held[pl.ds(head * list_size, list_size)].reshape(-1, cols)
        weights = weights_of(query_held[:, columns], key, lengths[head], list_size, scale)
        for item, part in enumerate(weights):
            weights_made[head, item * rows : (item + 1) * rows] = part
        weights_low = jnp.concatenate([part.astype(jnp.bfloat16) for part in weights], axis=0)
        return lax.dot_general(
            weights_low, grad_held[:, columns], NN, preferred_element_type=jnp.float32
        ).astype(jnp.bfloat16)

    walk.run(
        [(queries, query_held, query_sem), (grads, grad_held, grad_sem)],
        [(keys, key_held, key_sem)],
        [],
        made,
        [first, last],
        out_sem,
        compute,
        lambda index: walk.block(index, weights_made, weights_out, weights_sem),
    )


def key_kernel(
    list_size, group, scale, places, lengths, queries, grads, keys, values, weights,
    query_grad, terms,
    query_held, grad_held, key_held, weights_held, made, query_made,
    query_sem, grad_sem, key_sem, weights_sem, out_sem, query_out_sem,
):
    rows, cols = keys.shape[1:]
    groups = lengths.shape[0] // group
    parts = out_sem.shape[0]
    step = keys.shape[0] // parts
    width = group * cols

    def columns_of(index):
        return pl.ds(pl.multiple_of(index * width, width), width)

    def fetches(index):
        columns = columns_of(index)
        heads = pl.ds(index * group, group)
        return [
            copy(grads.at[:, columns], grad_held.at[:, columns], grad_sem.at[index]),
            copy(weights.at[heads], weights_held.at[heads], weights_sem.at[index]),
            copy(queries.at[:, columns], query_held.at[:, columns], query_sem.at[index]),
        ]

    def key_part(part):
        where = pl.ds(part * step, step)
        return copy(keys.at[where], key_held.at[where], key_sem.at[part])

    def made_part(part):
        where = pl.ds(part * step, step)
        return copy(made.at[where], terms.at[where], out_sem.at[part])

    def query_part(index):
        columns = columns_of(index)
        return copy(
            query_made.at[:, columns], query_grad.at[:, columns], query_out_sem.at[index]
        )

    for one in fetches(0):
        one.start()
    for part in range(parts):
        key_part(part).start()

    def compute(head):
        columns = pl.ds(pl.multiple_of(head * cols, cols), cols)
        where = [places[head * list_size + item] for item in range(list_size)]
        key = jnp.concatenate([key_held[place] for place in where], axis=0)
        value = jnp.concatenate([values[place] for place in where], axis=0)
        weight = weights_held[head]
        weight_low = weight.astype(jnp.bfloat16).astype(jnp.float32)
        dweights = lax.dot_general(
            value, grad_held[:, columns], NT, preferred_element_type=jnp.float32
        )
        row_delta = jnp.sum(weight_low * dweights, axis=0, keepdims=True)
        dscores = (weight * (dweights - row_delta)).astype(jnp.bfloat16)
        flipped = lax.dot_general(key, dscores, TN, preferred_element_type=jnp.float32)
        query_made[:, columns] = (flipped * scale).astype(jnp.bfloat16).T
        made_terms = lax.dot_general(
            dscores, query_held[:, columns], NN, preferred_element_type=jnp.float32
        )
        return (made_terms * scale).astype(jnp.bfloat16)

    def one_group(index, carry):
        @pl.when(index + 1 < groups)
        def _():
            for one in fetches(index + 1):
                one.start()

        for one in fetches(index):
            one.wait()

        @pl.when(index == 0)
        def _():
            for part in range(parts):
                key_part(part).wait()

        results = [compute(index * group + item) for item in range(group)]
        query_part(index).start()
        for item, result in enumerate(results):
            head = index * group + item
            for entry in range(list_size):

                @pl.when(entry < lengths[head])
                def _():
                    made[places[head * list_size + entry]] = result[
                        entry * rows : (entry + 1) * rows
                    ]

        return carry

    lax.fori_loop(0, groups, one_group, 0)
    for part in range(parts):
        made_part(part).start()
    for index in range(groups):
        query_part(index).wait()
    for part in range(parts):
        made_part(part).wait()


def local(queries, keys, values, out_grad, key_blocks, list_lengths):
    ctx_count = lax.axis_size("ctx")
    my_index = lax.axis_index("ctx")
    row_count, column_count = queries.shape[1:]
    head_count = list_lengths.shape[2]
    head_dim = column_count // head_count
    list_size = key_blocks.shape[3]
    block_rows = row_count // 2
    entries = head_count * list_size
    capacity = (entries + ctx_count - 1) // ctx_count
    slots = ctx_count * capacity
    scale = 1.0 / math.sqrt(head_dim)
    group = 4 if head_count % 4 == 0 else 1
    groups = head_count // group

    chosen = key_blocks[0]
    lengths = list_lengths[0]
    items = jnp.arange(list_size, dtype=jnp.int32)
    heads = jnp.arange(head_count, dtype=jnp.int32)
    is_used = items[None, None, :] < lengths[:, :, None]
    is_mine = is_used & ((chosen >> 1) == my_index)
    hit = jnp.sum(jnp.where(is_mine, 1 + (chosen & 1), 0), axis=2)
    rank = jnp.sum(
        jnp.where((heads[None, None, :] < heads[None, :, None]) & (hit[:, None, :] > 0), 1, 0),
        axis=2,
    )
    code = ((hit - 1) << HEAD_BITS) + heads[None, :]
    ranks = jnp.arange(capacity, dtype=jnp.int32)
    codes = jnp.max(
        jnp.where(
            (hit[:, None, :] > 0) & (rank[:, None, :] == ranks[None, :, None]),
            code[:, None, :],
            -1,
        ),
        axis=2,
    ).reshape(slots)

    my_lengths = lax.dynamic_index_in_dim(lengths, my_index, 0, keepdims=False)
    my_chosen = lax.dynamic_index_in_dim(chosen, my_index, 0, keepdims=False)
    my_used = items[None, :] < my_lengths[:, None]
    my_holder = jnp.where(my_used, my_chosen >> 1, -1)
    earlier = (heads[None, None, :, None] < heads[:, None, None, None]) & (
        my_holder[None, None, :, :] == my_holder[:, :, None, None]
    )
    my_rank = jnp.sum(jnp.where(earlier, 1, 0), axis=(2, 3))
    places = my_holder * capacity + my_rank
    places = jnp.where(my_used, places, places[:, :1]).reshape(entries)

    first_rows = block_rows // 2
    last_rows = block_rows - first_rows
    add_parts = 8 if slots % 8 == 0 else 1
    send_parts = 5 if head_count % 5 == 0 else 1
    flat_shape = jax.ShapeDtypeStruct((row_count, column_count), jnp.bfloat16)
    dma = pltpu.SemaphoreType.DMA

    def vmem(*shape):
        return pltpu.VMEM(shape, jnp.bfloat16)

    flat = vmem(row_count, column_count)

    def packed_shape(rows):
        return jax.ShapeDtypeStruct((slots, rows, head_dim), jnp.bfloat16)

    def exchanged(packed):
        parts = packed.reshape(ctx_count, capacity, *packed.shape[1:])
        parts = lax.all_to_all(parts, "ctx", split_axis=0, concat_axis=0, tiled=True)
        return parts.reshape(packed.shape)

    def pack(name, source):
        return pl.pallas_call(
            functools.partial(pack_kernel, add_parts),
            out_shape=packed_shape(block_rows),
            in_specs=[SMEM, ANY],
            out_specs=ANY,
            scratch_shapes=[flat, vmem(slots, block_rows, head_dim), dma, dma((add_parts,))],
            compiler_params=PARAMS,
            name=name,
        )(codes, source)

    def near(value):
        return pltpu.with_memory_space_constraint(value, pltpu.VMEM)

    def wide_sum(rows):
        return pltpu.VMEM((3 * rows, column_count), jnp.float32)

    def add_up(name, returned):
        rows = returned.shape[1]
        return pl.pallas_call(
            functools.partial(sum_kernel, add_parts),
            out_shape=jax.ShapeDtypeStruct((2 * rows, column_count), jnp.bfloat16),
            in_specs=[SMEM, VMEM],
            out_specs=ANY,
            scratch_shapes=[wide_sum(rows), vmem(2 * rows, column_count), dma((send_parts,))],
            compiler_params=PARAMS,
            name=name,
        )(codes, returned)

    tiles = vmem(entries, block_rows, head_dim)
    slot_tiles = vmem(slots, block_rows, head_dim)
    wide_sem, tile_sem = dma((groups,)), dma((entries,))
    fetched_keys = exchanged(pack("pack_keys", keys[0]))
    handed_codes = shifted(codes, "section", -1)
    packed_values, handed_codes = lax.optimization_barrier(
        (pack("pack_values", values[0]), handed_codes)
    )
    fetched_values = exchanged(packed_values)
    weights_shape = (head_count, list_size * block_rows, row_count)
    weights_tile = pltpu.VMEM(weights_shape, jnp.float32)
    first_terms, last_terms, weights = pl.pallas_call(
        functools.partial(value_kernel, list_size, group, scale),
        out_shape=(
            packed_shape(first_rows),
            packed_shape(last_rows),
            jax.ShapeDtypeStruct(weights_shape, jnp.float32),
        ),
        in_specs=[SMEM, SMEM, ANY, ANY, ANY],
        out_specs=(ANY, ANY, ANY),
        scratch_shapes=[flat, flat, tiles, tiles, weights_tile]
        + [wide_sem, wide_sem, tile_sem, dma((2, entries)), wide_sem],
        compiler_params=PARAMS,
        name="value_terms",
    )(places, my_lengths, queries[0], out_grad[0], fetched_keys)
    handed_first = shifted(first_terms, "section", -1)
    query_grad, key_terms = pl.pallas_call(
        functools.partial(key_kernel, list_size, group, scale),
        out_shape=(flat_shape, packed_shape(block_rows)),
        in_specs=[SMEM, SMEM, ANY, ANY, ANY, VMEM, ANY],
        out_specs=(ANY, ANY),
        scratch_shapes=[flat, flat, slot_tiles, weights_tile, slot_tiles, flat]
        + [wide_sem, wide_sem, dma((add_parts,)), wide_sem, dma((add_parts,)), wide_sem],
        compiler_params=PARAMS,
        name="key_terms",
    )(places, my_lengths, queries[0], out_grad[0], fetched_keys, near(fetched_values), weights)
    handed_queries = shifted(query_grad, "section", -1)
    handed_last = shifted(last_terms, "section", -1)
    key_terms, handed_first = lax.optimization_barrier((key_terms, handed_first))
    returned_keys = exchanged(key_terms)
    handed_terms = jnp.concatenate([handed_first, handed_last], axis=1)
    handed_queries = pl.pallas_call(
        place_kernel,
        out_shape=flat_shape,
        in_specs=[VMEM],
        out_specs=VMEM,
        compiler_params=PARAMS,
        name="place_queries",
    )(near(handed_queries))
    returned_keys, handed_queries, handed_terms = lax.optimization_barrier(
        (returned_keys, handed_queries, handed_terms)
    )
    key_grad = add_up("sum_keys", near(returned_keys))
    key_grad, handed_terms = lax.optimization_barrier((key_grad, handed_terms))
    handed_keys = shifted(key_grad, "section", -1)
    handed_keys, handed_values = pl.pallas_call(
        functools.partial(last_kernel, add_parts),
        out_shape=(flat_shape, flat_shape),
        in_specs=[SMEM, ANY, VMEM],
        out_specs=(ANY, ANY),
        scratch_shapes=[wide_sum(block_rows), flat, flat]
        + [dma((send_parts,)), dma, dma],
        compiler_params=PARAMS,
        name="last_values",
    )(handed_codes, handed_keys, near(exchanged(handed_terms)))
    return (handed_queries[None], handed_keys[None], handed_values[None])


def solution(mesh):
    placed = (
        P("section", "ctx", None),
        P("section", "ctx", None),
        P("section", "ctx", None),
        P("section", "ctx", None),
        P("section", None, None, None),
        P("section", None, None),
    )
    return jax.shard_map(
        local,
        mesh=mesh,
        in_specs=placed,
        out_specs=(P("section", "ctx", None), P("section", "ctx", None), P("section", "ctx", None)),
        check_vma=False,
    )
```

```python
import functools
import math

import jax
import jax.numpy as jnp
from jax import lax
from jax.experimental import pallas as pl
from jax.experimental.pallas import tpu as pltpu
from jax.sharding import PartitionSpec as P

HEAD_BITS = 8
VMEM = pl.BlockSpec(memory_space=pltpu.VMEM)
SMEM = pl.BlockSpec(memory_space=pltpu.SMEM)
ANY = pl.BlockSpec(memory_space=pl.ANY)
PARAMS = pltpu.CompilerParams(vmem_limit_bytes=56 * 1024 * 1024)
NT = (((1,), (1,)), ((), ()))
NN = (((1,), (0,)), ((), ()))
TN = (((0,), (0,)), ((), ()))
copy = pltpu.make_async_copy


def shifted(value, axis, steps):
    count = lax.axis_size(axis)
    pairs = [(source, (source + steps) % count) for source in range(count)]
    return lax.ppermute(value, axis, pairs)


def tile_of(code, rows, cols):
    block = lax.shift_right_logical(code, HEAD_BITS)
    head = lax.bitwise_and(code, (1 << HEAD_BITS) - 1)
    return (
        pl.ds(pl.multiple_of(block * rows, rows), rows),
        pl.ds(pl.multiple_of(head * cols, cols), cols),
    )


def pack_kernel(parts, codes, source, packed, held, made, got, sent):
    slots, rows, cols = packed.shape
    step = slots // parts
    whole = copy(source, held, got)
    whole.start()
    whole.wait()

    def part_of(part):
        where = pl.ds(part * step, step)
        return copy(made.at[where], packed.at[where], sent.at[part])

    def one_part(part, carry):
        for item in range(step):
            slot = part * step + item
            made[slot] = held[tile_of(jnp.maximum(codes[slot], 0), rows, cols)]
        part_of(part).start()
        return carry

    lax.fori_loop(0, parts, one_part, 0)
    for part in range(parts):
        part_of(part).wait()


def add_slots(codes, terms, wide, first, count):
    rows, cols = terms.shape[1:]
    for item in range(count):
        slot = first + item
        code = codes[slot]
        code = jnp.where(code < 0, 2 << HEAD_BITS, code)
        wide[tile_of(code, rows, cols)] += terms[slot].astype(jnp.float32)


def add_terms(codes, terms, wide, parts):
    wide[...] = jnp.zeros_like(wide)
    step = terms.shape[0] // parts

    def one_part(part, carry):
        add_slots(codes, terms, wide, part * step, step)
        return carry

    lax.fori_loop(0, parts, one_part, 0)


def send_columns(ready, total, sent, parts, fill):
    width = total.shape[1] // parts
    copies = []
    for part in range(parts):
        columns = pl.ds(part * width, width)
        fill(columns)
        copies.append(copy(ready.at[:, columns], total.at[:, columns], sent.at[part]))
        copies[-1].start()
    for one in copies:
        one.wait()


def sum_kernel(parts, codes, terms, total, wide, ready, sent):
    add_terms(codes, terms, wide, parts)
    rows = total.shape[0]

    def fill(columns):
        ready[:, columns] = wide[:rows, columns].astype(ready.dtype)

    send_columns(ready, total, sent, sent.shape[0], fill)


def join_kernel(
    parts, codes, head_part, terms, after, total, wide, ready, head, sent, got
):
    head_copy = copy(head_part, head, got)
    head_copy.start()
    add_terms(codes, terms, wide, parts)
    head_copy.wait()
    tail_rows = terms.shape[1]
    head_rows = total.shape[0] // 2 - tail_rows

    def fill(columns):
        for block in range(2):
            start = block * (head_rows + tail_rows)
            middle = start + head_rows
            ready[start:middle, columns] = head[
                block * head_rows : (block + 1) * head_rows, columns
            ]
            ready[middle : middle + tail_rows, columns] = wide[
                block * tail_rows : (block + 1) * tail_rows, columns
            ].astype(ready.dtype)

    send_columns(ready, total, sent, sent.shape[0], fill)


def place_kernel(source, out):
    out[...] = source[...]


def weights_of(query, key, length, list_size, scale):
    scores = lax.dot_general(key, query, NT, preferred_element_type=jnp.float32)
    row_max = jnp.max(scores, axis=0, keepdims=True)
    exp_scores = jnp.exp2((scores - row_max) * (scale * math.log2(math.e)))
    rows = key.shape[0] // list_size
    parts = [exp_scores[item * rows : (item + 1) * rows] for item in range(list_size)]
    kept = [jnp.where(item < length, 1.0, 0.0).astype(jnp.float32) for item in range(list_size)]
    total = sum(keep * jnp.sum(part, axis=0, keepdims=True) for keep, part in zip(kept, parts))
    inverse = 1.0 / total
    return [part * (inverse * keep) for keep, part in zip(kept, parts)]


class Grouped:
    def __init__(self, places, lengths, list_size, group, cols):
        self.places, self.lengths = places, lengths
        self.list_size, self.group, self.cols = list_size, group, cols
        self.groups = lengths.shape[0] // group

    def head(self, head):
        return pl.ds(pl.multiple_of(head * self.cols, self.cols), self.cols)

    def wide(self, index, source, held, sems):
        width = self.group * self.cols
        columns = pl.ds(pl.multiple_of(index * width, width), width)
        return copy(source.at[:, columns], held.at[:, columns], sems.at[index])

    def block(self, index, source, held, sems):
        where = pl.ds(index * self.group, self.group)
        return copy(source.at[where], held.at[where], sems.at[index])

    def fetches(self, index, sources, tiles, blocks):
        made = [self.wide(index, *source) for source in sources]
        made += [self.block(index, *source) for source in blocks]
        count = self.group * self.list_size
        for item in range(count):
            entry = index * count + item
            for source, held, sems in tiles:
                made.append(
                    copy(source.at[self.places[entry]], held.at[entry], sems.at[entry])
                )
        return made

    def puts(self, entry, made, outs, sems):
        start, copies = 0, []
        for which, out in enumerate(outs):
            count = out.shape[1]
            copies.append(
                copy(
                    made.at[entry, pl.ds(start, count)],
                    out.at[self.places[entry]],
                    sems.at[which, entry],
                )
            )
            start += count
        return copies

    def each_put(self, head, made, outs, sems, act):
        for item in range(self.list_size):

            @pl.when(item < self.lengths[head])
            def _():
                for one in self.puts(head * self.list_size + item, made, outs, sems):
                    act(one)

    def run(self, sources, tiles, blocks, made, outs, sems, compute, finish):
        def start(index):
            for one in self.fetches(index, sources, tiles, blocks):
                one.start()

        start(0)

        def one_group(index, carry):
            @pl.when(index + 1 < self.groups)
            def _():
                start(index + 1)

            for one in self.fetches(index, sources, tiles, blocks):
                one.wait()
            for item in range(self.group):
                head = index * self.group + item
                terms = compute(head)
                entries = pl.ds(head * self.list_size, self.list_size)
                made[entries] = terms.reshape(self.list_size, -1, self.cols)
                self.each_put(head, made, outs, sems, lambda one: one.start())
            finish(index).start()
            return carry

        lax.fori_loop(0, self.groups, one_group, 0)

        def last(head, carry):
            self.each_put(head, made, outs, sems, lambda one: one.wait())
            return carry

        lax.fori_loop(0, self.lengths.shape[0], last, 0)
        for index in range(self.groups):
            finish(index).wait()


def value_kernel(
    list_size, group, scale, places, lengths, queries, grads, keys, first, last, weights_out,
    query_held, grad_held, key_held, made, weights_made,
    query_sem, grad_sem, key_sem, out_sem, weights_sem,
):
    rows, cols = keys.shape[1:]
    walk = Grouped(places, lengths, list_size, group, cols)

    def compute(head):
        columns = walk.head(head)
        key = key_held[pl.ds(head * list_size, list_size)].reshape(-1, cols)
        weights = weights_of(query_held[:, columns], key, lengths[head], list_size, scale)
        for item, part in enumerate(weights):
            weights_made[head, item * rows : (item + 1) * rows] = part
        weights_low = jnp.concatenate([part.astype(jnp.bfloat16) for part in weights], axis=0)
        return lax.dot_general(
            weights_low, grad_held[:, columns], NN, preferred_element_type=jnp.float32
        ).astype(jnp.bfloat16)

    walk.run(
        [(queries, query_held, query_sem), (grads, grad_held, grad_sem)],
        [(keys, key_held, key_sem)],
        [],
        made,
        [first, last],
        out_sem,
        compute,
        lambda index: walk.block(index, weights_made, weights_out, weights_sem),
    )


def key_kernel(
    list_size, group, scale, places, lengths, queries, grads, keys, values, weights,
    query_grad, terms,
    query_held, grad_held, key_held, value_held, weights_held, made, query_made,
    query_sem, grad_sem, key_sem, value_sem, weights_sem, out_sem, query_out_sem,
):
    rows, cols = keys.shape[1:]
    groups = lengths.shape[0] // group
    parts = out_sem.shape[0]
    step = keys.shape[0] // parts
    width = group * cols

    def columns_of(index):
        return pl.ds(pl.multiple_of(index * width, width), width)

    def fetches(index):
        columns = columns_of(index)
        heads = pl.ds(index * group, group)
        return [
            copy(grads.at[:, columns], grad_held.at[:, columns], grad_sem.at[index]),
            copy(weights.at[heads], weights_held.at[heads], weights_sem.at[index]),
            copy(queries.at[:, columns], query_held.at[:, columns], query_sem.at[index]),
        ]

    def key_part(part):
        where = pl.ds(part * step, step)
        return copy(keys.at[where], key_held.at[where], key_sem.at[part])

    def value_part(part):
        where = pl.ds(part * step, step)
        return copy(values.at[where], value_held.at[where], value_sem.at[part])

    def made_part(part):
        where = pl.ds(part * step, step)
        return copy(made.at[where], terms.at[where], out_sem.at[part])

    def query_part(index):
        columns = columns_of(index)
        return copy(
            query_made.at[:, columns], query_grad.at[:, columns], query_out_sem.at[index]
        )

    for one in fetches(0):
        one.start()
    for part in range(parts):
        value_part(part).start()
    for part in range(parts):
        key_part(part).start()

    def compute(head):
        columns = pl.ds(pl.multiple_of(head * cols, cols), cols)
        where = [places[head * list_size + item] for item in range(list_size)]
        key = jnp.concatenate([key_held[place] for place in where], axis=0)
        value = jnp.concatenate([value_held[place] for place in where], axis=0)
        weight = weights_held[head]
        weight_low = weight.astype(jnp.bfloat16).astype(jnp.float32)
        dweights = lax.dot_general(
            value, grad_held[:, columns], NT, preferred_element_type=jnp.float32
        )
        row_delta = jnp.sum(weight_low * dweights, axis=0, keepdims=True)
        dscores = (weight * (dweights - row_delta)).astype(jnp.bfloat16)
        flipped = lax.dot_general(key, dscores, TN, preferred_element_type=jnp.float32)
        query_made[:, columns] = (flipped * scale).astype(jnp.bfloat16).T
        made_terms = lax.dot_general(
            dscores, query_held[:, columns], NN, preferred_element_type=jnp.float32
        )
        return (made_terms * scale).astype(jnp.bfloat16)

    def one_group(index, carry):
        @pl.when(index + 1 < groups)
        def _():
            for one in fetches(index + 1):
                one.start()

        for one in fetches(index):
            one.wait()

        @pl.when(index == 0)
        def _():
            for part in range(parts):
                value_part(part).wait()
                key_part(part).wait()

        results = [compute(index * group + item) for item in range(group)]
        query_part(index).start()
        for item, result in enumerate(results):
            head = index * group + item
            for entry in range(list_size):

                @pl.when(entry < lengths[head])
                def _():
                    made[places[head * list_size + entry]] = result[
                        entry * rows : (entry + 1) * rows
                    ]

        return carry

    lax.fori_loop(0, groups, one_group, 0)
    for part in range(parts):
        made_part(part).start()
    for index in range(groups):
        query_part(index).wait()
    for part in range(parts):
        made_part(part).wait()


def local(queries, keys, values, out_grad, key_blocks, list_lengths):
    ctx_count = lax.axis_size("ctx")
    my_index = lax.axis_index("ctx")
    row_count, column_count = queries.shape[1:]
    head_count = list_lengths.shape[2]
    head_dim = column_count // head_count
    list_size = key_blocks.shape[3]
    block_rows = row_count // 2
    entries = head_count * list_size
    capacity = (entries + ctx_count - 1) // ctx_count
    slots = ctx_count * capacity
    scale = 1.0 / math.sqrt(head_dim)
    group = 4 if head_count % 4 == 0 else 1
    groups = head_count // group

    chosen = key_blocks[0]
    lengths = list_lengths[0]
    items = jnp.arange(list_size, dtype=jnp.int32)
    heads = jnp.arange(head_count, dtype=jnp.int32)
    is_used = items[None, None, :] < lengths[:, :, None]
    is_mine = is_used & ((chosen >> 1) == my_index)
    hit = jnp.sum(jnp.where(is_mine, 1 + (chosen & 1), 0), axis=2)
    rank = jnp.sum(
        jnp.where((heads[None, None, :] < heads[None, :, None]) & (hit[:, None, :] > 0), 1, 0),
        axis=2,
    )
    code = ((hit - 1) << HEAD_BITS) + heads[None, :]
    ranks = jnp.arange(capacity, dtype=jnp.int32)
    codes = jnp.max(
        jnp.where(
            (hit[:, None, :] > 0) & (rank[:, None, :] == ranks[None, :, None]),
            code[:, None, :],
            -1,
        ),
        axis=2,
    ).reshape(slots)

    my_lengths = lax.dynamic_index_in_dim(lengths, my_index, 0, keepdims=False)
    my_chosen = lax.dynamic_index_in_dim(chosen, my_index, 0, keepdims=False)
    my_used = items[None, :] < my_lengths[:, None]
    my_holder = jnp.where(my_used, my_chosen >> 1, -1)
    earlier = (heads[None, None, :, None] < heads[:, None, None, None]) & (
        my_holder[None, None, :, :] == my_holder[:, :, None, None]
    )
    my_rank = jnp.sum(jnp.where(earlier, 1, 0), axis=(2, 3))
    places = my_holder * capacity + my_rank
    places = jnp.where(my_used, places, places[:, :1]).reshape(entries)

    first_rows = 3 * block_rows // 8
    last_rows = block_rows - first_rows
    add_parts = 8 if slots % 8 == 0 else 1
    send_parts = 5 if head_count % 5 == 0 else 1
    flat_shape = jax.ShapeDtypeStruct((row_count, column_count), jnp.bfloat16)
    dma = pltpu.SemaphoreType.DMA

    def vmem(*shape):
        return pltpu.VMEM(shape, jnp.bfloat16)

    flat = vmem(row_count, column_count)

    def packed_shape(rows):
        return jax.ShapeDtypeStruct((slots, rows, head_dim), jnp.bfloat16)

    def exchanged(packed):
        parts = packed.reshape(ctx_count, capacity, *packed.shape[1:])
        parts = lax.all_to_all(parts, "ctx", split_axis=0, concat_axis=0, tiled=True)
        return parts.reshape(packed.shape)

    def pack(name, source):
        return pl.pallas_call(
            functools.partial(pack_kernel, add_parts),
            out_shape=packed_shape(block_rows),
            in_specs=[SMEM, ANY],
            out_specs=ANY,
            scratch_shapes=[flat, vmem(slots, block_rows, head_dim), dma, dma((add_parts,))],
            compiler_params=PARAMS,
            name=name,
        )(codes, source)

    def near(value):
        return pltpu.with_memory_space_constraint(value, pltpu.VMEM)

    def wide_sum(rows):
        return pltpu.VMEM((3 * rows, column_count), jnp.float32)

    def placed(name, value, cost):
        return pl.pallas_call(
            place_kernel,
            out_shape=flat_shape,
            in_specs=[VMEM],
            out_specs=VMEM,
            compiler_params=PARAMS,
            cost_estimate=pl.CostEstimate(flops=0, transcendentals=0, bytes_accessed=cost),
            name=name,
        )(near(value))

    def add_up(name, returned):
        rows = returned.shape[1]
        return pl.pallas_call(
            functools.partial(sum_kernel, add_parts),
            out_shape=jax.ShapeDtypeStruct((2 * rows, column_count), jnp.bfloat16),
            in_specs=[SMEM, VMEM],
            out_specs=ANY,
            scratch_shapes=[wide_sum(rows), vmem(2 * rows, column_count), dma((send_parts,))],
            compiler_params=PARAMS,
            name=name,
        )(codes, returned)

    tiles = vmem(entries, block_rows, head_dim)
    slot_tiles = vmem(slots, block_rows, head_dim)
    wide_sem, tile_sem, part_sem = dma((groups,)), dma((entries,)), dma((add_parts,))
    fetched_keys = exchanged(pack("pack_keys", keys[0]))
    handed_codes = shifted(codes, "section", -1)
    packed_values, handed_codes = lax.optimization_barrier(
        (pack("pack_values", values[0]), handed_codes)
    )
    fetched_values = exchanged(packed_values)
    weights_shape = (head_count, list_size * block_rows, row_count)
    weights_tile = pltpu.VMEM(weights_shape, jnp.float32)
    first_terms, last_terms, weights = pl.pallas_call(
        functools.partial(value_kernel, list_size, group, scale),
        out_shape=(
            packed_shape(first_rows),
            packed_shape(last_rows),
            jax.ShapeDtypeStruct(weights_shape, jnp.float32),
        ),
        in_specs=[SMEM, SMEM, ANY, ANY, ANY],
        out_specs=(ANY, ANY, ANY),
        scratch_shapes=[flat, flat, tiles, tiles, weights_tile]
        + [wide_sem, wide_sem, tile_sem, dma((2, entries)), wide_sem],
        compiler_params=PARAMS,
        name="value_terms",
    )(places, my_lengths, queries[0], out_grad[0], fetched_keys)
    handed_terms = shifted(last_terms, "section", -1)
    query_grad, key_terms = pl.pallas_call(
        functools.partial(key_kernel, list_size, group, scale),
        out_shape=(flat_shape, packed_shape(block_rows)),
        in_specs=[SMEM, SMEM, ANY, ANY, ANY, ANY, ANY],
        out_specs=(ANY, ANY),
        scratch_shapes=[flat, flat, slot_tiles, slot_tiles, weights_tile, slot_tiles, flat]
        + [wide_sem, wide_sem, part_sem, part_sem, wide_sem, part_sem, wide_sem],
        compiler_params=PARAMS,
        name="key_terms",
    )(places, my_lengths, queries[0], out_grad[0], fetched_keys, fetched_values, weights)
    first_values = add_up("sum_values", exchanged(first_terms))
    handed_first = shifted(first_values, "section", -1)
    key_terms, handed_terms = lax.optimization_barrier((key_terms, handed_terms))
    returned_keys = exchanged(key_terms)
    handed_queries = placed("place_queries", shifted(query_grad, "section", -1), 5000000)
    returned_keys, handed_queries, first_values = lax.optimization_barrier(
        (returned_keys, handed_queries, first_values)
    )
    key_grad = add_up("sum_keys", near(returned_keys))
    key_grad, handed_terms, handed_first = lax.optimization_barrier(
        (key_grad, handed_terms, handed_first)
    )
    handed_keys = placed("place_keys", shifted(key_grad, "section", -1), 5000000)
    handed_values = pl.pallas_call(
        functools.partial(join_kernel, add_parts),
        out_shape=flat_shape,
        in_specs=[SMEM, ANY, VMEM, ANY],
        out_specs=ANY,
        scratch_shapes=[wide_sum(last_rows), flat, vmem(2 * first_rows, column_count)]
        + [dma((send_parts,)), dma],
        compiler_params=PARAMS,
        name="join_values",
    )(handed_codes, handed_first, near(exchanged(handed_terms)), handed_keys)
    return (handed_queries[None], handed_keys[None], handed_values[None])


def solution(mesh):
    placed = (
        P("section", "ctx", None),
        P("section", "ctx", None),
        P("section", "ctx", None),
        P("section", "ctx", None),
        P("section", None, None, None),
        P("section", None, None),
    )
    return jax.shard_map(
        local,
        mesh=mesh,
        in_specs=placed,
        out_specs=(P("section", "ctx", None), P("section", "ctx", None), P("section", "ctx", None)),
        check_vma=False,
    )
```

```python
import functools
import math

import jax
import jax.numpy as jnp
from jax import lax
from jax.experimental import pallas as pl
from jax.experimental.pallas import tpu as pltpu
from jax.sharding import PartitionSpec as P

HEAD_BITS = 8
VMEM = pl.BlockSpec(memory_space=pltpu.VMEM)
SMEM = pl.BlockSpec(memory_space=pltpu.SMEM)
ANY = pl.BlockSpec(memory_space=pl.ANY)
PARAMS = pltpu.CompilerParams(vmem_limit_bytes=56 * 1024 * 1024)
NT = (((1,), (1,)), ((), ()))
NN = (((1,), (0,)), ((), ()))
TN = (((0,), (0,)), ((), ()))
copy = pltpu.make_async_copy


def shifted(value, axis, steps):
    count = lax.axis_size(axis)
    pairs = [(source, (source + steps) % count) for source in range(count)]
    return lax.ppermute(value, axis, pairs)


def tile_of(code, rows, cols):
    block = lax.shift_right_logical(code, HEAD_BITS)
    head = lax.bitwise_and(code, (1 << HEAD_BITS) - 1)
    return (
        pl.ds(pl.multiple_of(block * rows, rows), rows),
        pl.ds(pl.multiple_of(head * cols, cols), cols),
    )


def pack_kernel(parts, codes, source, packed, held, made, got, sent):
    slots, rows, cols = packed.shape
    step = slots // parts
    whole = copy(source, held, got)
    whole.start()
    whole.wait()

    def part_of(part):
        where = pl.ds(part * step, step)
        return copy(made.at[where], packed.at[where], sent.at[part])

    def one_part(part, carry):
        for item in range(step):
            slot = part * step + item
            made[slot] = held[tile_of(jnp.maximum(codes[slot], 0), rows, cols)]
        part_of(part).start()
        return carry

    lax.fori_loop(0, parts, one_part, 0)
    for part in range(parts):
        part_of(part).wait()


def add_slots(codes, terms, wide, first, count):
    rows, cols = terms.shape[1:]
    for item in range(count):
        slot = first + item
        code = codes[slot]
        code = jnp.where(code < 0, 2 << HEAD_BITS, code)
        wide[tile_of(code, rows, cols)] += terms[slot].astype(jnp.float32)


def add_terms(codes, terms, wide, parts):
    wide[...] = jnp.zeros_like(wide)
    step = terms.shape[0] // parts

    def one_part(part, carry):
        add_slots(codes, terms, wide, part * step, step)
        return carry

    lax.fori_loop(0, parts, one_part, 0)


def send_columns(ready, total, sent, parts, fill):
    width = total.shape[1] // parts
    copies = []
    for part in range(parts):
        columns = pl.ds(part * width, width)
        fill(columns)
        copies.append(copy(ready.at[:, columns], total.at[:, columns], sent.at[part]))
        copies[-1].start()
    for one in copies:
        one.wait()


def sum_kernel(parts, codes, terms, total, wide, ready, sent):
    add_terms(codes, terms, wide, parts)
    rows = total.shape[0]

    def fill(columns):
        ready[:, columns] = wide[:rows, columns].astype(ready.dtype)

    send_columns(ready, total, sent, sent.shape[0], fill)


def join_kernel(
    parts, codes, head_part, terms, total, wide, ready, head, sent, got
):
    head_copy = copy(head_part, head, got)
    head_copy.start()
    add_terms(codes, terms, wide, parts)
    head_copy.wait()
    tail_rows = terms.shape[1]
    head_rows = total.shape[0] // 2 - tail_rows

    def fill(columns):
        for block in range(2):
            start = block * (head_rows + tail_rows)
            middle = start + head_rows
            ready[start:middle, columns] = head[
                block * head_rows : (block + 1) * head_rows, columns
            ]
            ready[middle : middle + tail_rows, columns] = wide[
                block * tail_rows : (block + 1) * tail_rows, columns
            ].astype(ready.dtype)

    send_columns(ready, total, sent, sent.shape[0], fill)


def place_last_kernel(source, after, out):
    out[...] = source[...]


def place_kernel(source, out):
    out[...] = source[...]


def weights_of(query, key, length, list_size, scale):
    scores = lax.dot_general(key, query, NT, preferred_element_type=jnp.float32)
    row_max = jnp.max(scores, axis=0, keepdims=True)
    exp_scores = jnp.exp2((scores - row_max) * (scale * math.log2(math.e)))
    rows = key.shape[0] // list_size
    parts = [exp_scores[item * rows : (item + 1) * rows] for item in range(list_size)]
    kept = [jnp.where(item < length, 1.0, 0.0).astype(jnp.float32) for item in range(list_size)]
    total = sum(keep * jnp.sum(part, axis=0, keepdims=True) for keep, part in zip(kept, parts))
    inverse = 1.0 / total
    return [part * (inverse * keep) for keep, part in zip(kept, parts)]


def in_parts(source, target, sems):
    parts = sems.shape[0]
    step = source.shape[0] // parts
    wheres = [pl.ds(part * step, step) for part in range(parts)]
    return [
        copy(source.at[where], target.at[where], sems.at[part])
        for part, where in enumerate(wheres)
    ]


def put_terms(places, lengths, list_size, head, result, outs):
    rows = result.shape[0] // list_size
    for entry in range(list_size):

        @pl.when(entry < lengths[head])
        def _():
            start = entry * rows
            for out in outs:
                count = out.shape[1]
                out[places[head * list_size + entry]] = result[start : start + count]
                start += count


def value_kernel(
    list_size, group, scale, places, lengths, queries, grads, keys, first, last, weights_out,
    query_held, grad_held, key_held, first_made, last_made, weights_made,
    query_sem, grad_sem, key_sem, first_sem, last_sem, weights_sem,
):
    rows, cols = keys.shape[1:]
    groups = lengths.shape[0] // group
    width = group * cols

    def fetches(index):
        columns = pl.ds(pl.multiple_of(index * width, width), width)
        return [
            copy(queries.at[:, columns], query_held.at[:, columns], query_sem.at[index]),
            copy(grads.at[:, columns], grad_held.at[:, columns], grad_sem.at[index]),
        ]

    def weights_part(index):
        heads = pl.ds(index * group, group)
        return copy(weights_made.at[heads], weights_out.at[heads], weights_sem.at[index])

    for one in fetches(0) + in_parts(keys, key_held, key_sem):
        one.start()

    def compute(head):
        columns = pl.ds(pl.multiple_of(head * cols, cols), cols)
        key = jnp.concatenate(
            [key_held[places[head * list_size + item]] for item in range(list_size)], axis=0
        )
        weights = weights_of(query_held[:, columns], key, lengths[head], list_size, scale)
        for item, part in enumerate(weights):
            weights_made[head, item * rows : (item + 1) * rows] = part
        weights_low = jnp.concatenate([part.astype(jnp.bfloat16) for part in weights], axis=0)
        return lax.dot_general(
            weights_low, grad_held[:, columns], NN, preferred_element_type=jnp.float32
        ).astype(jnp.bfloat16)

    def one_group(index, carry):
        @pl.when(index + 1 < groups)
        def _():
            for one in fetches(index + 1):
                one.start()

        for one in fetches(index):
            one.wait()

        @pl.when(index == 0)
        def _():
            for one in in_parts(keys, key_held, key_sem):
                one.wait()

        results = [compute(index * group + item) for item in range(group)]
        weights_part(index).start()
        for item, result in enumerate(results):
            put_terms(
                places, lengths, list_size, index * group + item, result, [first_made, last_made]
            )
        return carry

    lax.fori_loop(0, groups, one_group, 0)
    ends = in_parts(last_made, last, last_sem) + in_parts(first_made, first, first_sem)
    for one in ends:
        one.start()
    for index in range(groups):
        weights_part(index).wait()
    for one in ends:
        one.wait()


def key_kernel(
    list_size, group, scale, places, lengths, queries, grads, keys, values, weights,
    query_grad, terms,
    query_held, grad_held, key_held, value_held, weights_held, made, query_made,
    query_sem, grad_sem, key_sem, value_sem, weights_sem, out_sem, query_out_sem,
):
    cols = keys.shape[2]
    groups = lengths.shape[0] // group
    width = group * cols

    def columns_of(index):
        return pl.ds(pl.multiple_of(index * width, width), width)

    def fetches(index):
        columns = columns_of(index)
        heads = pl.ds(index * group, group)
        return [
            copy(grads.at[:, columns], grad_held.at[:, columns], grad_sem.at[index]),
            copy(weights.at[heads], weights_held.at[heads], weights_sem.at[index]),
            copy(queries.at[:, columns], query_held.at[:, columns], query_sem.at[index]),
        ]

    def tile_fetches():
        return in_parts(values, value_held, value_sem) + in_parts(keys, key_held, key_sem)

    def query_part(index):
        columns = columns_of(index)
        return copy(
            query_made.at[:, columns], query_grad.at[:, columns], query_out_sem.at[index]
        )

    for one in fetches(0) + tile_fetches():
        one.start()

    def compute(head):
        columns = pl.ds(pl.multiple_of(head * cols, cols), cols)
        where = [places[head * list_size + item] for item in range(list_size)]
        key = jnp.concatenate([key_held[place] for place in where], axis=0)
        value = jnp.concatenate([value_held[place] for place in where], axis=0)
        weight = weights_held[head]
        weight_low = weight.astype(jnp.bfloat16).astype(jnp.float32)
        dweights = lax.dot_general(
            value, grad_held[:, columns], NT, preferred_element_type=jnp.float32
        )
        row_delta = jnp.sum(weight_low * dweights, axis=0, keepdims=True)
        dscores = (weight * (dweights - row_delta)).astype(jnp.bfloat16)
        flipped = lax.dot_general(key, dscores, TN, preferred_element_type=jnp.float32)
        query_made[:, columns] = (flipped * scale).astype(jnp.bfloat16).T
        made_terms = lax.dot_general(
            dscores, query_held[:, columns], NN, preferred_element_type=jnp.float32
        )
        return (made_terms * scale).astype(jnp.bfloat16)

    def one_group(index, carry):
        @pl.when(index + 1 < groups)
        def _():
            for one in fetches(index + 1):
                one.start()

        for one in fetches(index):
            one.wait()

        @pl.when(index == 0)
        def _():
            for one in tile_fetches():
                one.wait()

        results = [compute(index * group + item) for item in range(group)]
        query_part(index).start()
        for item, result in enumerate(results):
            put_terms(places, lengths, list_size, index * group + item, result, [made])
        return carry

    lax.fori_loop(0, groups, one_group, 0)
    ends = in_parts(made, terms, out_sem)
    for one in ends:
        one.start()
    for index in range(groups):
        query_part(index).wait()
    for one in ends:
        one.wait()


def local(queries, keys, values, out_grad, key_blocks, list_lengths):
    ctx_count = lax.axis_size("ctx")
    my_index = lax.axis_index("ctx")
    row_count, column_count = queries.shape[1:]
    head_count = list_lengths.shape[2]
    head_dim = column_count // head_count
    list_size = key_blocks.shape[3]
    block_rows = row_count // 2
    entries = head_count * list_size
    capacity = (entries + ctx_count - 1) // ctx_count
    slots = ctx_count * capacity
    scale = 1.0 / math.sqrt(head_dim)
    group = 4 if head_count % 4 == 0 else 1
    groups = head_count // group

    chosen = key_blocks[0]
    lengths = list_lengths[0]
    items = jnp.arange(list_size, dtype=jnp.int32)
    heads = jnp.arange(head_count, dtype=jnp.int32)
    is_used = items[None, None, :] < lengths[:, :, None]
    is_mine = is_used & ((chosen >> 1) == my_index)
    hit = jnp.sum(jnp.where(is_mine, 1 + (chosen & 1), 0), axis=2)
    rank = jnp.sum(
        jnp.where((heads[None, None, :] < heads[None, :, None]) & (hit[:, None, :] > 0), 1, 0),
        axis=2,
    )
    code = ((hit - 1) << HEAD_BITS) + heads[None, :]
    ranks = jnp.arange(capacity, dtype=jnp.int32)
    codes = jnp.max(
        jnp.where(
            (hit[:, None, :] > 0) & (rank[:, None, :] == ranks[None, :, None]),
            code[:, None, :],
            -1,
        ),
        axis=2,
    ).reshape(slots)

    my_lengths = lax.dynamic_index_in_dim(lengths, my_index, 0, keepdims=False)
    my_chosen = lax.dynamic_index_in_dim(chosen, my_index, 0, keepdims=False)
    my_used = items[None, :] < my_lengths[:, None]
    my_holder = jnp.where(my_used, my_chosen >> 1, -1)
    earlier = (heads[None, None, :, None] < heads[:, None, None, None]) & (
        my_holder[None, None, :, :] == my_holder[:, :, None, None]
    )
    my_rank = jnp.sum(jnp.where(earlier, 1, 0), axis=(2, 3))
    places = my_holder * capacity + my_rank
    places = jnp.where(my_used, places, places[:, :1]).reshape(entries)

    first_rows = 3 * block_rows // 8
    last_rows = block_rows - first_rows
    add_parts = 8 if slots % 8 == 0 else 1
    send_parts = 5 if head_count % 5 == 0 else 1
    flat_shape = jax.ShapeDtypeStruct((row_count, column_count), jnp.bfloat16)
    dma = pltpu.SemaphoreType.DMA

    def vmem(*shape):
        return pltpu.VMEM(shape, jnp.bfloat16)

    flat = vmem(row_count, column_count)

    def packed_shape(rows):
        return jax.ShapeDtypeStruct((slots, rows, head_dim), jnp.bfloat16)

    def exchanged(packed):
        parts = packed.reshape(ctx_count, capacity, *packed.shape[1:])
        parts = lax.all_to_all(parts, "ctx", split_axis=0, concat_axis=0, tiled=True)
        return parts.reshape(packed.shape)

    def pack(name, source):
        return pl.pallas_call(
            functools.partial(pack_kernel, add_parts),
            out_shape=packed_shape(block_rows),
            in_specs=[SMEM, ANY],
            out_specs=ANY,
            scratch_shapes=[flat, vmem(slots, block_rows, head_dim), dma, dma((add_parts,))],
            compiler_params=PARAMS,
            name=name,
        )(codes, source)

    def near(value):
        return pltpu.with_memory_space_constraint(value, pltpu.VMEM)

    def wide_sum(rows):
        return pltpu.VMEM((3 * rows, column_count), jnp.float32)

    def placed(name, value, cost):
        return pl.pallas_call(
            place_kernel,
            out_shape=flat_shape,
            in_specs=[VMEM],
            out_specs=VMEM,
            compiler_params=PARAMS,
            cost_estimate=pl.CostEstimate(flops=0, transcendentals=0, bytes_accessed=cost),
            name=name,
        )(near(value))

    def add_up(name, returned):
        rows = returned.shape[1]
        return pl.pallas_call(
            functools.partial(sum_kernel, add_parts),
            out_shape=jax.ShapeDtypeStruct((2 * rows, column_count), jnp.bfloat16),
            in_specs=[SMEM, VMEM],
            out_specs=ANY,
            scratch_shapes=[wide_sum(rows), vmem(2 * rows, column_count), dma((send_parts,))],
            compiler_params=PARAMS,
            name=name,
        )(codes, returned)

    slot_tiles = vmem(slots, block_rows, head_dim)
    wide_sem, part_sem = dma((groups,)), dma((add_parts,))
    fetched_keys = exchanged(pack("pack_keys", keys[0]))
    handed_codes = shifted(codes, "section", -1)
    packed_values, handed_codes, places, my_lengths = lax.optimization_barrier(
        (pack("pack_values", values[0]), handed_codes, places, my_lengths)
    )
    fetched_values = exchanged(packed_values)
    weights_shape = (head_count, list_size * block_rows, row_count)
    weights_tile = pltpu.VMEM(weights_shape, jnp.float32)
    first_terms, last_terms, weights = pl.pallas_call(
        functools.partial(value_kernel, list_size, group, scale),
        out_shape=(
            packed_shape(first_rows),
            packed_shape(last_rows),
            jax.ShapeDtypeStruct(weights_shape, jnp.float32),
        ),
        in_specs=[SMEM, SMEM, ANY, ANY, ANY],
        out_specs=(ANY, ANY, ANY),
        scratch_shapes=[flat, flat, slot_tiles]
        + [vmem(slots, rows, head_dim) for rows in (first_rows, last_rows)]
        + [weights_tile, wide_sem, wide_sem, part_sem, part_sem, part_sem, wide_sem],
        compiler_params=PARAMS,
        name="value_terms",
    )(places, my_lengths, queries[0], out_grad[0], fetched_keys)
    handed_terms = shifted(last_terms, "section", -1)
    query_grad, key_terms = pl.pallas_call(
        functools.partial(key_kernel, list_size, group, scale),
        out_shape=(flat_shape, packed_shape(block_rows)),
        in_specs=[SMEM, SMEM, ANY, ANY, ANY, ANY, ANY],
        out_specs=(ANY, ANY),
        scratch_shapes=[flat, flat, slot_tiles, slot_tiles, weights_tile, slot_tiles, flat]
        + [wide_sem, wide_sem, part_sem, part_sem, wide_sem, part_sem, wide_sem],
        compiler_params=PARAMS,
        name="key_terms",
    )(places, my_lengths, queries[0], out_grad[0], fetched_keys, fetched_values, weights)
    first_values = add_up("sum_values", exchanged(first_terms))
    handed_first = shifted(first_values, "section", -1)
    key_terms, handed_terms = lax.optimization_barrier((key_terms, handed_terms))
    returned_keys = exchanged(key_terms)
    handed_queries = placed("place_queries", shifted(query_grad, "section", -1), 5000000)
    returned_keys, handed_queries, first_values = lax.optimization_barrier(
        (returned_keys, handed_queries, first_values)
    )
    key_grad = add_up("sum_keys", near(returned_keys))
    key_grad, handed_terms, handed_first = lax.optimization_barrier(
        (key_grad, handed_terms, handed_first)
    )
    handed_keys = shifted(key_grad, "section", -1)
    handed_values = pl.pallas_call(
        functools.partial(join_kernel, add_parts),
        out_shape=flat_shape,
        in_specs=[SMEM, ANY, VMEM],
        out_specs=ANY,
        scratch_shapes=[wide_sum(last_rows), flat, vmem(2 * first_rows, column_count)]
        + [dma((send_parts,)), dma],
        compiler_params=PARAMS,
        name="join_values",
    )(handed_codes, handed_first, near(exchanged(handed_terms)))
    handed_keys = pl.pallas_call(
        place_last_kernel,
        out_shape=flat_shape,
        in_specs=[VMEM, ANY],
        out_specs=VMEM,
        compiler_params=PARAMS,
        name="place_keys",
    )(near(handed_keys), handed_values)
    return (handed_queries[None], handed_keys[None], handed_values[None])


def solution(mesh):
    placed = (
        P("section", "ctx", None),
        P("section", "ctx", None),
        P("section", "ctx", None),
        P("section", "ctx", None),
        P("section", None, None, None),
        P("section", None, None),
    )
    return jax.shard_map(
        local,
        mesh=mesh,
        in_specs=placed,
        out_specs=(P("section", "ctx", None), P("section", "ctx", None), P("section", "ctx", None)),
        check_vma=False,
    )
```

```python
import functools
import math

import jax
import jax.numpy as jnp
from jax import lax
from jax.experimental import pallas as pl
from jax.experimental.pallas import tpu as pltpu
from jax.sharding import PartitionSpec as P

HEAD_BITS = 8
VMEM = pl.BlockSpec(memory_space=pltpu.VMEM)
SMEM = pl.BlockSpec(memory_space=pltpu.SMEM)
ANY = pl.BlockSpec(memory_space=pl.ANY)
PARAMS = pltpu.CompilerParams(vmem_limit_bytes=56 * 1024 * 1024)
NT = (((1,), (1,)), ((), ()))
NN = (((1,), (0,)), ((), ()))
TN = (((0,), (0,)), ((), ()))
copy = pltpu.make_async_copy


def shifted(value, axis, steps):
    count = lax.axis_size(axis)
    pairs = [(source, (source + steps) % count) for source in range(count)]
    return lax.ppermute(value, axis, pairs)


def tile_of(code, rows, cols):
    block = lax.shift_right_logical(code, HEAD_BITS)
    head = lax.bitwise_and(code, (1 << HEAD_BITS) - 1)
    return (
        pl.ds(pl.multiple_of(block * rows, rows), rows),
        pl.ds(pl.multiple_of(head * cols, cols), cols),
    )


def pack_kernel(parts, codes, source, packed, held, made, got, sent):
    slots, rows, cols = packed.shape
    step = slots // parts
    whole = copy(source, held, got)
    whole.start()
    whole.wait()

    def part_of(part):
        where = pl.ds(part * step, step)
        return copy(made.at[where], packed.at[where], sent.at[part])

    def one_part(part, carry):
        for item in range(step):
            slot = part * step + item
            made[slot] = held[tile_of(jnp.maximum(codes[slot], 0), rows, cols)]
        part_of(part).start()
        return carry

    lax.fori_loop(0, parts, one_part, 0)
    for part in range(parts):
        part_of(part).wait()


def add_terms(codes, terms, wide, heads, parts):
    for index in range(2 * heads):
        wide[index] = jnp.zeros_like(wide[index])
    step = terms.shape[0] // parts

    def one_part(part, carry):
        for item in range(step):
            slot = part * step + item
            code = codes[slot]
            block = lax.shift_right_logical(code, HEAD_BITS)
            head = lax.bitwise_and(code, (1 << HEAD_BITS) - 1)
            index = jnp.where(code < 0, 2 * heads, block * heads + head)
            wide[index] += terms[slot].astype(jnp.float32)
        return carry

    lax.fori_loop(0, parts, one_part, 0)


def fill_block(wide, ready, block, start, part, parts):
    heads = wide.shape[0] // 2
    rows, cols = wide.shape[1:]
    count = heads // parts
    for head in range(part * count, (part + 1) * count):
        ready[start : start + rows, head * cols : (head + 1) * cols] = wide[
            block * heads + head
        ].astype(ready.dtype)


def send_columns(ready, total, sent, parts, fill):
    width = total.shape[1] // parts
    copies = []
    for part in range(parts):
        columns = pl.ds(part * width, width)
        fill(part, columns)
        copies.append(copy(ready.at[:, columns], total.at[:, columns], sent.at[part]))
        copies[-1].start()
    for one in copies:
        one.wait()


def sum_kernel(parts, codes, terms, total, wide, ready, sent):
    add_terms(codes, terms, wide, wide.shape[0] // 2, parts)
    rows = terms.shape[1]

    def fill(part, columns):
        for block in range(2):
            fill_block(wide, ready, block, block * rows, part, sent.shape[0])

    send_columns(ready, total, sent, sent.shape[0], fill)


def join_kernel(
    parts, codes, head_part, terms, total, wide, ready, head, sent, got
):
    head_copy = copy(head_part, head, got)
    head_copy.start()
    add_terms(codes, terms, wide, wide.shape[0] // 2, parts)
    head_copy.wait()
    tail_rows = terms.shape[1]
    head_rows = total.shape[0] // 2 - tail_rows

    def fill(part, columns):
        for block in range(2):
            start = block * (head_rows + tail_rows)
            ready[start : start + head_rows, columns] = head[
                block * head_rows : (block + 1) * head_rows, columns
            ]
            fill_block(wide, ready, block, start + head_rows, part, sent.shape[0])

    send_columns(ready, total, sent, sent.shape[0], fill)


def place_last_kernel(source, after, out):
    out[...] = source[...]


def slot_kernel(list_size, places, lengths, listed, slotted, held, made, got, sent):
    fetched = in_parts(listed, held, got)
    for one in fetched:
        one.start()
    for one in fetched:
        one.wait()

    def one_head(head, carry):
        for item in range(list_size):

            @pl.when(item < lengths[head])
            def _():
                entry = head * list_size + item
                made[places[entry]] = held[entry]

        return carry

    lax.fori_loop(0, lengths.shape[0], one_head, 0)
    ends = in_parts(made, slotted, sent)
    for one in ends:
        one.start()
    for one in ends:
        one.wait()


def place_kernel(source, out):
    out[...] = source[...]


def weights_of(query, key, length, list_size, scale):
    scores = lax.dot_general(key, query, NT, preferred_element_type=jnp.float32)
    row_max = jnp.max(scores, axis=0, keepdims=True)
    exp_scores = jnp.exp2((scores - row_max) * (scale * math.log2(math.e)))
    rows = key.shape[0] // list_size
    parts = [exp_scores[item * rows : (item + 1) * rows] for item in range(list_size)]
    kept = [jnp.where(item < length, 1.0, 0.0).astype(jnp.float32) for item in range(list_size)]
    total = sum(keep * jnp.sum(part, axis=0, keepdims=True) for keep, part in zip(kept, parts))
    inverse = 1.0 / total
    return [part * (inverse * keep) for keep, part in zip(kept, parts)]


def in_parts(source, target, sems):
    parts = sems.shape[0]
    step = source.shape[0] // parts
    wheres = [pl.ds(part * step, step) for part in range(parts)]
    return [
        copy(source.at[where], target.at[where], sems.at[part])
        for part, where in enumerate(wheres)
    ]


def put_terms(places, lengths, list_size, head, result, outs):
    rows = result.shape[0] // list_size
    for entry in range(list_size):

        @pl.when(entry < lengths[head])
        def _():
            start = entry * rows
            for out in outs:
                count = out.shape[1]
                out[places[head * list_size + entry]] = result[start : start + count]
                start += count


def value_kernel(
    list_size, group, scale, places, lengths, queries, grads, keys, first, last, weights_out,
    query_held, grad_held, key_held, first_made, last_made, weights_made,
    query_sem, grad_sem, key_sem, first_sem, last_sem, weights_sem,
):
    rows, cols = keys.shape[1:]
    groups = lengths.shape[0] // group
    width = group * cols

    def fetches(index):
        columns = pl.ds(pl.multiple_of(index * width, width), width)
        return [
            copy(queries.at[:, columns], query_held.at[:, columns], query_sem.at[index]),
            copy(grads.at[:, columns], grad_held.at[:, columns], grad_sem.at[index]),
        ]

    def weights_part(index):
        heads = pl.ds(index * group, group)
        return copy(weights_made.at[heads], weights_out.at[heads], weights_sem.at[index])

    for one in fetches(0) + in_parts(keys, key_held, key_sem):
        one.start()

    def compute(head):
        columns = pl.ds(pl.multiple_of(head * cols, cols), cols)
        key = jnp.concatenate(
            [key_held[places[head * list_size + item]] for item in range(list_size)], axis=0
        )
        weights = weights_of(query_held[:, columns], key, lengths[head], list_size, scale)
        for item, part in enumerate(weights):
            weights_made[head, item * rows : (item + 1) * rows] = part
        weights_low = jnp.concatenate([part.astype(jnp.bfloat16) for part in weights], axis=0)
        return lax.dot_general(
            weights_low, grad_held[:, columns], NN, preferred_element_type=jnp.float32
        ).astype(jnp.bfloat16)

    def one_group(index, carry):
        @pl.when(index + 1 < groups)
        def _():
            for one in fetches(index + 1):
                one.start()

        for one in fetches(index):
            one.wait()

        @pl.when(index == 0)
        def _():
            for one in in_parts(keys, key_held, key_sem):
                one.wait()

        results = [compute(index * group + item) for item in range(group)]
        weights_part(index).start()
        for item, result in enumerate(results):
            head = index * group + item
            put_terms(places, lengths, list_size, head, result, [first_made])
            for entry in range(list_size):
                start, stop = entry * rows + first_made.shape[1], (entry + 1) * rows
                last_made[head * list_size + entry] = result[start:stop]
        return carry

    lax.fori_loop(0, groups, one_group, 0)
    ends = in_parts(last_made, last, last_sem) + in_parts(first_made, first, first_sem)
    for one in ends:
        one.start()
    for index in range(groups):
        weights_part(index).wait()
    for one in ends:
        one.wait()


def key_kernel(
    list_size, group, scale, places, lengths, queries, grads, keys, values, weights,
    query_grad, terms,
    query_held, grad_held, key_held, value_held, weights_held, made, query_made,
    query_sem, grad_sem, key_sem, value_sem, weights_sem, out_sem, query_out_sem,
):
    cols = keys.shape[2]
    groups = lengths.shape[0] // group
    width = group * cols

    def columns_of(index):
        return pl.ds(pl.multiple_of(index * width, width), width)

    def fetches(index):
        columns = columns_of(index)
        heads = pl.ds(index * group, group)
        return [
            copy(grads.at[:, columns], grad_held.at[:, columns], grad_sem.at[index]),
            copy(weights.at[heads], weights_held.at[heads], weights_sem.at[index]),
            copy(queries.at[:, columns], query_held.at[:, columns], query_sem.at[index]),
        ]

    def tile_fetches():
        return in_parts(values, value_held, value_sem) + in_parts(keys, key_held, key_sem)

    def query_part(index):
        columns = columns_of(index)
        return copy(
            query_made.at[:, columns], query_grad.at[:, columns], query_out_sem.at[index]
        )

    for one in fetches(0) + tile_fetches():
        one.start()

    def compute(head):
        columns = pl.ds(pl.multiple_of(head * cols, cols), cols)
        where = [places[head * list_size + item] for item in range(list_size)]
        key = jnp.concatenate([key_held[place] for place in where], axis=0)
        value = jnp.concatenate([value_held[place] for place in where], axis=0)
        weight = weights_held[head]
        weight_low = weight.astype(jnp.bfloat16).astype(jnp.float32)
        dweights = lax.dot_general(
            value, grad_held[:, columns], NT, preferred_element_type=jnp.float32
        )
        row_delta = jnp.sum(weight_low * dweights, axis=0, keepdims=True)
        dscores = (weight * (dweights - row_delta)).astype(jnp.bfloat16)
        flipped = lax.dot_general(key, dscores, TN, preferred_element_type=jnp.float32)
        query_made[:, columns] = (flipped * scale).astype(jnp.bfloat16).T
        made_terms = lax.dot_general(
            dscores, query_held[:, columns], NN, preferred_element_type=jnp.float32
        )
        return (made_terms * scale).astype(jnp.bfloat16)

    def one_group(index, carry):
        @pl.when(index + 1 < groups)
        def _():
            for one in fetches(index + 1):
                one.start()

        for one in fetches(index):
            one.wait()

        @pl.when(index == 0)
        def _():
            for one in tile_fetches():
                one.wait()

        results = [compute(index * group + item) for item in range(group)]
        query_part(index).start()
        for item, result in enumerate(results):
            put_terms(places, lengths, list_size, index * group + item, result, [made])
        return carry

    lax.fori_loop(0, groups, one_group, 0)
    ends = in_parts(made, terms, out_sem)
    for one in ends:
        one.start()
    for index in range(groups):
        query_part(index).wait()
    for one in ends:
        one.wait()


def local(queries, keys, values, out_grad, key_blocks, list_lengths):
    ctx_count = lax.axis_size("ctx")
    my_index = lax.axis_index("ctx")
    row_count, column_count = queries.shape[1:]
    head_count = list_lengths.shape[2]
    head_dim = column_count // head_count
    list_size = key_blocks.shape[3]
    block_rows = row_count // 2
    entries = head_count * list_size
    capacity = (entries + ctx_count - 1) // ctx_count
    slots = ctx_count * capacity
    scale = 1.0 / math.sqrt(head_dim)
    group = 4 if head_count % 4 == 0 else 1
    groups = head_count // group

    chosen = key_blocks[0]
    lengths = list_lengths[0]
    items = jnp.arange(list_size, dtype=jnp.int32)
    heads = jnp.arange(head_count, dtype=jnp.int32)
    is_used = items[None, None, :] < lengths[:, :, None]
    is_mine = is_used & ((chosen >> 1) == my_index)
    hit = jnp.sum(jnp.where(is_mine, 1 + (chosen & 1), 0), axis=2)
    rank = jnp.sum(
        jnp.where((heads[None, None, :] < heads[None, :, None]) & (hit[:, None, :] > 0), 1, 0),
        axis=2,
    )
    code = ((hit - 1) << HEAD_BITS) + heads[None, :]
    ranks = jnp.arange(capacity, dtype=jnp.int32)
    codes = jnp.max(
        jnp.where(
            (hit[:, None, :] > 0) & (rank[:, None, :] == ranks[None, :, None]),
            code[:, None, :],
            -1,
        ),
        axis=2,
    ).reshape(slots)

    my_lengths = lax.dynamic_index_in_dim(lengths, my_index, 0, keepdims=False)
    my_chosen = lax.dynamic_index_in_dim(chosen, my_index, 0, keepdims=False)
    my_used = items[None, :] < my_lengths[:, None]
    my_holder = jnp.where(my_used, my_chosen >> 1, -1)
    earlier = (heads[None, None, :, None] < heads[:, None, None, None]) & (
        my_holder[None, None, :, :] == my_holder[:, :, None, None]
    )
    my_rank = jnp.sum(jnp.where(earlier, 1, 0), axis=(2, 3))
    places = my_holder * capacity + my_rank
    places = jnp.where(my_used, places, places[:, :1]).reshape(entries)

    first_rows = block_rows // 4
    last_rows = block_rows - first_rows
    add_parts = 8 if slots % 8 == 0 and entries % 8 == 0 else 1
    send_parts = 5 if head_count % 5 == 0 else 1
    flat_shape = jax.ShapeDtypeStruct((row_count, column_count), jnp.bfloat16)
    dma = pltpu.SemaphoreType.DMA

    def vmem(*shape):
        return pltpu.VMEM(shape, jnp.bfloat16)

    flat = vmem(row_count, column_count)

    def packed_shape(rows):
        return jax.ShapeDtypeStruct((slots, rows, head_dim), jnp.bfloat16)

    def exchanged(packed):
        parts = packed.reshape(ctx_count, capacity, *packed.shape[1:])
        parts = lax.all_to_all(parts, "ctx", split_axis=0, concat_axis=0, tiled=True)
        return parts.reshape(packed.shape)

    def pack(name, source):
        return pl.pallas_call(
            functools.partial(pack_kernel, add_parts),
            out_shape=packed_shape(block_rows),
            in_specs=[SMEM, ANY],
            out_specs=ANY,
            scratch_shapes=[flat, vmem(slots, block_rows, head_dim), dma, dma((add_parts,))],
            compiler_params=PARAMS,
            name=name,
        )(codes, source)

    def near(value):
        return pltpu.with_memory_space_constraint(value, pltpu.VMEM)

    def wide_sum(rows):
        return pltpu.VMEM((2 * head_count + 1, rows, head_dim), jnp.float32)

    def placed(name, value, cost):
        return pl.pallas_call(
            place_kernel,
            out_shape=flat_shape,
            in_specs=[VMEM],
            out_specs=VMEM,
            compiler_params=PARAMS,
            cost_estimate=pl.CostEstimate(flops=0, transcendentals=0, bytes_accessed=cost),
            name=name,
        )(near(value))

    def add_up(name, returned):
        rows = returned.shape[1]
        return pl.pallas_call(
            functools.partial(sum_kernel, add_parts),
            out_shape=jax.ShapeDtypeStruct((2 * rows, column_count), jnp.bfloat16),
            in_specs=[SMEM, VMEM],
            out_specs=ANY,
            scratch_shapes=[wide_sum(rows), vmem(2 * rows, column_count), dma((send_parts,))],
            compiler_params=PARAMS,
            name=name,
        )(codes, returned)

    slot_tiles = vmem(slots, block_rows, head_dim)
    wide_sem, part_sem = dma((groups,)), dma((add_parts,))
    fetched_keys = exchanged(pack("pack_keys", keys[0]))
    handed_tables = shifted(jnp.concatenate([codes, places, my_lengths]), "section", -1)
    packed_values, handed_tables, places, my_lengths = lax.optimization_barrier(
        (pack("pack_values", values[0]), handed_tables, places, my_lengths)
    )
    handed_codes = handed_tables[:slots]
    handed_places = handed_tables[slots : slots + entries]
    handed_lengths = handed_tables[slots + entries :]
    fetched_values = exchanged(packed_values)
    weights_shape = (head_count, list_size * block_rows, row_count)
    weights_tile = pltpu.VMEM(weights_shape, jnp.float32)
    first_terms, last_terms, weights = pl.pallas_call(
        functools.partial(value_kernel, list_size, group, scale),
        out_shape=(
            packed_shape(first_rows),
            jax.ShapeDtypeStruct((entries, last_rows, head_dim), jnp.bfloat16),
            jax.ShapeDtypeStruct(weights_shape, jnp.float32),
        ),
        in_specs=[SMEM, SMEM, ANY, ANY, ANY],
        out_specs=(ANY, ANY, ANY),
        scratch_shapes=[flat, flat, slot_tiles]
        + [vmem(slots, first_rows, head_dim), vmem(entries, last_rows, head_dim)]
        + [weights_tile, wide_sem, wide_sem, part_sem, part_sem, part_sem, wide_sem],
        compiler_params=PARAMS,
        name="value_terms",
    )(places, my_lengths, queries[0], out_grad[0], fetched_keys)
    handed_terms = shifted(last_terms, "section", -1)
    query_grad, key_terms = pl.pallas_call(
        functools.partial(key_kernel, list_size, group, scale),
        out_shape=(flat_shape, packed_shape(block_rows)),
        in_specs=[SMEM, SMEM, ANY, ANY, ANY, ANY, ANY],
        out_specs=(ANY, ANY),
        scratch_shapes=[flat, flat, slot_tiles, slot_tiles, weights_tile, slot_tiles, flat]
        + [wide_sem, wide_sem, part_sem, part_sem, wide_sem, part_sem, wide_sem],
        compiler_params=PARAMS,
        name="key_terms",
    )(places, my_lengths, queries[0], out_grad[0], fetched_keys, fetched_values, weights)
    first_values = add_up("sum_values", exchanged(first_terms))
    handed_first = shifted(first_values, "section", -1)
    key_terms, handed_terms = lax.optimization_barrier((key_terms, handed_terms))
    returned_keys = exchanged(key_terms)
    handed_queries = placed("place_queries", shifted(query_grad, "section", -1), 5000000)
    handed_terms = pl.pallas_call(
        functools.partial(slot_kernel, list_size),
        out_shape=packed_shape(last_rows),
        in_specs=[SMEM, SMEM, ANY],
        out_specs=ANY,
        scratch_shapes=[vmem(entries, last_rows, head_dim), vmem(slots, last_rows, head_dim)]
        + [part_sem, part_sem],
        compiler_params=PARAMS,
        name="slot_values",
    )(handed_places, handed_lengths, handed_terms)
    returned_keys, handed_queries, first_values, handed_terms = lax.optimization_barrier(
        (returned_keys, handed_queries, first_values, handed_terms)
    )
    key_grad = add_up("sum_keys", near(returned_keys))
    key_grad, handed_terms, handed_first = lax.optimization_barrier(
        (key_grad, handed_terms, handed_first)
    )
    handed_keys = shifted(key_grad, "section", -1)
    handed_values = pl.pallas_call(
        functools.partial(join_kernel, add_parts),
        out_shape=flat_shape,
        in_specs=[SMEM, ANY, VMEM],
        out_specs=ANY,
        scratch_shapes=[wide_sum(last_rows), flat, vmem(2 * first_rows, column_count)]
        + [dma((send_parts,)), dma],
        compiler_params=PARAMS,
        name="join_values",
    )(handed_codes, handed_first, near(exchanged(handed_terms)))
    handed_keys = pl.pallas_call(
        place_last_kernel,
        out_shape=flat_shape,
        in_specs=[VMEM, ANY],
        out_specs=VMEM,
        compiler_params=PARAMS,
        name="place_keys",
    )(near(handed_keys), handed_values)
    return (handed_queries[None], handed_keys[None], handed_values[None])


def solution(mesh):
    placed = (
        P("section", "ctx", None),
        P("section", "ctx", None),
        P("section", "ctx", None),
        P("section", "ctx", None),
        P("section", None, None, None),
        P("section", None, None),
    )
    return jax.shard_map(
        local,
        mesh=mesh,
        in_specs=placed,
        out_specs=(P("section", "ctx", None), P("section", "ctx", None), P("section", "ctx", None)),
        check_vma=False,
    )
```

```python
import functools
import math

import jax
import jax.numpy as jnp
from jax import lax
from jax.experimental import pallas as pl
from jax.experimental.pallas import tpu as pltpu
from jax.sharding import PartitionSpec as P

HEAD_BITS = 8
VMEM = pl.BlockSpec(memory_space=pltpu.VMEM)
SMEM = pl.BlockSpec(memory_space=pltpu.SMEM)
ANY = pl.BlockSpec(memory_space=pl.ANY)
PARAMS = pltpu.CompilerParams(vmem_limit_bytes=56 * 1024 * 1024)
NT = (((1,), (1,)), ((), ()))
NN = (((1,), (0,)), ((), ()))
TN = (((0,), (0,)), ((), ()))
copy = pltpu.make_async_copy


def shifted(value, axis, steps):
    count = lax.axis_size(axis)
    pairs = [(source, (source + steps) % count) for source in range(count)]
    return lax.ppermute(value, axis, pairs)


def tile_of(code, rows, cols):
    block = lax.shift_right_logical(code, HEAD_BITS)
    head = lax.bitwise_and(code, (1 << HEAD_BITS) - 1)
    return (
        pl.ds(pl.multiple_of(block * rows, rows), rows),
        pl.ds(pl.multiple_of(head * cols, cols), cols),
    )


def pack_kernel(parts, codes, source, packed, held, made, got, sent):
    slots, rows, cols = packed.shape
    step = slots // parts
    whole = copy(source, held, got)
    whole.start()
    whole.wait()

    def part_of(part):
        where = pl.ds(part * step, step)
        return copy(made.at[where], packed.at[where], sent.at[part])

    def one_part(part, carry):
        for item in range(step):
            slot = part * step + item
            made[slot] = held[tile_of(jnp.maximum(codes[slot], 0), rows, cols)]
        part_of(part).start()
        return carry

    lax.fori_loop(0, parts, one_part, 0)
    for part in range(parts):
        part_of(part).wait()


def add_terms(codes, terms, wide, heads, parts):
    for index in range(2 * heads):
        wide[index] = jnp.zeros_like(wide[index])
    step = terms.shape[0] // parts

    def one_part(part, carry):
        for item in range(step):
            slot = part * step + item
            code = codes[slot]
            block = lax.shift_right_logical(code, HEAD_BITS)
            head = lax.bitwise_and(code, (1 << HEAD_BITS) - 1)
            index = jnp.where(code < 0, 2 * heads, block * heads + head)
            wide[index] += terms[slot].astype(jnp.float32)
        return carry

    lax.fori_loop(0, parts, one_part, 0)


def fill_block(wide, ready, block, start, part, parts):
    heads = wide.shape[0] // 2
    rows, cols = wide.shape[1:]
    count = heads // parts
    for head in range(part * count, (part + 1) * count):
        ready[start : start + rows, head * cols : (head + 1) * cols] = wide[
            block * heads + head
        ].astype(ready.dtype)


def send_columns(ready, total, sent, parts, fill):
    width = total.shape[1] // parts
    copies = []
    for part in range(parts):
        columns = pl.ds(part * width, width)
        fill(part, columns)
        copies.append(copy(ready.at[:, columns], total.at[:, columns], sent.at[part]))
        copies[-1].start()
    for one in copies:
        one.wait()


def sum_kernel(parts, codes, terms, total, wide, ready, sent):
    add_terms(codes, terms, wide, wide.shape[0] // 2, parts)
    rows = terms.shape[1]

    def fill(part, columns):
        for block in range(2):
            fill_block(wide, ready, block, block * rows, part, sent.shape[0])

    send_columns(ready, total, sent, sent.shape[0], fill)


def join_kernel(
    parts, codes, head_part, terms, total, wide, ready, head, sent, got
):
    head_copy = copy(head_part, head, got)
    head_copy.start()
    add_terms(codes, terms, wide, wide.shape[0] // 2, parts)
    head_copy.wait()
    tail_rows = terms.shape[1]
    head_rows = total.shape[0] // 2 - tail_rows

    def fill(part, columns):
        for block in range(2):
            start = block * (head_rows + tail_rows)
            ready[start : start + head_rows, columns] = head[
                block * head_rows : (block + 1) * head_rows, columns
            ]
            fill_block(wide, ready, block, start + head_rows, part, sent.shape[0])

    send_columns(ready, total, sent, sent.shape[0], fill)


def place_last_kernel(source, after, out):
    out[...] = source[...]


def place_kernel(source, out):
    out[...] = source[...]


def weights_of(query, key, length, list_size, scale):
    scores = lax.dot_general(key, query, NT, preferred_element_type=jnp.float32)
    row_max = jnp.max(scores, axis=0, keepdims=True)
    exp_scores = jnp.exp2((scores - row_max) * (scale * math.log2(math.e)))
    rows = key.shape[0] // list_size
    parts = [exp_scores[item * rows : (item + 1) * rows] for item in range(list_size)]
    kept = [jnp.where(item < length, 1.0, 0.0).astype(jnp.float32) for item in range(list_size)]
    total = sum(keep * jnp.sum(part, axis=0, keepdims=True) for keep, part in zip(kept, parts))
    inverse = 1.0 / total
    return [part * (inverse * keep) for keep, part in zip(kept, parts)]


def in_parts(source, target, sems):
    parts = sems.shape[0]
    step = source.shape[0] // parts
    wheres = [pl.ds(part * step, step) for part in range(parts)]
    return [
        copy(source.at[where], target.at[where], sems.at[part])
        for part, where in enumerate(wheres)
    ]


def put_terms(places, lengths, list_size, head, result, outs):
    rows = result.shape[0] // list_size
    for entry in range(list_size):

        @pl.when(entry < lengths[head])
        def _():
            start = entry * rows
            for out in outs:
                count = out.shape[1]
                out[places[head * list_size + entry]] = result[start : start + count]
                start += count


def value_kernel(
    list_size, group, scale, places, lengths, queries, grads, keys, first, last, weights_out,
    key_held, first_made, last_made, weights_made, key_sem, first_sem, last_sem, weights_sem,
):
    rows, cols = keys.shape[1:]
    groups = lengths.shape[0] // group

    def weights_part(index):
        heads = pl.ds(index * group, group)
        return copy(weights_made.at[heads], weights_out.at[heads], weights_sem.at[index])

    for one in in_parts(keys, key_held, key_sem):
        one.start()

    def compute(head):
        columns = pl.ds(pl.multiple_of(head * cols, cols), cols)
        key = jnp.concatenate(
            [key_held[places[head * list_size + item]] for item in range(list_size)], axis=0
        )
        weights = weights_of(queries[:, columns], key, lengths[head], list_size, scale)
        for item, part in enumerate(weights):
            weights_made[head, item * rows : (item + 1) * rows] = part
        weights_low = jnp.concatenate([part.astype(jnp.bfloat16) for part in weights], axis=0)
        return lax.dot_general(
            weights_low, grads[:, columns], NN, preferred_element_type=jnp.float32
        ).astype(jnp.bfloat16)

    def one_group(index, carry):
        @pl.when(index == 0)
        def _():
            for one in in_parts(keys, key_held, key_sem):
                one.wait()

        results = [compute(index * group + item) for item in range(group)]
        weights_part(index).start()
        for item, result in enumerate(results):
            put_terms(
                places, lengths, list_size, index * group + item, result, [first_made, last_made]
            )
        return carry

    lax.fori_loop(0, groups, one_group, 0)
    ends = in_parts(last_made, last, last_sem) + in_parts(first_made, first, first_sem)
    for one in ends:
        one.start()
    for index in range(groups):
        weights_part(index).wait()
    for one in ends:
        one.wait()


def key_kernel(
    list_size, group, scale, places, lengths, queries, grads, keys, values, weights,
    query_grad, terms,
    key_held, value_held, weights_held, made, query_made,
    key_sem, value_sem, weights_sem, out_sem, query_out_sem,
):
    cols = keys.shape[2]
    groups = lengths.shape[0] // group
    width = group * cols

    def columns_of(index):
        return pl.ds(pl.multiple_of(index * width, width), width)

    def weights_part(index):
        heads = pl.ds(index * group, group)
        return copy(weights.at[heads], weights_held.at[heads], weights_sem.at[index])

    def tile_fetches():
        return in_parts(values, value_held, value_sem) + in_parts(keys, key_held, key_sem)

    def query_part(index):
        columns = columns_of(index)
        return copy(
            query_made.at[:, columns], query_grad.at[:, columns], query_out_sem.at[index]
        )

    for one in tile_fetches() + [weights_part(index) for index in range(groups)]:
        one.start()

    def compute(head):
        columns = pl.ds(pl.multiple_of(head * cols, cols), cols)
        where = [places[head * list_size + item] for item in range(list_size)]
        key = jnp.concatenate([key_held[place] for place in where], axis=0)
        value = jnp.concatenate([value_held[place] for place in where], axis=0)
        weight = weights_held[head]
        weight_low = weight.astype(jnp.bfloat16).astype(jnp.float32)
        dweights = lax.dot_general(
            value, grads[:, columns], NT, preferred_element_type=jnp.float32
        )
        row_delta = jnp.sum(weight_low * dweights, axis=0, keepdims=True)
        dscores = (weight * (dweights - row_delta)).astype(jnp.bfloat16)
        flipped = lax.dot_general(key, dscores, TN, preferred_element_type=jnp.float32)
        query_made[:, columns] = (flipped * scale).astype(jnp.bfloat16).T
        made_terms = lax.dot_general(
            dscores, queries[:, columns], NN, preferred_element_type=jnp.float32
        )
        return (made_terms * scale).astype(jnp.bfloat16)

    def one_group(index, carry):
        weights_part(index).wait()

        @pl.when(index == 0)
        def _():
            for one in tile_fetches():
                one.wait()

        results = [compute(index * group + item) for item in range(group)]
        query_part(index).start()
        for item, result in enumerate(results):
            put_terms(places, lengths, list_size, index * group + item, result, [made])
        return carry

    lax.fori_loop(0, groups, one_group, 0)
    ends = in_parts(made, terms, out_sem)
    for one in ends:
        one.start()
    for index in range(groups):
        query_part(index).wait()
    for one in ends:
        one.wait()


def local(queries, keys, values, out_grad, key_blocks, list_lengths):
    ctx_count = lax.axis_size("ctx")
    my_index = lax.axis_index("ctx")
    row_count, column_count = queries.shape[1:]
    head_count = list_lengths.shape[2]
    head_dim = column_count // head_count
    list_size = key_blocks.shape[3]
    block_rows = row_count // 2
    entries = head_count * list_size
    capacity = (entries + ctx_count - 1) // ctx_count
    slots = ctx_count * capacity
    scale = 1.0 / math.sqrt(head_dim)
    group = 4 if head_count % 4 == 0 else 1
    groups = head_count // group

    chosen = key_blocks[0]
    lengths = list_lengths[0]
    items = jnp.arange(list_size, dtype=jnp.int32)
    heads = jnp.arange(head_count, dtype=jnp.int32)
    is_used = items[None, None, :] < lengths[:, :, None]
    is_mine = is_used & ((chosen >> 1) == my_index)
    hit = jnp.sum(jnp.where(is_mine, 1 + (chosen & 1), 0), axis=2)
    rank = jnp.sum(
        jnp.where((heads[None, None, :] < heads[None, :, None]) & (hit[:, None, :] > 0), 1, 0),
        axis=2,
    )
    code = ((hit - 1) << HEAD_BITS) + heads[None, :]
    ranks = jnp.arange(capacity, dtype=jnp.int32)
    codes = jnp.max(
        jnp.where(
            (hit[:, None, :] > 0) & (rank[:, None, :] == ranks[None, :, None]),
            code[:, None, :],
            -1,
        ),
        axis=2,
    ).reshape(slots)

    my_lengths = lax.dynamic_index_in_dim(lengths, my_index, 0, keepdims=False)
    my_chosen = lax.dynamic_index_in_dim(chosen, my_index, 0, keepdims=False)
    my_used = items[None, :] < my_lengths[:, None]
    my_holder = jnp.where(my_used, my_chosen >> 1, -1)
    earlier = (heads[None, None, :, None] < heads[:, None, None, None]) & (
        my_holder[None, None, :, :] == my_holder[:, :, None, None]
    )
    my_rank = jnp.sum(jnp.where(earlier, 1, 0), axis=(2, 3))
    places = my_holder * capacity + my_rank
    places = jnp.where(my_used, places, places[:, :1]).reshape(entries)

    first_rows = 3 * block_rows // 8
    last_rows = block_rows - first_rows
    add_parts = 8 if slots % 8 == 0 else 1
    send_parts = 5 if head_count % 5 == 0 else 1
    flat_shape = jax.ShapeDtypeStruct((row_count, column_count), jnp.bfloat16)
    dma = pltpu.SemaphoreType.DMA

    def vmem(*shape):
        return pltpu.VMEM(shape, jnp.bfloat16)

    flat = vmem(row_count, column_count)

    def packed_shape(rows):
        return jax.ShapeDtypeStruct((slots, rows, head_dim), jnp.bfloat16)

    def exchanged(packed):
        parts = packed.reshape(ctx_count, capacity, *packed.shape[1:])
        parts = lax.all_to_all(parts, "ctx", split_axis=0, concat_axis=0, tiled=True)
        return parts.reshape(packed.shape)

    def near(value):
        return pltpu.with_memory_space_constraint(value, pltpu.VMEM)

    def pack(name, source):
        return pl.pallas_call(
            functools.partial(pack_kernel, add_parts),
            out_shape=packed_shape(block_rows),
            in_specs=[SMEM, ANY],
            out_specs=ANY,
            scratch_shapes=[flat, vmem(slots, block_rows, head_dim), dma, dma((add_parts,))],
            compiler_params=PARAMS,
            name=name,
        )(codes, source)

    def wide_sum(rows):
        return pltpu.VMEM((2 * head_count + 1, rows, head_dim), jnp.float32)

    def placed(name, value, cost):
        return pl.pallas_call(
            place_kernel,
            out_shape=flat_shape,
            in_specs=[VMEM],
            out_specs=VMEM,
            compiler_params=PARAMS,
            cost_estimate=pl.CostEstimate(flops=0, transcendentals=0, bytes_accessed=cost),
            name=name,
        )(near(value))

    def add_up(name, returned):
        rows = returned.shape[1]
        return pl.pallas_call(
            functools.partial(sum_kernel, add_parts),
            out_shape=jax.ShapeDtypeStruct((2 * rows, column_count), jnp.bfloat16),
            in_specs=[SMEM, VMEM],
            out_specs=ANY,
            scratch_shapes=[wide_sum(rows), vmem(2 * rows, column_count), dma((send_parts,))],
            compiler_params=PARAMS,
            name=name,
        )(codes, returned)

    slot_tiles = vmem(slots, block_rows, head_dim)
    wide_sem, part_sem = dma((groups,)), dma((add_parts,))
    fetched_keys = exchanged(pack("pack_keys", keys[0]))
    handed_codes = shifted(codes, "section", -1)
    packed_values, handed_codes, places, my_lengths = lax.optimization_barrier(
        (pack("pack_values", near(values[0])), handed_codes, places, my_lengths)
    )
    fetched_values = exchanged(packed_values)
    weights_shape = (head_count, list_size * block_rows, row_count)
    weights_tile = pltpu.VMEM(weights_shape, jnp.float32)
    first_terms, last_terms, weights = pl.pallas_call(
        functools.partial(value_kernel, list_size, group, scale),
        out_shape=(
            packed_shape(first_rows),
            packed_shape(last_rows),
            jax.ShapeDtypeStruct(weights_shape, jnp.float32),
        ),
        in_specs=[SMEM, SMEM, VMEM, VMEM, ANY],
        out_specs=(ANY, ANY, ANY),
        scratch_shapes=[slot_tiles]
        + [vmem(slots, rows, head_dim) for rows in (first_rows, last_rows)]
        + [weights_tile, part_sem, part_sem, part_sem, wide_sem],
        compiler_params=PARAMS,
        name="value_terms",
    )(places, my_lengths, near(queries[0]), near(out_grad[0]), fetched_keys)
    handed_terms = shifted(last_terms, "section", -1)
    query_grad, key_terms = pl.pallas_call(
        functools.partial(key_kernel, list_size, group, scale),
        out_shape=(flat_shape, packed_shape(block_rows)),
        in_specs=[SMEM, SMEM, VMEM, VMEM, ANY, ANY, ANY],
        out_specs=(ANY, ANY),
        scratch_shapes=[slot_tiles, slot_tiles, weights_tile, slot_tiles, flat]
        + [part_sem, part_sem, wide_sem, part_sem, wide_sem],
        compiler_params=PARAMS,
        name="key_terms",
    )(
        places,
        my_lengths,
        near(queries[0]),
        near(out_grad[0]),
        fetched_keys,
        fetched_values,
        weights,
    )
    first_values = add_up("sum_values", exchanged(first_terms))
    handed_first = shifted(first_values, "section", -1)
    key_terms, handed_terms = lax.optimization_barrier((key_terms, handed_terms))
    returned_keys = exchanged(key_terms)
    handed_queries = placed("place_queries", shifted(query_grad, "section", -1), 5000000)
    returned_keys, handed_queries, first_values = lax.optimization_barrier(
        (returned_keys, handed_queries, first_values)
    )
    key_grad = add_up("sum_keys", near(returned_keys))
    key_grad, handed_terms, handed_first = lax.optimization_barrier(
        (key_grad, handed_terms, handed_first)
    )
    handed_keys = shifted(key_grad, "section", -1)
    handed_values = pl.pallas_call(
        functools.partial(join_kernel, add_parts),
        out_shape=flat_shape,
        in_specs=[SMEM, ANY, VMEM],
        out_specs=ANY,
        scratch_shapes=[wide_sum(last_rows), flat, vmem(2 * first_rows, column_count)]
        + [dma((send_parts,)), dma],
        compiler_params=PARAMS,
        name="join_values",
    )(handed_codes, handed_first, near(exchanged(handed_terms)))
    handed_keys = pl.pallas_call(
        place_last_kernel,
        out_shape=flat_shape,
        in_specs=[VMEM, ANY],
        out_specs=VMEM,
        compiler_params=PARAMS,
        name="place_keys",
    )(near(handed_keys), handed_values)
    return (handed_queries[None], handed_keys[None], handed_values[None])


def solution(mesh):
    placed = (
        P("section", "ctx", None),
        P("section", "ctx", None),
        P("section", "ctx", None),
        P("section", "ctx", None),
        P("section", None, None, None),
        P("section", None, None),
    )
    return jax.shard_map(
        local,
        mesh=mesh,
        in_specs=placed,
        out_specs=(P("section", "ctx", None), P("section", "ctx", None), P("section", "ctx", None)),
        check_vma=False,
    )
```

```python
import functools
import math

import jax
import jax.numpy as jnp
from jax import lax
from jax.experimental import pallas as pl
from jax.experimental.pallas import tpu as pltpu
from jax.sharding import PartitionSpec as P

HEAD_BITS = 8
VMEM = pl.BlockSpec(memory_space=pltpu.VMEM)
SMEM = pl.BlockSpec(memory_space=pltpu.SMEM)
ANY = pl.BlockSpec(memory_space=pl.ANY)
PARAMS = pltpu.CompilerParams(vmem_limit_bytes=56 * 1024 * 1024)
NT = (((1,), (1,)), ((), ()))
NN = (((1,), (0,)), ((), ()))
TN = (((0,), (0,)), ((), ()))
copy = pltpu.make_async_copy


def shifted(value, axis, steps):
    count = lax.axis_size(axis)
    pairs = [(source, (source + steps) % count) for source in range(count)]
    return lax.ppermute(value, axis, pairs)


def tile_of(code, rows, cols):
    block = lax.shift_right_logical(code, HEAD_BITS)
    head = lax.bitwise_and(code, (1 << HEAD_BITS) - 1)
    return (
        pl.ds(pl.multiple_of(block * rows, rows), rows),
        pl.ds(pl.multiple_of(head * cols, cols), cols),
    )


def pack_kernel(parts, codes, source, packed, made, sent):
    slots, rows, cols = packed.shape
    step = slots // parts

    def part_of(part):
        where = pl.ds(part * step, step)
        return copy(made.at[where], packed.at[where], sent.at[part])

    def one_part(part, carry):
        for item in range(step):
            slot = part * step + item
            made[slot] = source[tile_of(jnp.maximum(codes[slot], 0), rows, cols)]
        part_of(part).start()
        return carry

    lax.fori_loop(0, parts, one_part, 0)
    for part in range(parts):
        part_of(part).wait()


def add_terms(codes, terms, wide, heads, parts):
    for index in range(2 * heads):
        wide[index] = jnp.zeros_like(wide[index])
    step = terms.shape[0] // parts

    def one_part(part, carry):
        for item in range(step):
            slot = part * step + item
            code = codes[slot]
            block = lax.shift_right_logical(code, HEAD_BITS)
            head = lax.bitwise_and(code, (1 << HEAD_BITS) - 1)
            index = jnp.where(code < 0, 2 * heads, block * heads + head)
            wide[index] += terms[slot].astype(jnp.float32)
        return carry

    lax.fori_loop(0, parts, one_part, 0)


def fill_block(wide, ready, block, start, part, parts):
    heads = wide.shape[0] // 2
    rows, cols = wide.shape[1:]
    count = heads // parts
    for head in range(part * count, (part + 1) * count):
        ready[start : start + rows, head * cols : (head + 1) * cols] = wide[
            block * heads + head
        ].astype(ready.dtype)


def send_columns(ready, total, sent, parts, fill):
    width = total.shape[1] // parts
    copies = []
    for part in range(parts):
        columns = pl.ds(part * width, width)
        fill(part, columns)
        copies.append(copy(ready.at[:, columns], total.at[:, columns], sent.at[part]))
        copies[-1].start()
    for one in copies:
        one.wait()


def sum_kernel(parts, codes, terms, total, wide, ready, sent):
    add_terms(codes, terms, wide, wide.shape[0] // 2, parts)
    rows = terms.shape[1]

    def fill(part, columns):
        for block in range(2):
            fill_block(wide, ready, block, block * rows, part, sent.shape[0])

    send_columns(ready, total, sent, sent.shape[0], fill)


def join_kernel(
    parts, codes, head_part, terms, total, wide, ready, head, sent, got
):
    head_copy = copy(head_part, head, got)
    head_copy.start()
    add_terms(codes, terms, wide, wide.shape[0] // 2, parts)
    head_copy.wait()
    tail_rows = terms.shape[1]
    head_rows = total.shape[0] // 2 - tail_rows

    def fill(part, columns):
        for block in range(2):
            start = block * (head_rows + tail_rows)
            ready[start : start + head_rows, columns] = head[
                block * head_rows : (block + 1) * head_rows, columns
            ]
            fill_block(wide, ready, block, start + head_rows, part, sent.shape[0])

    send_columns(ready, total, sent, sent.shape[0], fill)


def place_last_kernel(source, after, out):
    out[...] = source[...]


def place_kernel(source, out):
    out[...] = source[...]


def weights_of(query, key, length, list_size, scale):
    scores = lax.dot_general(key, query, NT, preferred_element_type=jnp.float32)
    row_max = jnp.max(scores, axis=0, keepdims=True)
    exp_scores = jnp.exp2((scores - row_max) * (scale * math.log2(math.e)))
    rows = key.shape[0] // list_size
    parts = [exp_scores[item * rows : (item + 1) * rows] for item in range(list_size)]
    kept = [jnp.where(item < length, 1.0, 0.0).astype(jnp.float32) for item in range(list_size)]
    total = sum(keep * jnp.sum(part, axis=0, keepdims=True) for keep, part in zip(kept, parts))
    inverse = 1.0 / total
    return [part * (inverse * keep) for keep, part in zip(kept, parts)]


def in_parts(source, target, sems):
    parts = sems.shape[0]
    step = source.shape[0] // parts
    wheres = [pl.ds(part * step, step) for part in range(parts)]
    return [
        copy(source.at[where], target.at[where], sems.at[part])
        for part, where in enumerate(wheres)
    ]


def put_terms(places, lengths, list_size, head, result, outs):
    rows = result.shape[0] // list_size
    for entry in range(list_size):

        @pl.when(entry < lengths[head])
        def _():
            start = entry * rows
            for out in outs:
                count = out.shape[1]
                out[places[head * list_size + entry]] = result[start : start + count]
                start += count


def value_kernel(
    list_size, group, scale, places, lengths, queries, grads, keys, first, last, weights_out,
    key_held, first_made, last_made, weights_made, key_sem, first_sem, last_sem, weights_sem,
):
    rows, cols = keys.shape[1:]
    groups = lengths.shape[0] // group

    def weights_part(index):
        heads = pl.ds(index * group, group)
        return copy(weights_made.at[heads], weights_out.at[heads], weights_sem.at[index])

    for one in in_parts(keys, key_held, key_sem):
        one.start()

    def compute(head):
        columns = pl.ds(pl.multiple_of(head * cols, cols), cols)
        key = jnp.concatenate(
            [key_held[places[head * list_size + item]] for item in range(list_size)], axis=0
        )
        weights = weights_of(queries[:, columns], key, lengths[head], list_size, scale)
        for item, part in enumerate(weights):
            weights_made[head, item * rows : (item + 1) * rows] = part
        weights_low = jnp.concatenate([part.astype(jnp.bfloat16) for part in weights], axis=0)
        return lax.dot_general(
            weights_low, grads[:, columns], NN, preferred_element_type=jnp.float32
        ).astype(jnp.bfloat16)

    def one_group(index, carry):
        @pl.when(index == 0)
        def _():
            for one in in_parts(keys, key_held, key_sem):
                one.wait()

        results = [compute(index * group + item) for item in range(group)]
        weights_part(index).start()
        for item, result in enumerate(results):
            put_terms(
                places, lengths, list_size, index * group + item, result, [first_made, last_made]
            )
        return carry

    lax.fori_loop(0, groups, one_group, 0)
    ends = in_parts(last_made, last, last_sem) + in_parts(first_made, first, first_sem)
    for one in ends:
        one.start()
    for index in range(groups):
        weights_part(index).wait()
    for one in ends:
        one.wait()


def key_kernel(
    list_size, group, scale, places, lengths, queries, grads, keys, values, weights,
    query_grad, terms,
    key_held, value_held, weights_held, made, query_made,
    key_sem, value_sem, weights_sem, out_sem, query_out_sem,
):
    cols = keys.shape[2]
    groups = lengths.shape[0] // group
    width = group * cols

    def columns_of(index):
        return pl.ds(pl.multiple_of(index * width, width), width)

    def weights_part(index):
        heads = pl.ds(index * group, group)
        return copy(weights.at[heads], weights_held.at[heads], weights_sem.at[index])

    def tile_fetches():
        return in_parts(values, value_held, value_sem) + in_parts(keys, key_held, key_sem)

    def query_part(index):
        columns = columns_of(index)
        return copy(
            query_made.at[:, columns], query_grad.at[:, columns], query_out_sem.at[index]
        )

    parts = key_sem.shape[0]
    tile_starts = tile_fetches()
    for one in tile_starts[:parts] + [weights_part(0)] + tile_starts[parts:]:
        one.start()

    def compute(head):
        columns = pl.ds(pl.multiple_of(head * cols, cols), cols)
        where = [places[head * list_size + item] for item in range(list_size)]
        key = jnp.concatenate([key_held[place] for place in where], axis=0)
        value = jnp.concatenate([value_held[place] for place in where], axis=0)
        weight = weights_held[head]
        weight_low = weight.astype(jnp.bfloat16).astype(jnp.float32)
        dweights = lax.dot_general(
            value, grads[:, columns], NT, preferred_element_type=jnp.float32
        )
        row_delta = jnp.sum(weight_low * dweights, axis=0, keepdims=True)
        dscores = (weight * (dweights - row_delta)).astype(jnp.bfloat16)
        flipped = lax.dot_general(key, dscores, TN, preferred_element_type=jnp.float32)
        query_made[:, columns] = (flipped * scale).astype(jnp.bfloat16).T
        made_terms = lax.dot_general(
            dscores, queries[:, columns], NN, preferred_element_type=jnp.float32
        )
        return (made_terms * scale).astype(jnp.bfloat16)

    def one_group(index, carry):
        @pl.when(index + 1 < groups)
        def _():
            weights_part(index + 1).start()

        weights_part(index).wait()

        @pl.when(index == 0)
        def _():
            for one in tile_fetches():
                one.wait()

        results = [compute(index * group + item) for item in range(group)]
        query_part(index).start()
        for item, result in enumerate(results):
            put_terms(places, lengths, list_size, index * group + item, result, [made])
        return carry

    lax.fori_loop(0, groups, one_group, 0)
    ends = in_parts(made, terms, out_sem)
    for one in ends:
        one.start()
    for index in range(groups):
        query_part(index).wait()
    for one in ends:
        one.wait()


def local(queries, keys, values, out_grad, key_blocks, list_lengths):
    ctx_count = lax.axis_size("ctx")
    my_index = lax.axis_index("ctx")
    row_count, column_count = queries.shape[1:]
    head_count = list_lengths.shape[2]
    head_dim = column_count // head_count
    list_size = key_blocks.shape[3]
    block_rows = row_count // 2
    entries = head_count * list_size
    capacity = (entries + ctx_count - 1) // ctx_count
    slots = ctx_count * capacity
    scale = 1.0 / math.sqrt(head_dim)
    group = 4 if head_count % 4 == 0 else 1
    groups = head_count // group

    chosen = key_blocks[0]
    lengths = list_lengths[0]
    items = jnp.arange(list_size, dtype=jnp.int32)
    heads = jnp.arange(head_count, dtype=jnp.int32)
    is_used = items[None, None, :] < lengths[:, :, None]
    is_mine = is_used & ((chosen >> 1) == my_index)
    hit = jnp.sum(jnp.where(is_mine, 1 + (chosen & 1), 0), axis=2)
    rank = jnp.sum(
        jnp.where((heads[None, None, :] < heads[None, :, None]) & (hit[:, None, :] > 0), 1, 0),
        axis=2,
    )
    code = ((hit - 1) << HEAD_BITS) + heads[None, :]
    ranks = jnp.arange(capacity, dtype=jnp.int32)
    codes = jnp.max(
        jnp.where(
            (hit[:, None, :] > 0) & (rank[:, None, :] == ranks[None, :, None]),
            code[:, None, :],
            -1,
        ),
        axis=2,
    ).reshape(slots)

    my_lengths = lax.dynamic_index_in_dim(lengths, my_index, 0, keepdims=False)
    my_chosen = lax.dynamic_index_in_dim(chosen, my_index, 0, keepdims=False)
    my_used = items[None, :] < my_lengths[:, None]
    my_holder = jnp.where(my_used, my_chosen >> 1, -1)
    earlier = (heads[None, None, :, None] < heads[:, None, None, None]) & (
        my_holder[None, None, :, :] == my_holder[:, :, None, None]
    )
    my_rank = jnp.sum(jnp.where(earlier, 1, 0), axis=(2, 3))
    places = my_holder * capacity + my_rank
    places = jnp.where(my_used, places, places[:, :1]).reshape(entries)

    first_rows = 3 * block_rows // 8
    last_rows = block_rows - first_rows
    add_parts = 8 if slots % 8 == 0 else 1
    send_parts = 5 if head_count % 5 == 0 else 1
    flat_shape = jax.ShapeDtypeStruct((row_count, column_count), jnp.bfloat16)
    dma = pltpu.SemaphoreType.DMA

    def vmem(*shape):
        return pltpu.VMEM(shape, jnp.bfloat16)

    flat = vmem(row_count, column_count)

    def packed_shape(rows):
        return jax.ShapeDtypeStruct((slots, rows, head_dim), jnp.bfloat16)

    def exchanged(packed):
        parts = packed.reshape(ctx_count, capacity, *packed.shape[1:])
        parts = lax.all_to_all(parts, "ctx", split_axis=0, concat_axis=0, tiled=True)
        return parts.reshape(packed.shape)

    def near(value):
        return pltpu.with_memory_space_constraint(value, pltpu.VMEM)

    def pack(name, source):
        return pl.pallas_call(
            functools.partial(pack_kernel, add_parts),
            out_shape=packed_shape(block_rows),
            in_specs=[SMEM, VMEM],
            out_specs=ANY,
            scratch_shapes=[vmem(slots, block_rows, head_dim), dma((add_parts,))],
            compiler_params=PARAMS,
            name=name,
        )(codes, source)

    def wide_sum(rows):
        return pltpu.VMEM((2 * head_count + 1, rows, head_dim), jnp.float32)

    def placed(name, value, cost):
        return pl.pallas_call(
            place_kernel,
            out_shape=flat_shape,
            in_specs=[VMEM],
            out_specs=VMEM,
            compiler_params=PARAMS,
            cost_estimate=pl.CostEstimate(flops=0, transcendentals=0, bytes_accessed=cost),
            name=name,
        )(near(value))

    def add_up(name, returned):
        rows = returned.shape[1]
        return pl.pallas_call(
            functools.partial(sum_kernel, add_parts),
            out_shape=jax.ShapeDtypeStruct((2 * rows, column_count), jnp.bfloat16),
            in_specs=[SMEM, VMEM],
            out_specs=ANY,
            scratch_shapes=[wide_sum(rows), vmem(2 * rows, column_count), dma((send_parts,))],
            compiler_params=PARAMS,
            name=name,
        )(codes, returned)

    slot_tiles = vmem(slots, block_rows, head_dim)
    wide_sem, part_sem = dma((groups,)), dma((add_parts,))
    fetched_keys = exchanged(pack("pack_keys", near(keys[0])))
    handed_codes = shifted(codes, "section", -1)
    packed_values, handed_codes, places, my_lengths = lax.optimization_barrier(
        (pack("pack_values", near(values[0])), handed_codes, places, my_lengths)
    )
    fetched_values = exchanged(packed_values)
    weights_shape = (head_count, list_size * block_rows, row_count)
    weights_tile = pltpu.VMEM(weights_shape, jnp.float32)
    first_terms, last_terms, weights = pl.pallas_call(
        functools.partial(value_kernel, list_size, group, scale),
        out_shape=(
            packed_shape(first_rows),
            packed_shape(last_rows),
            jax.ShapeDtypeStruct(weights_shape, jnp.float32),
        ),
        in_specs=[SMEM, SMEM, VMEM, VMEM, ANY],
        out_specs=(ANY, ANY, ANY),
        scratch_shapes=[slot_tiles]
        + [vmem(slots, rows, head_dim) for rows in (first_rows, last_rows)]
        + [weights_tile, part_sem, part_sem, part_sem, wide_sem],
        compiler_params=PARAMS,
        name="value_terms",
    )(places, my_lengths, near(queries[0]), near(out_grad[0]), fetched_keys)
    handed_terms = shifted(last_terms, "section", -1)
    query_grad, key_terms = pl.pallas_call(
        functools.partial(key_kernel, list_size, group, scale),
        out_shape=(flat_shape, packed_shape(block_rows)),
        in_specs=[SMEM, SMEM, VMEM, VMEM, ANY, ANY, ANY],
        out_specs=(ANY, ANY),
        scratch_shapes=[slot_tiles, slot_tiles, weights_tile, slot_tiles, flat]
        + [part_sem, part_sem, wide_sem, part_sem, wide_sem],
        compiler_params=PARAMS,
        name="key_terms",
    )(
        places,
        my_lengths,
        near(queries[0]),
        near(out_grad[0]),
        fetched_keys,
        fetched_values,
        weights,
    )
    first_values = add_up("sum_values", exchanged(first_terms))
    handed_first = shifted(first_values, "section", -1)
    key_terms, handed_terms = lax.optimization_barrier((key_terms, handed_terms))
    returned_keys = exchanged(key_terms)
    handed_queries = placed("place_queries", shifted(query_grad, "section", -1), 5000000)
    returned_keys, handed_queries, first_values = lax.optimization_barrier(
        (returned_keys, handed_queries, first_values)
    )
    key_grad = add_up("sum_keys", near(returned_keys))
    key_grad, handed_terms, handed_first = lax.optimization_barrier(
        (key_grad, handed_terms, handed_first)
    )
    handed_keys = shifted(key_grad, "section", -1)
    handed_values = pl.pallas_call(
        functools.partial(join_kernel, add_parts),
        out_shape=flat_shape,
        in_specs=[SMEM, ANY, VMEM],
        out_specs=ANY,
        scratch_shapes=[wide_sum(last_rows), flat, vmem(2 * first_rows, column_count)]
        + [dma((send_parts,)), dma],
        compiler_params=PARAMS,
        name="join_values",
    )(handed_codes, handed_first, near(exchanged(handed_terms)))
    handed_keys = pl.pallas_call(
        place_last_kernel,
        out_shape=flat_shape,
        in_specs=[VMEM, ANY],
        out_specs=VMEM,
        compiler_params=PARAMS,
        name="place_keys",
    )(near(handed_keys), handed_values)
    return (handed_queries[None], handed_keys[None], handed_values[None])


def solution(mesh):
    placed = (
        P("section", "ctx", None),
        P("section", "ctx", None),
        P("section", "ctx", None),
        P("section", "ctx", None),
        P("section", None, None, None),
        P("section", None, None),
    )
    return jax.shard_map(
        local,
        mesh=mesh,
        in_specs=placed,
        out_specs=(P("section", "ctx", None), P("section", "ctx", None), P("section", "ctx", None)),
        check_vma=False,
    )
```

```python
import functools
import math

import jax
import jax.numpy as jnp
from jax import lax
from jax.experimental import pallas as pl
from jax.experimental.pallas import tpu as pltpu
from jax.sharding import PartitionSpec as P

HEAD_BITS = 8
VMEM = pl.BlockSpec(memory_space=pltpu.VMEM)
SMEM = pl.BlockSpec(memory_space=pltpu.SMEM)
ANY = pl.BlockSpec(memory_space=pl.ANY)
PARAMS = pltpu.CompilerParams(vmem_limit_bytes=56 * 1024 * 1024)
NT = (((1,), (1,)), ((), ()))
NN = (((1,), (0,)), ((), ()))
TN = (((0,), (0,)), ((), ()))
copy = pltpu.make_async_copy


def shifted(value, axis, steps):
    count = lax.axis_size(axis)
    pairs = [(source, (source + steps) % count) for source in range(count)]
    return lax.ppermute(value, axis, pairs)


def tile_of(code, rows, cols):
    block = lax.shift_right_logical(code, HEAD_BITS)
    head = lax.bitwise_and(code, (1 << HEAD_BITS) - 1)
    return (
        pl.ds(pl.multiple_of(block * rows, rows), rows),
        pl.ds(pl.multiple_of(head * cols, cols), cols),
    )


def code_at(codes, part, step, item):
    capacity = codes.shape[1]
    return codes[part * (step // capacity) + item // capacity, item % capacity]


def pack_kernel(parts, codes, source, packed, made, sent):
    slots, rows, cols = packed.shape
    step = slots // parts

    def part_of(part):
        where = pl.ds(part * step, step)
        return copy(made.at[where], packed.at[where], sent.at[part])

    def one_part(part, carry):
        for item in range(step):
            code = jnp.maximum(code_at(codes, part, step, item), 0)
            made[part * step + item] = source[tile_of(code, rows, cols)]
        part_of(part).start()
        return carry

    lax.fori_loop(0, parts, one_part, 0)
    for part in range(parts):
        part_of(part).wait()


def add_terms(codes, terms, wide, heads, parts):
    for index in range(2 * heads):
        wide[index] = jnp.zeros_like(wide[index])
    step = terms.shape[0] // parts

    def one_part(part, carry):
        for item in range(step):
            slot = part * step + item
            code = code_at(codes, part, step, item)
            block = lax.shift_right_logical(code, HEAD_BITS)
            head = lax.bitwise_and(code, (1 << HEAD_BITS) - 1)
            index = jnp.where(code < 0, 2 * heads, block * heads + head)
            wide[index] += terms[slot].astype(jnp.float32)
        return carry

    lax.fori_loop(0, parts, one_part, 0)


def fill_block(wide, ready, block, start, part, parts):
    heads = wide.shape[0] // 2
    rows, cols = wide.shape[1:]
    count = heads // parts
    for head in range(part * count, (part + 1) * count):
        ready[start : start + rows, head * cols : (head + 1) * cols] = wide[
            block * heads + head
        ].astype(ready.dtype)


def send_columns(ready, total, sent, parts, fill):
    width = total.shape[1] // parts
    copies = []
    for part in range(parts):
        columns = pl.ds(part * width, width)
        fill(part, columns)
        copies.append(copy(ready.at[:, columns], total.at[:, columns], sent.at[part]))
        copies[-1].start()
    for one in copies:
        one.wait()


def sum_kernel(parts, codes, terms, total, wide, ready, sent):
    add_terms(codes, terms, wide, wide.shape[0] // 2, parts)
    rows = terms.shape[1]

    def fill(part, columns):
        for block in range(2):
            fill_block(wide, ready, block, block * rows, part, sent.shape[0])

    send_columns(ready, total, sent, sent.shape[0], fill)


def join_kernel(
    parts, codes, head_part, terms, total, wide, ready, head, sent, got
):
    head_copy = copy(head_part, head, got)
    head_copy.start()
    add_terms(codes, terms, wide, wide.shape[0] // 2, parts)
    head_copy.wait()
    tail_rows = terms.shape[1]
    head_rows = total.shape[0] // 2 - tail_rows

    def fill(part, columns):
        for block in range(2):
            start = block * (head_rows + tail_rows)
            ready[start : start + head_rows, columns] = head[
                block * head_rows : (block + 1) * head_rows, columns
            ]
            fill_block(wide, ready, block, start + head_rows, part, sent.shape[0])

    send_columns(ready, total, sent, sent.shape[0], fill)


def place_last_kernel(source, after, out):
    out[...] = source[...]


def place_kernel(source, out):
    out[...] = source[...]


def weights_of(query, key, length, list_size, scale):
    scores = lax.dot_general(key, query, NT, preferred_element_type=jnp.float32)
    row_max = jnp.max(scores, axis=0, keepdims=True)
    exp_scores = jnp.exp2((scores - row_max) * (scale * math.log2(math.e)))
    rows = key.shape[0] // list_size
    parts = [exp_scores[item * rows : (item + 1) * rows] for item in range(list_size)]
    kept = [jnp.where(item < length, 1.0, 0.0).astype(jnp.float32) for item in range(list_size)]
    total = sum(keep * jnp.sum(part, axis=0, keepdims=True) for keep, part in zip(kept, parts))
    inverse = 1.0 / total
    return [part * (inverse * keep) for keep, part in zip(kept, parts)]


def in_parts(source, target, sems):
    parts = sems.shape[0]
    step = source.shape[0] // parts
    wheres = [pl.ds(part * step, step) for part in range(parts)]
    return [
        copy(source.at[where], target.at[where], sems.at[part])
        for part, where in enumerate(wheres)
    ]


def put_terms(places, lengths, list_size, head, result, outs):
    rows = result.shape[0] // list_size
    for entry in range(list_size):

        @pl.when(entry < lengths[head])
        def _():
            start = entry * rows
            for out in outs:
                count = out.shape[1]
                out[places[head * list_size + entry]] = result[start : start + count]
                start += count


def value_kernel(
    list_size, group, scale, places, lengths, queries, grads, keys, first, last, weights_out,
    key_held, first_made, last_made, weights_made, key_sem, first_sem, last_sem, weights_sem,
):
    rows, cols = keys.shape[1:]
    groups = lengths.shape[0] // group

    def weights_part(index):
        heads = pl.ds(index * group, group)
        return copy(weights_made.at[heads], weights_out.at[heads], weights_sem.at[index])

    for one in in_parts(keys, key_held, key_sem):
        one.start()

    def compute(head):
        columns = pl.ds(pl.multiple_of(head * cols, cols), cols)
        key = jnp.concatenate(
            [key_held[places[head * list_size + item]] for item in range(list_size)], axis=0
        )
        weights = weights_of(queries[:, columns], key, lengths[head], list_size, scale)
        for item, part in enumerate(weights):
            weights_made[head, item * rows : (item + 1) * rows] = part
        weights_low = jnp.concatenate([part.astype(jnp.bfloat16) for part in weights], axis=0)
        return lax.dot_general(
            weights_low, grads[:, columns], NN, preferred_element_type=jnp.float32
        ).astype(jnp.bfloat16)

    def one_group(index, carry):
        @pl.when(index == 0)
        def _():
            for one in in_parts(keys, key_held, key_sem):
                one.wait()

        results = [compute(index * group + item) for item in range(group)]
        weights_part(index).start()
        for item, result in enumerate(results):
            put_terms(
                places, lengths, list_size, index * group + item, result, [first_made, last_made]
            )
        return carry

    lax.fori_loop(0, groups, one_group, 0)
    ends = in_parts(last_made, last, last_sem) + in_parts(first_made, first, first_sem)
    for one in ends:
        one.start()
    for index in range(groups):
        weights_part(index).wait()
    for one in ends:
        one.wait()


def key_kernel(
    list_size, group, scale, places, lengths, queries, grads, keys, values, weights,
    query_grad, terms,
    key_held, value_held, weights_held, made, query_made,
    key_sem, value_sem, weights_sem, out_sem, query_out_sem,
):
    cols = keys.shape[2]
    groups = lengths.shape[0] // group
    width = group * cols

    def columns_of(index):
        return pl.ds(pl.multiple_of(index * width, width), width)

    def weights_part(index):
        heads = pl.ds(index * group, group)
        return copy(weights.at[heads], weights_held.at[heads], weights_sem.at[index])

    def value_fetches():
        return in_parts(values, value_held, value_sem)

    def key_fetches():
        return in_parts(keys, key_held, key_sem)

    def query_part(index):
        columns = columns_of(index)
        return copy(
            query_made.at[:, columns], query_grad.at[:, columns], query_out_sem.at[index]
        )

    for one in value_fetches() + [weights_part(0)] + key_fetches():
        one.start()

    def listed(head, tiles):
        return jnp.concatenate(
            [tiles[places[head * list_size + item]] for item in range(list_size)], axis=0
        )

    def columns_at(head):
        return pl.ds(pl.multiple_of(head * cols, cols), cols)

    def dscores_of(head):
        weight = weights_held[head]
        weight_low = weight.astype(jnp.bfloat16).astype(jnp.float32)
        dweights = lax.dot_general(
            listed(head, value_held),
            grads[:, columns_at(head)],
            NT,
            preferred_element_type=jnp.float32,
        )
        row_delta = jnp.sum(weight_low * dweights, axis=0, keepdims=True)
        return (weight * (dweights - row_delta)).astype(jnp.bfloat16)

    def terms_of(head, dscores):
        made_terms = lax.dot_general(
            dscores, queries[:, columns_at(head)], NN, preferred_element_type=jnp.float32
        )
        return (made_terms * scale).astype(jnp.bfloat16)

    def put_query(head, dscores):
        flipped = lax.dot_general(
            listed(head, key_held), dscores, TN, preferred_element_type=jnp.float32
        )
        query_made[:, columns_at(head)] = (flipped * scale).astype(jnp.bfloat16).T

    def one_group(index, carry):
        heads = [index * group + item for item in range(group)]

        @pl.when(index + 1 < groups)
        def _():
            weights_part(index + 1).start()

        weights_part(index).wait()

        @pl.when(index == 0)
        def _():
            for one in value_fetches():
                one.wait()

        dscores = [dscores_of(head) for head in heads]
        results = [terms_of(head, part) for head, part in zip(heads, dscores)]

        @pl.when(index == 0)
        def _():
            for one in key_fetches():
                one.wait()

        for head, part in zip(heads, dscores):
            put_query(head, part)
        query_part(index).start()
        for item, result in enumerate(results):
            put_terms(places, lengths, list_size, index * group + item, result, [made])
        return carry

    lax.fori_loop(0, groups, one_group, 0)
    ends = in_parts(made, terms, out_sem)
    for one in ends:
        one.start()
    for index in range(groups):
        query_part(index).wait()
    for one in ends:
        one.wait()


def local(queries, keys, values, out_grad, key_blocks, list_lengths):
    ctx_count = lax.axis_size("ctx")
    my_index = lax.axis_index("ctx")
    row_count, column_count = queries.shape[1:]
    head_count = list_lengths.shape[2]
    head_dim = column_count // head_count
    list_size = key_blocks.shape[3]
    block_rows = row_count // 2
    entries = head_count * list_size
    capacity = (entries + ctx_count - 1) // ctx_count
    slots = ctx_count * capacity
    scale = 1.0 / math.sqrt(head_dim)
    group = 4 if head_count % 4 == 0 else 1
    groups = head_count // group

    chosen = key_blocks[0]
    lengths = list_lengths[0]
    items = jnp.arange(list_size, dtype=jnp.int32)
    heads = jnp.arange(head_count, dtype=jnp.int32)
    is_used = items[None, None, :] < lengths[:, :, None]
    is_mine = is_used & ((chosen >> 1) == my_index)
    hit = jnp.sum(jnp.where(is_mine, 1 + (chosen & 1), 0), axis=2)
    rank = jnp.sum(
        jnp.where((heads[None, None, :] < heads[None, :, None]) & (hit[:, None, :] > 0), 1, 0),
        axis=2,
    )
    code = ((hit - 1) << HEAD_BITS) + heads[None, :]
    ranks = jnp.arange(capacity, dtype=jnp.int32)
    codes = jnp.max(
        jnp.where(
            (hit[:, None, :] > 0) & (rank[:, None, :] == ranks[None, :, None]),
            code[:, None, :],
            -1,
        ),
        axis=2,
    )

    my_lengths = lax.dynamic_index_in_dim(lengths, my_index, 0, keepdims=False)
    my_chosen = lax.dynamic_index_in_dim(chosen, my_index, 0, keepdims=False)
    my_used = items[None, :] < my_lengths[:, None]
    my_holder = jnp.where(my_used, my_chosen >> 1, -1)
    earlier = (heads[None, None, :, None] < heads[:, None, None, None]) & (
        my_holder[None, None, :, :] == my_holder[:, :, None, None]
    )
    my_rank = jnp.sum(jnp.where(earlier, 1, 0), axis=(2, 3))
    places = my_holder * capacity + my_rank
    places = jnp.where(my_used, places, places[:, :1]).reshape(entries)

    first_rows = 3 * block_rows // 8
    last_rows = block_rows - first_rows
    add_parts = 8 if ctx_count % 8 == 0 else 1
    send_parts = 5 if head_count % 5 == 0 else 1
    flat_shape = jax.ShapeDtypeStruct((row_count, column_count), jnp.bfloat16)
    dma = pltpu.SemaphoreType.DMA

    def vmem(*shape):
        return pltpu.VMEM(shape, jnp.bfloat16)

    flat = vmem(row_count, column_count)

    def packed_shape(rows):
        return jax.ShapeDtypeStruct((slots, rows, head_dim), jnp.bfloat16)

    def exchanged(packed):
        parts = packed.reshape(ctx_count, capacity, *packed.shape[1:])
        parts = lax.all_to_all(parts, "ctx", split_axis=0, concat_axis=0, tiled=True)
        return parts.reshape(packed.shape)

    def near(value):
        return pltpu.with_memory_space_constraint(value, pltpu.VMEM)

    def pack(name, source):
        return pl.pallas_call(
            functools.partial(pack_kernel, add_parts),
            out_shape=packed_shape(block_rows),
            in_specs=[SMEM, VMEM],
            out_specs=ANY,
            scratch_shapes=[vmem(slots, block_rows, head_dim), dma((add_parts,))],
            compiler_params=PARAMS,
            name=name,
        )(codes, source)

    def wide_sum(rows):
        return pltpu.VMEM((2 * head_count + 1, rows, head_dim), jnp.float32)

    def placed(name, value, cost):
        return pl.pallas_call(
            place_kernel,
            out_shape=flat_shape,
            in_specs=[VMEM],
            out_specs=VMEM,
            compiler_params=PARAMS,
            cost_estimate=pl.CostEstimate(flops=0, transcendentals=0, bytes_accessed=cost),
            name=name,
        )(near(value))

    def add_up(name, returned):
        rows = returned.shape[1]
        return pl.pallas_call(
            functools.partial(sum_kernel, add_parts),
            out_shape=jax.ShapeDtypeStruct((2 * rows, column_count), jnp.bfloat16),
            in_specs=[SMEM, VMEM],
            out_specs=ANY,
            scratch_shapes=[wide_sum(rows), vmem(2 * rows, column_count), dma((send_parts,))],
            compiler_params=PARAMS,
            name=name,
        )(codes, returned)

    slot_tiles = vmem(slots, block_rows, head_dim)
    wide_sem, part_sem = dma((groups,)), dma((add_parts,))
    fetched_keys = exchanged(pack("pack_keys", near(keys[0])))
    handed_codes = shifted(codes, "section", -1)
    packed_values, handed_codes, places, my_lengths = lax.optimization_barrier(
        (pack("pack_values", near(values[0])), handed_codes, places, my_lengths)
    )
    fetched_values = exchanged(packed_values)
    weights_shape = (head_count, list_size * block_rows, row_count)
    weights_tile = pltpu.VMEM(weights_shape, jnp.float32)
    first_terms, last_terms, weights = pl.pallas_call(
        functools.partial(value_kernel, list_size, group, scale),
        out_shape=(
            packed_shape(first_rows),
            packed_shape(last_rows),
            jax.ShapeDtypeStruct(weights_shape, jnp.float32),
        ),
        in_specs=[SMEM, SMEM, VMEM, VMEM, ANY],
        out_specs=(ANY, ANY, ANY),
        scratch_shapes=[slot_tiles]
        + [vmem(slots, rows, head_dim) for rows in (first_rows, last_rows)]
        + [weights_tile, part_sem, part_sem, part_sem, wide_sem],
        compiler_params=PARAMS,
        name="value_terms",
    )(places, my_lengths, near(queries[0]), near(out_grad[0]), fetched_keys)
    handed_terms = shifted(last_terms, "section", -1)
    query_grad, key_terms = pl.pallas_call(
        functools.partial(key_kernel, list_size, group, scale),
        out_shape=(flat_shape, packed_shape(block_rows)),
        in_specs=[SMEM, SMEM, VMEM, VMEM, ANY, ANY, ANY],
        out_specs=(ANY, ANY),
        scratch_shapes=[slot_tiles, slot_tiles, weights_tile, slot_tiles, flat]
        + [part_sem, part_sem, wide_sem, part_sem, wide_sem],
        compiler_params=PARAMS,
        name="key_terms",
    )(
        places,
        my_lengths,
        near(queries[0]),
        near(out_grad[0]),
        fetched_keys,
        fetched_values,
        weights,
    )
    first_values = add_up("sum_values", exchanged(first_terms))
    handed_first = shifted(first_values, "section", -1)
    key_terms, handed_terms = lax.optimization_barrier((key_terms, handed_terms))
    returned_keys = exchanged(key_terms)
    handed_queries = placed("place_queries", shifted(query_grad, "section", -1), 5000000)
    returned_keys, handed_queries, first_values = lax.optimization_barrier(
        (returned_keys, handed_queries, first_values)
    )
    key_grad = add_up("sum_keys", near(returned_keys))
    key_grad, handed_terms, handed_first = lax.optimization_barrier(
        (key_grad, handed_terms, handed_first)
    )
    handed_keys = shifted(key_grad, "section", -1)
    handed_values = pl.pallas_call(
        functools.partial(join_kernel, add_parts),
        out_shape=flat_shape,
        in_specs=[SMEM, ANY, VMEM],
        out_specs=ANY,
        scratch_shapes=[wide_sum(last_rows), flat, vmem(2 * first_rows, column_count)]
        + [dma((send_parts,)), dma],
        compiler_params=PARAMS,
        name="join_values",
    )(handed_codes, handed_first, near(exchanged(handed_terms)))
    handed_keys = pl.pallas_call(
        place_last_kernel,
        out_shape=flat_shape,
        in_specs=[VMEM, ANY],
        out_specs=VMEM,
        compiler_params=PARAMS,
        name="place_keys",
    )(near(handed_keys), handed_values)
    return (handed_queries[None], handed_keys[None], handed_values[None])


def solution(mesh):
    placed = (
        P("section", "ctx", None),
        P("section", "ctx", None),
        P("section", "ctx", None),
        P("section", "ctx", None),
        P("section", None, None, None),
        P("section", None, None),
    )
    return jax.shard_map(
        local,
        mesh=mesh,
        in_specs=placed,
        out_specs=(P("section", "ctx", None), P("section", "ctx", None), P("section", "ctx", None)),
        check_vma=False,
    )
```

```python
import functools
import math

import jax
import jax.numpy as jnp
from jax import lax
from jax.experimental import pallas as pl
from jax.experimental.pallas import tpu as pltpu
from jax.sharding import PartitionSpec as P

HEAD_BITS = 8
VMEM = pl.BlockSpec(memory_space=pltpu.VMEM)
SMEM = pl.BlockSpec(memory_space=pltpu.SMEM)
ANY = pl.BlockSpec(memory_space=pl.ANY)
PARAMS = pltpu.CompilerParams(vmem_limit_bytes=56 * 1024 * 1024)
NT = (((1,), (1,)), ((), ()))
NN = (((1,), (0,)), ((), ()))
TN = (((0,), (0,)), ((), ()))
copy = pltpu.make_async_copy


def shifted(value, axis, steps):
    count = lax.axis_size(axis)
    pairs = [(source, (source + steps) % count) for source in range(count)]
    return lax.ppermute(value, axis, pairs)


def tile_of(code, rows, cols):
    block = lax.shift_right_logical(code, HEAD_BITS)
    head = lax.bitwise_and(code, (1 << HEAD_BITS) - 1)
    return (
        pl.ds(pl.multiple_of(block * rows, rows), rows),
        pl.ds(pl.multiple_of(head * cols, cols), cols),
    )


def pack_kernel(parts, codes, source, packed, made, sent):
    slots, rows, cols = packed.shape
    step = slots // parts

    def part_of(part):
        where = pl.ds(part * step, step)
        return copy(made.at[where], packed.at[where], sent.at[part])

    def one_part(part, carry):
        for item in range(step):
            slot = part * step + item
            made[slot] = source[tile_of(jnp.maximum(codes[slot], 0), rows, cols)]
        part_of(part).start()
        return carry

    lax.fori_loop(0, parts, one_part, 0)
    for part in range(parts):
        part_of(part).wait()


def add_terms(codes, terms, wide, heads, parts):
    for index in range(2 * heads):
        wide[index] = jnp.zeros_like(wide[index])
    step = terms.shape[0] // parts

    def one_part(part, carry):
        for item in range(step):
            slot = part * step + item
            code = codes[slot]
            block = lax.shift_right_logical(code, HEAD_BITS)
            head = lax.bitwise_and(code, (1 << HEAD_BITS) - 1)
            index = jnp.where(code < 0, 2 * heads, block * heads + head)
            wide[index] += terms[slot].astype(jnp.float32)
        return carry

    lax.fori_loop(0, parts, one_part, 0)


def fill_block(wide, ready, block, start, part, parts):
    heads = wide.shape[0] // 2
    rows, cols = wide.shape[1:]
    count = heads // parts
    for head in range(part * count, (part + 1) * count):
        ready[start : start + rows, head * cols : (head + 1) * cols] = wide[
            block * heads + head
        ].astype(ready.dtype)


def send_columns(ready, total, sent, parts, fill):
    width = total.shape[1] // parts
    copies = []
    for part in range(parts):
        columns = pl.ds(part * width, width)
        fill(part, columns)
        copies.append(copy(ready.at[:, columns], total.at[:, columns], sent.at[part]))
        copies[-1].start()
    for one in copies:
        one.wait()


def sum_kernel(parts, codes, terms, total, wide, ready, sent):
    add_terms(codes, terms, wide, wide.shape[0] // 2, parts)
    rows = terms.shape[1]

    def fill(part, columns):
        for block in range(2):
            fill_block(wide, ready, block, block * rows, part, sent.shape[0])

    send_columns(ready, total, sent, sent.shape[0], fill)


def join_kernel(
    parts, codes, head_part, terms, total, wide, ready, head, sent, got
):
    head_copy = copy(head_part, head, got)
    head_copy.start()
    add_terms(codes, terms, wide, wide.shape[0] // 2, parts)
    head_copy.wait()
    tail_rows = terms.shape[1]
    head_rows = total.shape[0] // 2 - tail_rows

    def fill(part, columns):
        for block in range(2):
            start = block * (head_rows + tail_rows)
            ready[start : start + head_rows, columns] = head[
                block * head_rows : (block + 1) * head_rows, columns
            ]
            fill_block(wide, ready, block, start + head_rows, part, sent.shape[0])

    send_columns(ready, total, sent, sent.shape[0], fill)


def place_last_kernel(source, after, out):
    out[...] = source[...]


def place_kernel(source, out):
    out[...] = source[...]


def weights_of(query, key, length, list_size, scale):
    scores = lax.dot_general(key, query, NT, preferred_element_type=jnp.float32)
    row_max = jnp.max(scores, axis=0, keepdims=True)
    exp_scores = jnp.exp2((scores - row_max) * (scale * math.log2(math.e)))
    rows = key.shape[0] // list_size
    parts = [exp_scores[item * rows : (item + 1) * rows] for item in range(list_size)]
    kept = [jnp.where(item < length, 1.0, 0.0).astype(jnp.float32) for item in range(list_size)]
    total = sum(keep * jnp.sum(part, axis=0, keepdims=True) for keep, part in zip(kept, parts))
    inverse = 1.0 / total
    return [part * (inverse * keep) for keep, part in zip(kept, parts)]


def in_parts(source, target, sems):
    parts = sems.shape[0]
    step = source.shape[0] // parts
    wheres = [pl.ds(part * step, step) for part in range(parts)]
    return [
        copy(source.at[where], target.at[where], sems.at[part])
        for part, where in enumerate(wheres)
    ]


def put_terms(places, lengths, list_size, head, result, outs):
    rows = result.shape[0] // list_size
    for entry in range(list_size):

        @pl.when(entry < lengths[head])
        def _():
            start = entry * rows
            for out in outs:
                count = out.shape[1]
                out[places[head * list_size + entry]] = result[start : start + count]
                start += count


def value_kernel(
    list_size, group, scale, places, lengths, queries, grads, keys, first, last, weights_out,
    key_held, first_made, last_made, weights_made, key_sem, first_sem, last_sem, weights_sem,
):
    rows, cols = keys.shape[1:]
    groups = lengths.shape[0] // group

    def weights_part(index):
        heads = pl.ds(index * group, group)
        return copy(weights_made.at[heads], weights_out.at[heads], weights_sem.at[index])

    for one in in_parts(keys, key_held, key_sem):
        one.start()

    def compute(head):
        columns = pl.ds(pl.multiple_of(head * cols, cols), cols)
        key = jnp.concatenate(
            [key_held[places[head * list_size + item]] for item in range(list_size)], axis=0
        )
        weights = weights_of(queries[:, columns], key, lengths[head], list_size, scale)
        for item, part in enumerate(weights):
            weights_made[head, item * rows : (item + 1) * rows] = part
        weights_low = jnp.concatenate([part.astype(jnp.bfloat16) for part in weights], axis=0)
        return lax.dot_general(
            weights_low, grads[:, columns], NN, preferred_element_type=jnp.float32
        ).astype(jnp.bfloat16)

    def one_group(index, carry):
        @pl.when(index == 0)
        def _():
            for one in in_parts(keys, key_held, key_sem):
                one.wait()

        results = [compute(index * group + item) for item in range(group)]
        weights_part(index).start()
        for item, result in enumerate(results):
            put_terms(
                places, lengths, list_size, index * group + item, result, [first_made, last_made]
            )
        return carry

    lax.fori_loop(0, groups, one_group, 0)
    ends = in_parts(last_made, last, last_sem) + in_parts(first_made, first, first_sem)
    for one in ends:
        one.start()
    for index in range(groups):
        weights_part(index).wait()
    for one in ends:
        one.wait()


def key_kernel(
    list_size, group, scale, places, lengths, queries, grads, keys, values, weights,
    query_grad, terms,
    key_held, value_held, weights_held, made, query_made,
    key_sem, value_sem, weights_sem, out_sem, query_out_sem,
):
    cols = keys.shape[2]
    groups = lengths.shape[0] // group
    width = group * cols

    def columns_of(index):
        return pl.ds(pl.multiple_of(index * width, width), width)

    def weights_part(index):
        heads = pl.ds(index * group, group)
        return copy(weights.at[heads], weights_held.at[heads], weights_sem.at[index])

    def value_fetches():
        return in_parts(values, value_held, value_sem)

    def key_fetches():
        return in_parts(keys, key_held, key_sem)

    def query_part(index):
        columns = columns_of(index)
        return copy(
            query_made.at[:, columns], query_grad.at[:, columns], query_out_sem.at[index]
        )

    for one in value_fetches() + [weights_part(0)] + key_fetches():
        one.start()

    def listed(head, tiles):
        return jnp.concatenate(
            [tiles[places[head * list_size + item]] for item in range(list_size)], axis=0
        )

    def columns_at(head):
        return pl.ds(pl.multiple_of(head * cols, cols), cols)

    def dscores_of(head):
        weight = weights_held[head]
        weight_low = weight.astype(jnp.bfloat16).astype(jnp.float32)
        dweights = lax.dot_general(
            listed(head, value_held),
            grads[:, columns_at(head)],
            NT,
            preferred_element_type=jnp.float32,
        )
        row_delta = jnp.sum(weight_low * dweights, axis=0, keepdims=True)
        return (weight * (dweights - row_delta)).astype(jnp.bfloat16)

    def terms_of(head, dscores):
        made_terms = lax.dot_general(
            dscores, queries[:, columns_at(head)], NN, preferred_element_type=jnp.float32
        )
        return (made_terms * scale).astype(jnp.bfloat16)

    def put_query(head, dscores):
        flipped = lax.dot_general(
            listed(head, key_held), dscores, TN, preferred_element_type=jnp.float32
        )
        query_made[:, columns_at(head)] = (flipped * scale).astype(jnp.bfloat16).T

    def one_group(index, carry):
        heads = [index * group + item for item in range(group)]

        @pl.when(index + 1 < groups)
        def _():
            weights_part(index + 1).start()

        weights_part(index).wait()

        @pl.when(index == 0)
        def _():
            for one in value_fetches():
                one.wait()

        dscores = [dscores_of(head) for head in heads]
        results = [terms_of(head, part) for head, part in zip(heads, dscores)]

        @pl.when(index == 0)
        def _():
            for one in key_fetches():
                one.wait()

        for head, part in zip(heads, dscores):
            put_query(head, part)
        query_part(index).start()
        for item, result in enumerate(results):
            put_terms(places, lengths, list_size, index * group + item, result, [made])
        return carry

    lax.fori_loop(0, groups, one_group, 0)
    ends = in_parts(made, terms, out_sem)
    for one in ends:
        one.start()
    for index in range(groups):
        query_part(index).wait()
    for one in ends:
        one.wait()


def local(queries, keys, values, out_grad, key_blocks, list_lengths):
    ctx_count = lax.axis_size("ctx")
    my_index = lax.axis_index("ctx")
    row_count, column_count = queries.shape[1:]
    head_count = list_lengths.shape[2]
    head_dim = column_count // head_count
    list_size = key_blocks.shape[3]
    block_rows = row_count // 2
    entries = head_count * list_size
    capacity = (entries + ctx_count - 1) // ctx_count
    slots = ctx_count * capacity
    scale = 1.0 / math.sqrt(head_dim)
    group = 4 if head_count % 4 == 0 else 1
    groups = head_count // group

    chosen = key_blocks[0]
    lengths = list_lengths[0]
    items = jnp.arange(list_size, dtype=jnp.int32)
    heads = jnp.arange(head_count, dtype=jnp.int32)
    is_used = items[None, None, :] < lengths[:, :, None]
    is_mine = is_used & ((chosen >> 1) == my_index)
    hit = jnp.sum(jnp.where(is_mine, 1 + (chosen & 1), 0), axis=2)
    rank = jnp.sum(
        jnp.where((heads[None, None, :] < heads[None, :, None]) & (hit[:, None, :] > 0), 1, 0),
        axis=2,
    )
    code = ((hit - 1) << HEAD_BITS) + heads[None, :]
    ranks = jnp.arange(capacity, dtype=jnp.int32)
    codes = jnp.max(
        jnp.where(
            (hit[:, None, :] > 0) & (rank[:, None, :] == ranks[None, :, None]),
            code[:, None, :],
            -1,
        ),
        axis=2,
    ).reshape(slots)

    my_lengths = lax.dynamic_index_in_dim(lengths, my_index, 0, keepdims=False)
    my_chosen = lax.dynamic_index_in_dim(chosen, my_index, 0, keepdims=False)
    my_used = items[None, :] < my_lengths[:, None]
    my_holder = jnp.where(my_used, my_chosen >> 1, -1)
    earlier = (heads[None, None, :, None] < heads[:, None, None, None]) & (
        my_holder[None, None, :, :] == my_holder[:, :, None, None]
    )
    my_rank = jnp.sum(jnp.where(earlier, 1, 0), axis=(2, 3))
    places = my_holder * capacity + my_rank
    places = jnp.where(my_used, places, places[:, :1]).reshape(entries)

    first_rows = 3 * block_rows // 8
    last_rows = block_rows - first_rows
    add_parts = 8 if slots % 8 == 0 else 1
    send_parts = 5 if head_count % 5 == 0 else 1
    flat_shape = jax.ShapeDtypeStruct((row_count, column_count), jnp.bfloat16)
    dma = pltpu.SemaphoreType.DMA

    def vmem(*shape):
        return pltpu.VMEM(shape, jnp.bfloat16)

    flat = vmem(row_count, column_count)

    def packed_shape(rows):
        return jax.ShapeDtypeStruct((slots, rows, head_dim), jnp.bfloat16)

    def exchanged(packed):
        parts = packed.reshape(ctx_count, capacity, *packed.shape[1:])
        parts = lax.all_to_all(parts, "ctx", split_axis=0, concat_axis=0, tiled=True)
        return parts.reshape(packed.shape)

    def near(value):
        return pltpu.with_memory_space_constraint(value, pltpu.VMEM)

    def pack(name, source):
        return pl.pallas_call(
            functools.partial(pack_kernel, add_parts),
            out_shape=packed_shape(block_rows),
            in_specs=[SMEM, VMEM],
            out_specs=ANY,
            scratch_shapes=[vmem(slots, block_rows, head_dim), dma((add_parts,))],
            compiler_params=PARAMS,
            name=name,
        )(codes, source)

    def wide_sum(rows):
        return pltpu.VMEM((2 * head_count + 1, rows, head_dim), jnp.float32)

    def placed(name, value, cost):
        return pl.pallas_call(
            place_kernel,
            out_shape=flat_shape,
            in_specs=[VMEM],
            out_specs=VMEM,
            compiler_params=PARAMS,
            cost_estimate=pl.CostEstimate(flops=0, transcendentals=0, bytes_accessed=cost),
            name=name,
        )(near(value))

    def add_up(name, returned):
        rows = returned.shape[1]
        return pl.pallas_call(
            functools.partial(sum_kernel, add_parts),
            out_shape=jax.ShapeDtypeStruct((2 * rows, column_count), jnp.bfloat16),
            in_specs=[SMEM, VMEM],
            out_specs=ANY,
            scratch_shapes=[wide_sum(rows), vmem(2 * rows, column_count), dma((send_parts,))],
            compiler_params=PARAMS,
            name=name,
        )(codes, returned)

    slot_tiles = vmem(slots, block_rows, head_dim)
    wide_sem, part_sem = dma((groups,)), dma((add_parts,))
    fetched_keys = exchanged(pack("pack_keys", near(keys[0])))
    handed_codes = shifted(codes, "section", -1)
    packed_values, handed_codes, places, my_lengths = lax.optimization_barrier(
        (pack("pack_values", near(values[0])), handed_codes, places, my_lengths)
    )
    fetched_values = exchanged(packed_values)
    weights_shape = (head_count, list_size * block_rows, row_count)
    weights_tile = pltpu.VMEM(weights_shape, jnp.float32)
    first_terms, last_terms, weights = pl.pallas_call(
        functools.partial(value_kernel, list_size, group, scale),
        out_shape=(
            packed_shape(first_rows),
            packed_shape(last_rows),
            jax.ShapeDtypeStruct(weights_shape, jnp.float32),
        ),
        in_specs=[SMEM, SMEM, VMEM, VMEM, ANY],
        out_specs=(ANY, ANY, ANY),
        scratch_shapes=[slot_tiles]
        + [vmem(slots, rows, head_dim) for rows in (first_rows, last_rows)]
        + [weights_tile, part_sem, part_sem, part_sem, wide_sem],
        compiler_params=PARAMS,
        name="value_terms",
    )(places, my_lengths, near(queries[0]), near(out_grad[0]), fetched_keys)
    handed_terms = shifted(last_terms, "section", -1)
    query_grad, key_terms = pl.pallas_call(
        functools.partial(key_kernel, list_size, group, scale),
        out_shape=(flat_shape, packed_shape(block_rows)),
        in_specs=[SMEM, SMEM, VMEM, VMEM, ANY, ANY, ANY],
        out_specs=(ANY, ANY),
        scratch_shapes=[slot_tiles, slot_tiles, weights_tile, slot_tiles, flat]
        + [part_sem, part_sem, wide_sem, part_sem, wide_sem],
        compiler_params=PARAMS,
        name="key_terms",
    )(
        places,
        my_lengths,
        near(queries[0]),
        near(out_grad[0]),
        fetched_keys,
        fetched_values,
        weights,
    )
    first_values = add_up("sum_values", exchanged(first_terms))
    handed_first = shifted(first_values, "section", -1)
    key_terms, handed_terms = lax.optimization_barrier((key_terms, handed_terms))
    returned_keys = exchanged(key_terms)
    handed_queries = placed("place_queries", shifted(query_grad, "section", -1), 5000000)
    returned_keys, handed_queries, first_values = lax.optimization_barrier(
        (returned_keys, handed_queries, first_values)
    )
    key_grad = add_up("sum_keys", near(returned_keys))
    key_grad, handed_terms, handed_first = lax.optimization_barrier(
        (key_grad, handed_terms, handed_first)
    )
    handed_keys = shifted(key_grad, "section", -1)
    handed_values = pl.pallas_call(
        functools.partial(join_kernel, add_parts),
        out_shape=flat_shape,
        in_specs=[SMEM, ANY, VMEM],
        out_specs=ANY,
        scratch_shapes=[wide_sum(last_rows), flat, vmem(2 * first_rows, column_count)]
        + [dma((send_parts,)), dma],
        compiler_params=PARAMS,
        name="join_values",
    )(handed_codes, handed_first, near(exchanged(handed_terms)))
    handed_keys = pl.pallas_call(
        place_last_kernel,
        out_shape=flat_shape,
        in_specs=[VMEM, ANY],
        out_specs=VMEM,
        compiler_params=PARAMS,
        name="place_keys",
    )(near(handed_keys), handed_values)
    return (handed_queries[None], handed_keys[None], handed_values[None])


def solution(mesh):
    placed = (
        P("section", "ctx", None),
        P("section", "ctx", None),
        P("section", "ctx", None),
        P("section", "ctx", None),
        P("section", None, None, None),
        P("section", None, None),
    )
    return jax.shard_map(
        local,
        mesh=mesh,
        in_specs=placed,
        out_specs=(P("section", "ctx", None), P("section", "ctx", None), P("section", "ctx", None)),
        check_vma=False,
    )
```

```python
import functools
import math

import jax
import jax.numpy as jnp
from jax import lax
from jax.experimental import pallas as pl
from jax.experimental.pallas import tpu as pltpu
from jax.sharding import PartitionSpec as P

HEAD_BITS = 8
VMEM = pl.BlockSpec(memory_space=pltpu.VMEM)
SMEM = pl.BlockSpec(memory_space=pltpu.SMEM)
ANY = pl.BlockSpec(memory_space=pl.ANY)
PARAMS = pltpu.CompilerParams(vmem_limit_bytes=56 * 1024 * 1024)
NT = (((1,), (1,)), ((), ()))
NN = (((1,), (0,)), ((), ()))
TN = (((0,), (0,)), ((), ()))
copy = pltpu.make_async_copy


def shifted(value, axis, steps):
    count = lax.axis_size(axis)
    pairs = [(source, (source + steps) % count) for source in range(count)]
    return lax.ppermute(value, axis, pairs)


def tile_of(code, rows, cols):
    block = lax.shift_right_logical(code, HEAD_BITS)
    head = lax.bitwise_and(code, (1 << HEAD_BITS) - 1)
    return (
        pl.ds(pl.multiple_of(block * rows, rows), rows),
        pl.ds(pl.multiple_of(head * cols, cols), cols),
    )


def code_at(codes, part, step, item):
    capacity = codes.shape[1]
    return codes[part * (step // capacity) + item // capacity, item % capacity]


def pack_kernel(parts, codes, source, packed, made, sent):
    slots, rows, cols = packed.shape
    step = slots // parts

    def part_of(part):
        where = pl.ds(part * step, step)
        return copy(made.at[where], packed.at[where], sent.at[part])

    def one_part(part, carry):
        for item in range(step):
            code = jnp.maximum(code_at(codes, part, step, item), 0)
            made[part * step + item] = source[tile_of(code, rows, cols)]
        part_of(part).start()
        return carry

    lax.fori_loop(0, parts, one_part, 0)
    for part in range(parts):
        part_of(part).wait()


def add_terms(codes, terms, wide, heads, parts):
    for index in range(2 * heads):
        wide[index] = jnp.zeros_like(wide[index])
    step = terms.shape[0] // parts

    def one_part(part, carry):
        for item in range(step):
            slot = part * step + item
            code = code_at(codes, part, step, item)
            block = lax.shift_right_logical(code, HEAD_BITS)
            head = lax.bitwise_and(code, (1 << HEAD_BITS) - 1)
            index = jnp.where(code < 0, 2 * heads, block * heads + head)
            wide[index] += terms[slot].astype(jnp.float32)
        return carry

    lax.fori_loop(0, parts, one_part, 0)


def fill_block(wide, ready, block, start, part, parts):
    heads = wide.shape[0] // 2
    rows, cols = wide.shape[1:]
    count = heads // parts
    for head in range(part * count, (part + 1) * count):
        ready[start : start + rows, head * cols : (head + 1) * cols] = wide[
            block * heads + head
        ].astype(ready.dtype)


def send_columns(ready, total, sent, parts, fill):
    width = total.shape[1] // parts
    copies = []
    for part in range(parts):
        columns = pl.ds(part * width, width)
        fill(part, columns)
        copies.append(copy(ready.at[:, columns], total.at[:, columns], sent.at[part]))
        copies[-1].start()
    for one in copies:
        one.wait()


def sum_kernel(parts, codes, terms, total, wide, ready, sent):
    add_terms(codes, terms, wide, wide.shape[0] // 2, parts)
    rows = terms.shape[1]

    def fill(part, columns):
        for block in range(2):
            fill_block(wide, ready, block, block * rows, part, sent.shape[0])

    send_columns(ready, total, sent, sent.shape[0], fill)


def join_kernel(
    parts, codes, head_part, terms, total, wide, ready, head, sent, got
):
    head_copy = copy(head_part, head, got)
    head_copy.start()
    add_terms(codes, terms, wide, wide.shape[0] // 2, parts)
    head_copy.wait()
    tail_rows = terms.shape[1]
    head_rows = total.shape[0] // 2 - tail_rows

    def fill(part, columns):
        for block in range(2):
            start = block * (head_rows + tail_rows)
            ready[start : start + head_rows, columns] = head[
                block * head_rows : (block + 1) * head_rows, columns
            ]
            fill_block(wide, ready, block, start + head_rows, part, sent.shape[0])

    send_columns(ready, total, sent, sent.shape[0], fill)


def place_last_kernel(source, after, out):
    out[...] = source[...]


def place_kernel(source, out):
    out[...] = source[...]


def weights_of(query, key, length, list_size, scale):
    scores = lax.dot_general(key, query, NT, preferred_element_type=jnp.float32)
    row_max = jnp.max(scores, axis=0, keepdims=True)
    exp_scores = jnp.exp2((scores - row_max) * (scale * math.log2(math.e)))
    rows = key.shape[0] // list_size
    parts = [exp_scores[item * rows : (item + 1) * rows] for item in range(list_size)]
    kept = [jnp.where(item < length, 1.0, 0.0).astype(jnp.float32) for item in range(list_size)]
    total = sum(keep * jnp.sum(part, axis=0, keepdims=True) for keep, part in zip(kept, parts))
    inverse = 1.0 / total
    return [part * (inverse * keep) for keep, part in zip(kept, parts)]


def in_parts(source, target, sems):
    parts = sems.shape[0]
    step = source.shape[0] // parts
    wheres = [pl.ds(part * step, step) for part in range(parts)]
    return [
        copy(source.at[where], target.at[where], sems.at[part])
        for part, where in enumerate(wheres)
    ]


def put_terms(places, lengths, list_size, head, result, outs):
    rows = result.shape[0] // list_size
    for entry in range(list_size):

        @pl.when(entry < lengths[head])
        def _():
            start = entry * rows
            for out in outs:
                count = out.shape[1]
                out[places[head * list_size + entry]] = result[start : start + count]
                start += count


def value_kernel(
    list_size, group, scale, places, lengths, queries, grads, keys, first, last, weights_out,
    key_held, first_made, last_made, weights_made, key_sem, first_sem, last_sem, weights_sem,
):
    rows, cols = keys.shape[1:]
    groups = lengths.shape[0] // group

    def weights_part(index):
        heads = pl.ds(index * group, group)
        return copy(weights_made.at[heads], weights_out.at[heads], weights_sem.at[index])

    for one in in_parts(keys, key_held, key_sem):
        one.start()

    def compute(head):
        columns = pl.ds(pl.multiple_of(head * cols, cols), cols)
        key = jnp.concatenate(
            [key_held[places[head * list_size + item]] for item in range(list_size)], axis=0
        )
        weights = weights_of(queries[:, columns], key, lengths[head], list_size, scale)
        for item, part in enumerate(weights):
            weights_made[head, item * rows : (item + 1) * rows] = part
        weights_low = jnp.concatenate([part.astype(jnp.bfloat16) for part in weights], axis=0)
        return lax.dot_general(
            weights_low, grads[:, columns], NN, preferred_element_type=jnp.float32
        ).astype(jnp.bfloat16)

    def one_group(index, carry):
        @pl.when(index == 0)
        def _():
            for one in in_parts(keys, key_held, key_sem):
                one.wait()

        results = [compute(index * group + item) for item in range(group)]
        weights_part(index).start()
        for item, result in enumerate(results):
            put_terms(
                places, lengths, list_size, index * group + item, result, [first_made, last_made]
            )
        return carry

    lax.fori_loop(0, groups, one_group, 0)
    ends = in_parts(last_made, last, last_sem) + in_parts(first_made, first, first_sem)
    for one in ends:
        one.start()
    for index in range(groups):
        weights_part(index).wait()
    for one in ends:
        one.wait()


def key_kernel(
    list_size, group, scale, places, lengths, queries, grads, keys, values, weights,
    query_grad, terms,
    key_held, value_held, weights_held, made, query_made,
    key_sem, value_sem, weights_sem, out_sem, query_out_sem,
):
    cols = keys.shape[2]
    groups = lengths.shape[0] // group
    width = group * cols

    def columns_of(index):
        return pl.ds(pl.multiple_of(index * width, width), width)

    def weights_part(index):
        heads = pl.ds(index * group, group)
        return copy(weights.at[heads], weights_held.at[heads], weights_sem.at[index])

    def value_fetches():
        return in_parts(values, value_held, value_sem)

    def key_fetches():
        return in_parts(keys, key_held, key_sem)

    def query_part(index):
        columns = columns_of(index)
        return copy(
            query_made.at[:, columns], query_grad.at[:, columns], query_out_sem.at[index]
        )

    for one in value_fetches() + [weights_part(0)] + key_fetches():
        one.start()

    def listed(head, tiles):
        return jnp.concatenate(
            [tiles[places[head * list_size + item]] for item in range(list_size)], axis=0
        )

    def columns_at(head):
        return pl.ds(pl.multiple_of(head * cols, cols), cols)

    def dscores_of(head):
        weight = weights_held[head]
        weight_low = weight.astype(jnp.bfloat16).astype(jnp.float32)
        dweights = lax.dot_general(
            listed(head, value_held),
            grads[:, columns_at(head)],
            NT,
            preferred_element_type=jnp.float32,
        )
        row_delta = jnp.sum(weight_low * dweights, axis=0, keepdims=True)
        return (weight * (dweights - row_delta)).astype(jnp.bfloat16)

    def terms_of(head, dscores):
        made_terms = lax.dot_general(
            dscores, queries[:, columns_at(head)], NN, preferred_element_type=jnp.float32
        )
        return (made_terms * scale).astype(jnp.bfloat16)

    def put_query(head, dscores):
        flipped = lax.dot_general(
            listed(head, key_held), dscores, TN, preferred_element_type=jnp.float32
        )
        query_made[:, columns_at(head)] = (flipped * scale).astype(jnp.bfloat16).T

    def one_group(index, carry):
        heads = [index * group + item for item in range(group)]

        @pl.when(index + 1 < groups)
        def _():
            weights_part(index + 1).start()

        weights_part(index).wait()

        @pl.when(index == 0)
        def _():
            for one in value_fetches():
                one.wait()

        dscores = [dscores_of(head) for head in heads]
        results = [terms_of(head, part) for head, part in zip(heads, dscores)]

        @pl.when(index == 0)
        def _():
            for one in key_fetches():
                one.wait()

        for head, part in zip(heads, dscores):
            put_query(head, part)
        query_part(index).start()
        for item, result in enumerate(results):
            put_terms(places, lengths, list_size, index * group + item, result, [made])
        return carry

    lax.fori_loop(0, groups, one_group, 0)
    ends = in_parts(made, terms, out_sem)
    for one in ends:
        one.start()
    for index in range(groups):
        query_part(index).wait()
    for one in ends:
        one.wait()


def local(queries, keys, values, out_grad, key_blocks, list_lengths):
    ctx_count = lax.axis_size("ctx")
    my_index = lax.axis_index("ctx")
    row_count, column_count = queries.shape[1:]
    head_count = list_lengths.shape[2]
    head_dim = column_count // head_count
    list_size = key_blocks.shape[3]
    block_rows = row_count // 2
    entries = head_count * list_size
    capacity = (entries + ctx_count - 1) // ctx_count
    slots = ctx_count * capacity
    scale = 1.0 / math.sqrt(head_dim)
    group = 5 if head_count % 5 == 0 else 1
    groups = head_count // group

    chosen = key_blocks[0]
    lengths = list_lengths[0]
    items = jnp.arange(list_size, dtype=jnp.int32)
    heads = jnp.arange(head_count, dtype=jnp.int32)
    is_used = items[None, None, :] < lengths[:, :, None]
    is_mine = is_used & ((chosen >> 1) == my_index)
    hit = jnp.sum(jnp.where(is_mine, 1 + (chosen & 1), 0), axis=2)
    rank = jnp.sum(
        jnp.where((heads[None, None, :] < heads[None, :, None]) & (hit[:, None, :] > 0), 1, 0),
        axis=2,
    )
    code = ((hit - 1) << HEAD_BITS) + heads[None, :]
    ranks = jnp.arange(capacity, dtype=jnp.int32)
    codes = jnp.max(
        jnp.where(
            (hit[:, None, :] > 0) & (rank[:, None, :] == ranks[None, :, None]),
            code[:, None, :],
            -1,
        ),
        axis=2,
    )

    my_lengths = lax.dynamic_index_in_dim(lengths, my_index, 0, keepdims=False)
    my_chosen = lax.dynamic_index_in_dim(chosen, my_index, 0, keepdims=False)
    my_used = items[None, :] < my_lengths[:, None]
    my_holder = jnp.where(my_used, my_chosen >> 1, -1)
    earlier = (heads[None, None, :, None] < heads[:, None, None, None]) & (
        my_holder[None, None, :, :] == my_holder[:, :, None, None]
    )
    my_rank = jnp.sum(jnp.where(earlier, 1, 0), axis=(2, 3))
    places = my_holder * capacity + my_rank
    places = jnp.where(my_used, places, places[:, :1]).reshape(entries)

    first_rows = 3 * block_rows // 8
    last_rows = block_rows - first_rows
    add_parts = 8 if ctx_count % 8 == 0 else 1
    send_parts = 5 if head_count % 5 == 0 else 1
    flat_shape = jax.ShapeDtypeStruct((row_count, column_count), jnp.bfloat16)
    dma = pltpu.SemaphoreType.DMA

    def vmem(*shape):
        return pltpu.VMEM(shape, jnp.bfloat16)

    flat = vmem(row_count, column_count)

    def packed_shape(rows):
        return jax.ShapeDtypeStruct((slots, rows, head_dim), jnp.bfloat16)

    def exchanged(packed):
        parts = packed.reshape(ctx_count, capacity, *packed.shape[1:])
        parts = lax.all_to_all(parts, "ctx", split_axis=0, concat_axis=0, tiled=True)
        return parts.reshape(packed.shape)

    def near(value):
        return pltpu.with_memory_space_constraint(value, pltpu.VMEM)

    def pack(name, source):
        return pl.pallas_call(
            functools.partial(pack_kernel, add_parts),
            out_shape=packed_shape(block_rows),
            in_specs=[SMEM, VMEM],
            out_specs=ANY,
            scratch_shapes=[vmem(slots, block_rows, head_dim), dma((add_parts,))],
            compiler_params=PARAMS,
            name=name,
        )(codes, source)

    def wide_sum(rows):
        return pltpu.VMEM((2 * head_count + 1, rows, head_dim), jnp.float32)

    def placed(name, value, cost):
        return pl.pallas_call(
            place_kernel,
            out_shape=flat_shape,
            in_specs=[VMEM],
            out_specs=VMEM,
            compiler_params=PARAMS,
            cost_estimate=pl.CostEstimate(flops=0, transcendentals=0, bytes_accessed=cost),
            name=name,
        )(near(value))

    def add_up(name, returned):
        rows = returned.shape[1]
        return pl.pallas_call(
            functools.partial(sum_kernel, add_parts),
            out_shape=jax.ShapeDtypeStruct((2 * rows, column_count), jnp.bfloat16),
            in_specs=[SMEM, VMEM],
            out_specs=ANY,
            scratch_shapes=[wide_sum(rows), vmem(2 * rows, column_count), dma((send_parts,))],
            compiler_params=PARAMS,
            name=name,
        )(codes, returned)

    slot_tiles = vmem(slots, block_rows, head_dim)
    wide_sem, part_sem = dma((groups,)), dma((add_parts,))
    fetched_keys = exchanged(pack("pack_keys", near(keys[0])))
    handed_codes = shifted(codes, "section", -1)
    packed_values, handed_codes, places, my_lengths = lax.optimization_barrier(
        (pack("pack_values", near(values[0])), handed_codes, places, my_lengths)
    )
    fetched_values = exchanged(packed_values)
    weights_shape = (head_count, list_size * block_rows, row_count)
    weights_tile = pltpu.VMEM(weights_shape, jnp.float32)
    first_terms, last_terms, weights = pl.pallas_call(
        functools.partial(value_kernel, list_size, group, scale),
        out_shape=(
            packed_shape(first_rows),
            packed_shape(last_rows),
            jax.ShapeDtypeStruct(weights_shape, jnp.float32),
        ),
        in_specs=[SMEM, SMEM, VMEM, VMEM, ANY],
        out_specs=(ANY, ANY, ANY),
        scratch_shapes=[slot_tiles]
        + [vmem(slots, rows, head_dim) for rows in (first_rows, last_rows)]
        + [weights_tile, part_sem, part_sem, part_sem, wide_sem],
        compiler_params=PARAMS,
        name="value_terms",
    )(places, my_lengths, near(queries[0]), near(out_grad[0]), fetched_keys)
    handed_terms = shifted(last_terms, "section", -1)
    query_grad, key_terms = pl.pallas_call(
        functools.partial(key_kernel, list_size, group, scale),
        out_shape=(flat_shape, packed_shape(block_rows)),
        in_specs=[SMEM, SMEM, VMEM, VMEM, ANY, ANY, ANY],
        out_specs=(ANY, ANY),
        scratch_shapes=[slot_tiles, slot_tiles, weights_tile, slot_tiles, flat]
        + [part_sem, part_sem, wide_sem, part_sem, wide_sem],
        compiler_params=PARAMS,
        name="key_terms",
    )(
        places,
        my_lengths,
        near(queries[0]),
        near(out_grad[0]),
        fetched_keys,
        fetched_values,
        weights,
    )
    first_values = add_up("sum_values", exchanged(first_terms))
    handed_first = shifted(first_values, "section", -1)
    key_terms, handed_terms = lax.optimization_barrier((key_terms, handed_terms))
    returned_keys = exchanged(key_terms)
    handed_queries = placed("place_queries", shifted(query_grad, "section", -1), 5000000)
    returned_keys, handed_queries, first_values = lax.optimization_barrier(
        (returned_keys, handed_queries, first_values)
    )
    key_grad = add_up("sum_keys", near(returned_keys))
    key_grad, handed_terms, handed_first = lax.optimization_barrier(
        (key_grad, handed_terms, handed_first)
    )
    handed_keys = shifted(key_grad, "section", -1)
    handed_values = pl.pallas_call(
        functools.partial(join_kernel, add_parts),
        out_shape=flat_shape,
        in_specs=[SMEM, ANY, VMEM],
        out_specs=ANY,
        scratch_shapes=[wide_sum(last_rows), flat, vmem(2 * first_rows, column_count)]
        + [dma((send_parts,)), dma],
        compiler_params=PARAMS,
        name="join_values",
    )(handed_codes, handed_first, near(exchanged(handed_terms)))
    handed_keys = pl.pallas_call(
        place_last_kernel,
        out_shape=flat_shape,
        in_specs=[VMEM, ANY],
        out_specs=VMEM,
        compiler_params=PARAMS,
        name="place_keys",
    )(near(handed_keys), handed_values)
    return (handed_queries[None], handed_keys[None], handed_values[None])


def solution(mesh):
    placed = (
        P("section", "ctx", None),
        P("section", "ctx", None),
        P("section", "ctx", None),
        P("section", "ctx", None),
        P("section", None, None, None),
        P("section", None, None),
    )
    return jax.shard_map(
        local,
        mesh=mesh,
        in_specs=placed,
        out_specs=(P("section", "ctx", None), P("section", "ctx", None), P("section", "ctx", None)),
        check_vma=False,
    )
```
